32 devices in a mesh: dp: 4 (over z), mp: 8 (over y, x, core).
Axes of the slice: x: 2, y: 2, z: 4, core: 2. Of those that a mesh axis runs over, the one named last changes fastest.
Arguments:
- block_input: bfloat16 [8192, 2048], P(('dp', 'mp')), may hold values from -6 to 6
- out_cotangent: bfloat16 [8192, 2048], P(('dp', 'mp')), may hold values from -6 to 6
- objective: int32 [16], P('dp'), may hold values from 0 to 1, as said below
- prefix_len: int32 [16], P('dp'), may hold values from 64 to 511
- target_mask: int32 [8192], P(('dp', 'mp')), may hold values from 0 to 1, as said below
- qkv_weight: float32 [2048, 3, 2048], P('dp', None, 'mp'), may hold values from -0.125 to 0.125
- out_weight: float32 [2048, 2048], P('mp', 'dp'), may hold values from -3 to 3
- gateup_weight: float32 [2048, 2, 5472], P('dp', None, 'mp'), may hold values from -0.125 to 0.125
- down_weight: float32 [5472, 2048], P('mp', 'dp'), may hold values from -0.625 to 0.625
- norm_params: float32 [4, 2048], replicated, as said below
- qkv_first: float32 [2048, 3, 2048], P('dp', None, 'mp'), may hold values from -0.125 to 0.125
- out_first: float32 [2048, 2048], P('mp', 'dp'), may hold values from -0.005859375 to 0.005859375
- gateup_first: float32 [2048, 2, 5472], P('dp', None, 'mp'), may hold values from -0.09375 to 0.09375
- down_first: float32 [5472, 2048], P('mp', 'dp'), may hold values from -0.013671875 to 0.013671875
- norm_first: float32 [4, 2048], replicated, may hold values from -0.21875 to 0.21875
- qkv_second: float32 [2048, 3, 2048], P('dp', None, 'mp'), may hold values from 3.0517578e-05 to 0.00048828125
- out_second: float32 [2048, 2048], P('mp', 'dp'), may hold values from 7.080078e-08 to 1.1230469e-06
- gateup_second: float32 [2048, 2, 5472], P('dp', None, 'mp'), may hold values from 1.953125e-05 to 0.0003125
- down_second: float32 [5472, 2048], P('mp', 'dp'), may hold values from 4.3945312e-07 to 7.080078e-06
- norm_second: float32 [4, 2048], replicated, may hold values from 0.00012207031 to 0.001953125
Outputs:
- block_output: bfloat16 [8192, 2048], P(('dp', 'mp'))
- input_grad: float32 [8192, 2048], P(('dp', 'mp'))
- qkv_new: float32 [2048, 3, 2048], P('dp', None, 'mp')
- qkv_first_new: float32 [2048, 3, 2048], P('dp', None, 'mp')
- qkv_second_new: float32 [2048, 3, 2048], P('dp', None, 'mp')
- out_new: float32 [2048, 2048], P('mp', 'dp')
- out_first_new: float32 [2048, 2048], P('mp', 'dp')
- out_second_new: float32 [2048, 2048], P('mp', 'dp')
- gateup_new: float32 [2048, 2, 5472], P('dp', None, 'mp')
- gateup_first_new: float32 [2048, 2, 5472], P('dp', None, 'mp')
- gateup_second_new: float32 [2048, 2, 5472], P('dp', None, 'mp')
- down_new: float32 [5472, 2048], P('mp', 'dp')
- down_first_new: float32 [5472, 2048], P('mp', 'dp')
- down_second_new: float32 [5472, 2048], P('mp', 'dp')
- norm_new: float32 [4, 2048], replicated
- norm_first_new: float32 [4, 2048], replicated
- norm_second_new: float32 [4, 2048], replicated
The draws below stay inside these ranges and needn't reach their ends.
Inputs may be any that keep to these rules, and one draw needn't show every extreme that they name: `objective`: at least one sequence of each kind. `target_mask`: the last residue of every sequence is a target. `norm_params`: rows 0 and 2 are the gains of the first and second norm, rows 1 and 3 their biases.
All inputs are finite; a program needn't handle non-finite values.
Results may differ from the reference program's by a relative error of at most 0.024.
Values may be sent and summed in bfloat16 or wider, within the bound.
No kernel may reach another device: no remote copies, remote signals or barrier semaphores. Data moves between devices by JAX's collectives and lax.ppermute only.
A program may use at most 256 MiB of HBM per device.

```python
import math
from functools import partial
import jax
import jax.numpy as jnp
from jax import lax

D = 2048
HEADS = 16
HD = 128
FF = 5461
FF_PAD = 5472
LEN = 512
STEP = 5
SEQ_DEV = 4
SEQS = 16
TOKENS = 8192
N_DP = 4


def draw_objective(key, part):
    base_key = jax.random.fold_in(key, 21)
    first_key = jax.random.fold_in(key, 22)
    second_key = jax.random.fold_in(key, 23)
    seq_index = jnp.arange(SEQS, dtype=jnp.int32)
    coins = (jax.random.randint(base_key, (SEQS,), 0, 4, dtype=jnp.int32) == 0).astype(jnp.int32)
    first_pick = jax.random.randint(first_key, (), 0, SEQS, dtype=jnp.int32)
    second_pick = (first_pick + 1 + jax.random.randint(second_key, (), 0, SEQS - 1, dtype=jnp.int32)) % SEQS
    flags = jnp.where(seq_index == first_pick, 1, jnp.where(seq_index == second_pick, 0, coins))
    return flags.astype(jnp.int32)


def draw_target_mask(key, part):
    token_index = jnp.arange(TOKENS, dtype=jnp.int32)
    seq_index = token_index // LEN
    drawn = jax.random.randint(key, (TOKENS,), 0, 4 * SEQS, dtype=jnp.int32)
    chosen = (drawn < SEQS + 2 * seq_index) | (token_index % LEN == LEN - 1)
    return chosen.astype(jnp.int32)


def draw_norm_params(key, part):
    gain_key = jax.random.fold_in(key, 11)
    bias_key = jax.random.fold_in(key, 12)
    gains = jnp.clip(1.0 + 0.1 * jax.random.normal(gain_key, (2, D), jnp.float32), 0.6, 1.4)
    biases = jnp.clip(0.2 * jax.random.normal(bias_key, (2, D), jnp.float32), -0.8, 0.8)
    return jnp.stack([gains[0], biases[0], gains[1], biases[1]], 0)


def plant(entries, stream_key, smallest, high):
    index_at = [jax.random.randint(jax.random.fold_in(stream_key, axis), (), 0, length) for axis, length in enumerate(entries.shape)]
    longest = entries.shape.index(max(entries.shape))
    neighbour = index_at[:longest] + [(index_at[longest] + 1) % entries.shape[longest]] + index_at[longest + 1:]
    return entries.at[tuple(index_at)].set(smallest).at[tuple(neighbour)].set(high)


def block_levels(key, dims, shards, least, top_value):
    level, own = 1.0, jax.random.fold_in(key, 6)
    for dim, shards_of in shards:
        steps = jnp.exp(jax.random.uniform(jax.random.fold_in(own, dim), (shards_of,), jnp.float32, least / len(shards), top_value / len(shards)))
        level = level * jnp.repeat(steps, dims[dim] // shards_of).reshape([-1 if axis == dim else 1 for axis in range(len(dims))])
    return level


def gaussian(own_key, shape, scale, reach, split=(), kind=jnp.bfloat16):
    entries = jax.random.normal(own_key, shape, jnp.float32) * scale
    if len(split) > 0:
        entries = block_levels(own_key, shape, split, -0.22, 0.18) * entries
    return jnp.clip(entries, min=-reach, max=reach).astype(kind)


def setup_inputs(seed: int = 0) -> dict:
    streams_of = jax.random.split(jax.random.key(seed), 21)
    return {
        "block_input": gaussian(streams_of[0], (TOKENS, D), 1.0, 6.0, ((0, 32),)),
        "out_cotangent": gaussian(streams_of[1], (TOKENS, D), 1.0, 6.0, ((0, 32),)),
        "objective": draw_objective(jax.random.fold_in(streams_of[20], 71), 0),
        "prefix_len": plant(jax.random.randint(streams_of[3], (SEQS,), LEN // 8, LEN), jax.random.fold_in(streams_of[3], 1), LEN // 8, LEN - 1).astype(jnp.int32),
        "target_mask": draw_target_mask(jax.random.fold_in(streams_of[20], 71), 0),
        "qkv_weight": gaussian(streams_of[5], (D, 3, D), D ** -0.5, 0.125, ((0, 4), (2, 8)), jnp.float32),
        "out_weight": gaussian(streams_of[6], (D, D), 4 ** -0.5, 3.0, ((0, 8), (1, 4)), jnp.float32),
        "gateup_weight": gaussian(streams_of[7], (D, 2, FF_PAD), D ** -0.5, 0.125, ((0, 4), (2, 8)), jnp.float32),
        "down_weight": gaussian(streams_of[8], (FF_PAD, D), (FF_PAD // 64) ** -0.5, 0.625, ((0, 8), (1, 4)), jnp.float32),
        "norm_params": draw_norm_params(jax.random.fold_in(streams_of[20], 71), 0),
        "qkv_first": gaussian(streams_of[10], (D, 3, D), (0.71 * TOKENS ** -0.5), 0.125, ((0, 4), (2, 8)), jnp.float32),
        "out_first": gaussian(streams_of[11], (D, D), (0.034 * TOKENS ** -0.5), 0.005859375, ((0, 8), (1, 4)), jnp.float32),
        "gateup_first": gaussian(streams_of[12], (D, 2, FF_PAD), (0.57 * TOKENS ** -0.5), 0.09375, ((0, 4), (2, 8)), jnp.float32),
        "down_first": gaussian(streams_of[13], (FF_PAD, D), (0.085 * TOKENS ** -0.5), 0.013671875, ((0, 8), (1, 4)), jnp.float32),
        "norm_first": gaussian(streams_of[14], (4, D), (1.41 * TOKENS ** -0.5), 0.21875, (), jnp.float32),
        "qkv_second": jnp.clip(jnp.exp(math.log(0.00048828125) - 2.7725887 * jax.random.uniform(streams_of[15], (D, 3, D), jnp.float32) ** block_levels(streams_of[15], (D, 3, D), ((0, 4), (2, 8)), -0.2, 0.2)), 3.0517578125e-05, 0.00048828125),
        "out_second": jnp.clip(jnp.exp(math.log(1.1230468999201548e-06) - 2.7639307 * jax.random.uniform(streams_of[16], (D, D), jnp.float32) ** block_levels(streams_of[16], (D, D), ((0, 8), (1, 4)), -0.2, 0.2)), 7.080078034960025e-08, 1.1230468999201548e-06),
        "gateup_second": jnp.clip(jnp.exp(math.log(0.0003125) - 2.7725887 * jax.random.uniform(streams_of[17], (D, 2, FF_PAD), jnp.float32) ** block_levels(streams_of[17], (D, 2, FF_PAD), ((0, 4), (2, 8)), -0.2, 0.2)), 1.9531249563442543e-05, 0.0003125),
        "down_second": jnp.clip(jnp.exp(math.log(7.080077921273187e-06) - 2.779509 * jax.random.uniform(streams_of[18], (FF_PAD, D), jnp.float32) ** block_levels(streams_of[18], (FF_PAD, D), ((0, 8), (1, 4)), -0.2, 0.2)), 4.39453117451194e-07, 7.080077921273187e-06),
        "norm_second": jnp.clip(jnp.exp(jax.random.uniform(streams_of[19], (4, D), jnp.float32, math.log(0.00012207031), math.log(0.001953125))), 0.00012207031, 0.001953125),
    }


highest = lax.Precision.HIGHEST
deep_alpha = 48.0 ** 0.5
norm_eps = 1e-05
masked_score = -1e+30
rope_base = 10000.0
beta_one = 0.5
beta_two = 0.5
adam_eps = 1e-08
decay_rate = 0.1

@jax.custom_vjp
def low(v):
    return lax.optimization_barrier(v.astype(jnp.bfloat16)).astype(jnp.float32)

@jax.custom_vjp
def low_back(v):
    return v

def low_keep(v):
    return (low(v), None)

def low_pass(kept, grad):
    return (grad,)

def back_keep(v):
    return (v, None)

def back_low(kept, grad):
    return (low(grad),)
low.defvjp(low_keep, low_pass)
low_back.defvjp(back_keep, back_low)

def rope_tables():
    position = jnp.arange(LEN, dtype=jnp.float32)
    freqs = rope_base ** (-jnp.arange(0, HD, 2, dtype=jnp.float32) / HD)
    angles = position[:, None] * freqs[None, :]
    return (jnp.cos(angles), jnp.sin(angles))

def rotate(values, cosine, sine_table):
    half_dim = values.shape[-1] // 2
    first_half = values[..., :half_dim]
    second_half = values[..., half_dim:]
    cos_b = cosine[:, None, :]
    sin_b = sine_table[:, None, :]
    return jnp.concatenate([first_half * cos_b - second_half * sin_b, second_half * cos_b + first_half * sin_b], -1)

def layer_norm(hidden, norm_gain, norm_bias):
    row_mean = lax.optimization_barrier(jnp.mean(hidden, -1, keepdims=True))
    centred = hidden - row_mean
    variance = lax.optimization_barrier(jnp.mean(centred * centred, -1, keepdims=True))
    return centred * lax.rsqrt(variance + norm_eps) * norm_gain + norm_bias

def attend(query_rows, key_rows, value_rows, objective_flag, prefix_size):
    scores = jnp.einsum('ihe,jhe->hij', query_rows, key_rows, precision=highest) * HD ** (-0.5)
    scores = low_back(scores)
    row_index = jnp.arange(LEN)[:, None]
    col_index = jnp.arange(LEN)[None, :]
    visible = (objective_flag > 0) | (col_index < prefix_size) | (col_index <= row_index)
    scores = jnp.where(visible[None], scores, masked_score)
    soft_low = low(jax.nn.softmax(scores, axis=-1))
    return jnp.einsum('hij,jhe->ihe', soft_low, value_rows, precision=highest)

def attend_items(group_items):
    return attend(group_items[0], group_items[1], group_items[2], group_items[3], group_items[4])

def group_forward(weights, group_input, group_flags, group_prefix):
    qkv_w, out_w, gateup_w, down_w, norm_w = weights
    rows_total = group_input.shape[0]
    projected = low_back(jnp.einsum('td,dce->tce', group_input, qkv_w, precision=highest))
    shaped = projected.reshape(SEQ_DEV, LEN, 3, HEADS, HD)
    cosine, sine_table = rope_tables()
    query_rows = low(rotate(shaped[:, :, 0], cosine, sine_table))
    key_rows = low(rotate(shaped[:, :, 1], cosine, sine_table))
    value_rows = low(shaped[:, :, 2])
    attention_out = lax.map(jax.checkpoint(attend_items), (query_rows, key_rows, value_rows, group_flags, group_prefix))
    attended = low(low_back(attention_out.reshape(rows_total, HEADS * HD)))
    attn_branch = low_back(jnp.dot(attended, out_w, precision=highest, preferred_element_type=jnp.float32))
    hidden_one = deep_alpha * group_input + attn_branch
    middle = layer_norm(hidden_one, norm_w[0], norm_w[1])
    middle_low = low(middle)
    gate_up = low_back(jnp.einsum('td,dcf->tcf', middle_low, gateup_w, precision=highest))
    live_units = (jnp.arange(FF_PAD) < FF).astype(jnp.float32)
    hidden = jax.nn.gelu(gate_up[:, 0]) * gate_up[:, 1] * live_units
    hidden_low = low(hidden)
    ffn_branch = low_back(jnp.dot(hidden_low, down_w, precision=highest, preferred_element_type=jnp.float32))
    hidden_two = deep_alpha * middle + ffn_branch
    return layer_norm(hidden_two, norm_w[2], norm_w[3])

def forward(objective, prefix_len, block_f32, qkv_weight, out_weight, gateup_weight, down_weight, norm_params):
    weights = (low(qkv_weight), low(out_weight), low(gateup_weight), low(down_weight), norm_params)
    checked = jax.checkpoint(group_forward)

    def scan_step(carried, group_items):
        return (carried, checked(weights, group_items[0], group_items[1], group_items[2]))
    grouped = (block_f32.reshape(N_DP, SEQ_DEV * LEN, D), objective.reshape(N_DP, SEQ_DEV), prefix_len.reshape(N_DP, SEQ_DEV))
    _, outputs = lax.scan(scan_step, jnp.zeros((), jnp.float32), grouped)
    return outputs.reshape(N_DP * SEQ_DEV * LEN, D)

def adamw(weight, gradient, first_moment, second, step_rate):
    first_new = beta_one * first_moment + (1.0 - beta_one) * gradient
    second_new = beta_two * second + (1.0 - beta_two) * gradient * gradient
    first_hat = first_new / (1.0 - beta_one ** STEP)
    second_hat = second_new / (1.0 - beta_two ** STEP)
    weight_new = weight - step_rate * (first_hat / (jnp.sqrt(second_hat) + adam_eps) + decay_rate * weight)
    return (weight_new, first_new, second_new)

def reference(block_input, out_cotangent, objective, prefix_len, target_mask, qkv_weight, out_weight, gateup_weight, down_weight, norm_params, qkv_first, out_first, gateup_first, down_first, norm_first, qkv_second, out_second, gateup_second, down_second, norm_second):
    block_f32 = block_input.astype(jnp.float32)
    output_f32, pullback = jax.vjp(partial(forward, objective, prefix_len), block_f32, qkv_weight, out_weight, gateup_weight, down_weight, norm_params)
    mask_f32 = target_mask.astype(jnp.float32)
    seed_rows = out_cotangent.astype(jnp.float32) * mask_f32[:, None]
    gradients = pullback(seed_rows)
    target_count = jnp.sum(mask_f32)
    gradients = [grad_part / target_count for grad_part in gradients]
    rate_list = (D ** (-0.5), 0.5, D ** (-0.5), (FF_PAD // 64) ** (-0.5), 0.4)
    qkv_res = adamw(qkv_weight, gradients[1], qkv_first, qkv_second, rate_list[0])
    out_res = adamw(out_weight, gradients[2], out_first, out_second, rate_list[1])
    gateup_res = adamw(gateup_weight, gradients[3], gateup_first, gateup_second, rate_list[2])
    down_res = adamw(down_weight, gradients[4], down_first, down_second, rate_list[3])
    norm_res = adamw(norm_params, gradients[5], norm_first, norm_second, rate_list[4])
    return (output_f32.astype(jnp.bfloat16), gradients[0], qkv_res[0], qkv_res[1], qkv_res[2], out_res[0], out_res[1], out_res[2], gateup_res[0], gateup_res[1], gateup_res[2], down_res[0], down_res[1], down_res[2], norm_res[0], norm_res[1], norm_res[2])
```

```python
import functools

import jax
import jax.numpy as jnp
from jax import lax
from jax.experimental import pallas as pl
from jax.experimental.pallas import tpu as pltpu
from jax.sharding import PartitionSpec as P

D = 2048
HD = 128
FF = 5461
FF_PAD = 5472
STEP = 5


deep_alpha = 48.0**0.5
norm_eps = 1e-05
masked_score = -1e30
rope_base = 10000.0
beta_one = 0.5
beta_two = 0.5
adam_eps = 1e-08
decay_rate = 0.1


def rope_tables(position, head_dim):
    freqs = rope_base ** (-jnp.arange(0, head_dim, 2, dtype=jnp.float32) / head_dim)
    angles = position.astype(jnp.float32)[:, None] * freqs[None, :]
    cosine, sine = jnp.cos(angles), jnp.sin(angles)
    return (jnp.concatenate([cosine, cosine], -1), jnp.concatenate([-sine, sine], -1))


def turn(values, cosine, sine):
    return values * cosine + pltpu.roll(values, HD // 2, 1) * sine


def dot_nt(left, right):
    return lax.dot_general(
        left, right, (((1,), (1,)), ((), ())), preferred_element_type=jnp.float32
    )


def dot_nn(left, right):
    return lax.dot_general(
        left, right, (((1,), (0,)), ((), ())), preferred_element_type=jnp.float32
    )


def dot_tn(left, right):
    return lax.dot_general(
        left, right, (((0,), (0,)), ((), ())), preferred_element_type=jnp.float32
    )


def soft_rows(info_ref, query, key):
    seq_len = query.shape[0]
    flip = info_ref[2]
    row_at = lax.broadcasted_iota(jnp.int32, (seq_len, seq_len), 0) ^ flip
    col_at = lax.broadcasted_iota(jnp.int32, (seq_len, seq_len), 1) ^ flip
    bound = jnp.where(info_ref[0] > 0, seq_len, info_ref[1])
    visible = (col_at < bound) | (col_at <= row_at)
    scores = jnp.where(visible, dot_nt(query, key) * HD ** (-0.5), masked_score)
    exp_scores = jnp.exp(scores - jnp.max(scores, -1, keepdims=True))
    return exp_scores / jnp.sum(exp_scores, -1, keepdims=True)


def attend_kernel(info_ref, proj_ref, cos_ref, sin_ref, query_ref, key_ref, value_ref, out_ref):
    local_dim = out_ref.shape[1]
    cosine, sine = cos_ref[...], sin_ref[...]
    for start in range(0, local_dim, HD):
        cols = slice(start, start + HD)
        query = turn(proj_ref[:, start : start + HD], cosine, sine).astype(jnp.bfloat16)
        key_at = local_dim + start
        key = turn(proj_ref[:, key_at : key_at + HD], cosine, sine).astype(jnp.bfloat16)
        value_at = 2 * local_dim + start
        value = proj_ref[:, value_at : value_at + HD].astype(jnp.bfloat16)
        soft = soft_rows(info_ref, query, key).astype(jnp.bfloat16)
        query_ref[:, cols] = query
        key_ref[:, cols] = key
        value_ref[:, cols] = value
        out_ref[:, cols] = dot_nn(soft, value).astype(jnp.bfloat16)


def attend_back_kernel(
    info_ref, query_ref, key_ref, value_ref, grad_ref, cos_ref, sin_ref, out_ref
):
    local_dim = grad_ref.shape[1]
    cosine, sine = cos_ref[...], sin_ref[...]
    scale = HD ** (-0.5)
    for start in range(0, local_dim, HD):
        cols = slice(start, start + HD)
        query, key, value = query_ref[:, cols], key_ref[:, cols], value_ref[:, cols]
        grad = grad_ref[:, cols]
        soft = soft_rows(info_ref, query, key)
        grad_soft = dot_nt(grad, value)
        row_dot = jnp.sum(soft * grad_soft, -1, keepdims=True)
        grad_scores = (soft * (grad_soft - row_dot)).astype(jnp.bfloat16)
        value_grad = dot_tn(soft.astype(jnp.bfloat16), grad)
        query_grad = turn(dot_nn(grad_scores, key) * scale, cosine, -sine)
        key_grad = turn(dot_tn(grad_scores, query) * scale, cosine, -sine)
        for index, rows in enumerate((query_grad, key_grad, value_grad)):
            at = index * local_dim + start
            out_ref[:, at : at + HD] = rows.astype(jnp.bfloat16)


def attend_forward(info, proj, cosine, sine):
    seq_len, width = proj.shape
    low = jax.ShapeDtypeStruct((seq_len, width // 3), jnp.bfloat16)
    vmem = pl.BlockSpec(memory_space=pltpu.VMEM)
    return pl.pallas_call(
        attend_kernel,
        out_shape=(low, low, low, low),
        in_specs=[pl.BlockSpec(memory_space=pltpu.SMEM), vmem, vmem, vmem],
        out_specs=(vmem, vmem, vmem, vmem),
        name="attend_forward",
    )(info, proj, cosine, sine)


def attend_backward(info, query, key, value, grad, cosine, sine):
    seq_len, local_dim = query.shape
    vmem = pl.BlockSpec(memory_space=pltpu.VMEM)
    return pl.pallas_call(
        attend_back_kernel,
        out_shape=jax.ShapeDtypeStruct((seq_len, 3 * local_dim), jnp.bfloat16),
        in_specs=[pl.BlockSpec(memory_space=pltpu.SMEM)] + [vmem] * 6,
        out_specs=vmem,
        name="attend_backward",
    )(info, query, key, value, grad, cosine, sine)


def norm_forward(hidden, norm_gain, norm_bias):
    row_mean = jnp.mean(hidden, -1, keepdims=True)
    centred = hidden - row_mean
    variance = jnp.mean(centred * centred, -1, keepdims=True)
    inv_std = lax.rsqrt(variance + norm_eps)
    normed = centred * inv_std
    return (normed * norm_gain + norm_bias, normed, inv_std)


def norm_backward(grad_rows, normed, inv_std, norm_gain):
    grad_normed = grad_rows * norm_gain
    mean_grad = jnp.mean(grad_normed, -1, keepdims=True)
    mean_proj = jnp.mean(grad_normed * normed, -1, keepdims=True)
    grad_in = inv_std * (grad_normed - mean_grad - normed * mean_proj)
    return (grad_in, jnp.sum(grad_rows * normed, 0), jnp.sum(grad_rows, 0))


def adamw(weight, gradient, first_moment, second, step_rate):
    first_new = beta_one * first_moment + (1.0 - beta_one) * gradient
    second_new = beta_two * second + (1.0 - beta_two) * gradient * gradient
    first_hat = first_new / (1.0 - beta_one**STEP)
    second_hat = second_new / (1.0 - beta_two**STEP)
    weight_new = weight - step_rate * (
        first_hat / (jnp.sqrt(second_hat) + adam_eps) + decay_rate * weight
    )
    return (weight_new, first_new, second_new)


def swap(values, axis, bit):
    size = lax.axis_size(axis)
    return lax.ppermute(values, axis, [(at, at ^ bit) for at in range(size)])


def sum_everywhere(values):
    for axis in ("mp", "dp"):
        bit = 1
        while bit < lax.axis_size(axis):
            values = values + swap(values, axis, bit)
            bit *= 2
    return values


def gather_near(rows):
    half = rows.shape[0] // 2
    near_x, near_y = swap(rows, "mp", 2), swap(rows, "mp", 4)
    far_low, far_high = swap(near_x[:half], "mp", 4), swap(near_y[half:], "mp", 2)
    mates = [swap(part, "mp", 1) for part in (rows, near_x, near_y, far_low, far_high)]
    return [
        jnp.concatenate(parts, 0)
        for parts in (
            (rows, mates[0]),
            (near_x, mates[1]),
            (near_y, mates[2]),
            (far_low, far_high, mates[3], mates[4]),
        )
    ]


def scatter_near(parts):
    own_rows = parts[0].shape[0] // 2
    half = own_rows // 2
    sums = [
        part[:own_rows].astype(jnp.float32)
        + swap(part[own_rows:].astype(jnp.bfloat16), "mp", 1).astype(jnp.float32)
        for part in parts
    ]
    far = sums[3].astype(jnp.bfloat16)
    far_low, far_high = swap(far[:half], "mp", 4), swap(far[half:], "mp", 2)
    x_low = (sums[1][:half] + far_low.astype(jnp.float32)).astype(jnp.bfloat16)
    y_high = (sums[2][half:] + far_high.astype(jnp.float32)).astype(jnp.bfloat16)
    x_high, y_low = sums[1][half:].astype(jnp.bfloat16), sums[2][:half].astype(jnp.bfloat16)
    x_low, x_high = swap(x_low, "mp", 2), swap(x_high, "mp", 2)
    y_low, y_high = swap(y_low, "mp", 4), swap(y_high, "mp", 4)
    across_x = jnp.concatenate([x_low, x_high], 0).astype(jnp.float32)
    across_y = jnp.concatenate([y_low, y_high], 0).astype(jnp.float32)
    return sums[0] + across_x + across_y


def gather_all(rows, seq_count):
    whole = lax.all_gather(rows, "mp", axis=0, tiled=True)
    return jnp.split(whole, seq_count, 0)


def scatter_all(parts):
    whole = jnp.concatenate(parts, 0).astype(jnp.bfloat16)
    return lax.psum_scatter(whole, "mp", scatter_dimension=0, tiled=True).astype(jnp.float32)


def local(
    block_input,
    out_cotangent,
    objective,
    prefix_len,
    target_mask,
    qkv_weight,
    out_weight,
    gateup_weight,
    down_weight,
    norm_params,
    qkv_first,
    out_first,
    gateup_first,
    down_first,
    norm_first,
    qkv_second,
    out_second,
    gateup_second,
    down_second,
    norm_second,
):
    mp_index = lax.axis_index("mp")
    own_rows = block_input.shape[0]
    seq_count = objective.shape[0]
    seq_len = own_rows * lax.axis_size("mp") // seq_count
    shard_rows, _, local_dim = qkv_weight.shape
    local_units = gateup_weight.shape[2]
    seqs = range(seq_count)
    near = lax.axis_size("mp") == 8 and seq_count == 4 and own_rows % 32 == 0
    if near:
        gather_rows, scatter_rows = gather_near, scatter_near
        flip = (mp_index % 2) * own_rows
        seq_at = [(mp_index // 2) ^ seq for seq in seqs]
    else:
        gather_rows = functools.partial(gather_all, seq_count=seq_count)
        scatter_rows = scatter_all
        flip = jnp.zeros((), jnp.int32)
        seq_at = list(seqs)
    infos = [
        jnp.stack([objective[at], prefix_len[at], flip.astype(jnp.int32)]) for at in seq_at
    ]
    cosine, sine = rope_tables(jnp.arange(seq_len, dtype=jnp.int32) ^ flip, HD)

    qkv_low = qkv_weight.astype(jnp.bfloat16).reshape(shard_rows, 3 * local_dim)
    qkv_full = lax.all_gather(qkv_low, "dp", axis=0, tiled=True)
    out_full = lax.all_gather(out_weight.astype(jnp.bfloat16), "dp", axis=1, tiled=True)
    gateup_full = lax.all_gather(gateup_weight.astype(jnp.bfloat16), "dp", axis=0, tiled=True)
    down_full = lax.all_gather(down_weight.astype(jnp.bfloat16), "dp", axis=1, tiled=True)

    mask_f32 = target_mask.astype(jnp.float32)
    target_count = sum_everywhere(jnp.full((8, 128), jnp.sum(mask_f32)))[0, 0]

    inputs = gather_rows(block_input)
    attended, kept = [], []
    for seq in seqs:
        proj = jnp.dot(inputs[seq], qkv_full, preferred_element_type=jnp.float32)
        query, key, value, out = attend_forward(infos[seq], proj, cosine, sine)
        kept.append((query, key, value))
        attended.append(out)
    attn_own = scatter_rows(
        [jnp.dot(rows, out_full, preferred_element_type=jnp.bfloat16) for rows in attended]
    )
    hidden_one = deep_alpha * block_input.astype(jnp.float32) + attn_own
    middle, normed_one, inv_one = norm_forward(hidden_one, norm_params[0], norm_params[1])
    middles = gather_rows(middle.astype(jnp.bfloat16))

    live_units = (mp_index * local_units + jnp.arange(local_units) < FF).astype(jnp.float32)
    gate_ups = [
        jnp.einsum("td,dcf->tcf", rows, gateup_full, preferred_element_type=jnp.float32)
        for rows in middles
    ]
    hiddens = [
        (jax.nn.gelu(gate_up[:, 0]) * gate_up[:, 1] * live_units).astype(jnp.bfloat16)
        for gate_up in gate_ups
    ]
    ffn_own = scatter_rows(
        [jnp.dot(rows, down_full, preferred_element_type=jnp.bfloat16) for rows in hiddens]
    )
    hidden_two = deep_alpha * middle + ffn_own
    output_rows, normed_two, inv_two = norm_forward(hidden_two, norm_params[2], norm_params[3])
    grad_rows = out_cotangent.astype(jnp.float32) * mask_f32[:, None]
    grad_two, gain_two, bias_two = norm_backward(grad_rows, normed_two, inv_two, norm_params[2])

    ffn_backs = gather_rows(grad_two.astype(jnp.bfloat16))
    grad_gateups, middle_parts = [], []
    for seq in seqs:
        gate_act, gelu_pull = jax.vjp(jax.nn.gelu, gate_ups[seq][:, 0])
        grad_hidden = (
            jnp.einsum("td,fd->tf", ffn_backs[seq], down_full, preferred_element_type=jnp.float32)
            * live_units
        )
        grad_gate = gelu_pull(grad_hidden * gate_ups[seq][:, 1])[0]
        grad_up = grad_hidden * gate_act
        grad_gateup = jnp.stack([grad_gate, grad_up], 1).astype(jnp.bfloat16)
        grad_gateups.append(grad_gateup)
        middle_parts.append(
            jnp.einsum(
                "tcf,dcf->td", grad_gateup, gateup_full, preferred_element_type=jnp.bfloat16
            )
        )
    ffn_back_all = jnp.concatenate(ffn_backs, 0)
    down_grad = jnp.einsum(
        "tf,td->fd", jnp.concatenate(hiddens, 0), ffn_back_all, preferred_element_type=jnp.bfloat16
    )
    gateup_grad = jnp.einsum(
        "td,tcf->dcf",
        jnp.concatenate(middles, 0),
        jnp.concatenate(grad_gateups, 0),
        preferred_element_type=jnp.bfloat16,
    )
    grad_middle = scatter_rows(middle_parts) + deep_alpha * grad_two
    grad_one, gain_one, bias_one = norm_backward(grad_middle, normed_one, inv_one, norm_params[0])

    attn_backs = gather_rows(grad_one.astype(jnp.bfloat16))
    grad_projs = []
    for seq in seqs:
        grad_attended = jnp.einsum(
            "td,ed->te", attn_backs[seq], out_full, preferred_element_type=jnp.float32
        ).astype(jnp.bfloat16)
        grad_projs.append(attend_backward(infos[seq], *kept[seq], grad_attended, cosine, sine))
    out_grad = jnp.einsum(
        "te,td->ed",
        jnp.concatenate(attended, 0),
        jnp.concatenate(attn_backs, 0),
        preferred_element_type=jnp.bfloat16,
    )
    qkv_grad = jnp.einsum(
        "td,te->de",
        jnp.concatenate(inputs, 0),
        jnp.concatenate(grad_projs, 0),
        preferred_element_type=jnp.bfloat16,
    )
    input_raw = (
        scatter_rows(
            [
                jnp.einsum("te,de->td", rows, qkv_full, preferred_element_type=jnp.bfloat16)
                for rows in grad_projs
            ]
        )
        + deep_alpha * grad_one
    )
    qkv_grad, out_grad, gateup_grad, down_grad = (
        lax.psum_scatter(qkv_grad, "dp", scatter_dimension=0, tiled=True)
        .astype(jnp.float32)
        .reshape(qkv_weight.shape),
        lax.psum_scatter(out_grad, "dp", scatter_dimension=1, tiled=True).astype(jnp.float32),
        lax.psum_scatter(gateup_grad, "dp", scatter_dimension=0, tiled=True).astype(jnp.float32),
        lax.psum_scatter(down_grad, "dp", scatter_dimension=1, tiled=True).astype(jnp.float32),
    )
    norm_grad = sum_everywhere(jnp.stack([gain_one, bias_one, gain_two, bias_two], 0))
    rate_list = (D ** (-0.5), 0.5, D ** (-0.5), (FF_PAD // 64) ** (-0.5), 0.4)
    qkv_res = adamw(qkv_weight, qkv_grad / target_count, qkv_first, qkv_second, rate_list[0])
    out_res = adamw(out_weight, out_grad / target_count, out_first, out_second, rate_list[1])
    gateup_res = adamw(
        gateup_weight, gateup_grad / target_count, gateup_first, gateup_second, rate_list[2]
    )
    down_res = adamw(down_weight, down_grad / target_count, down_first, down_second, rate_list[3])
    norm_res = adamw(norm_params, norm_grad / target_count, norm_first, norm_second, rate_list[4])
    return (
        output_rows.astype(jnp.bfloat16),
        input_raw / target_count,
        qkv_res[0],
        qkv_res[1],
        qkv_res[2],
        out_res[0],
        out_res[1],
        out_res[2],
        gateup_res[0],
        gateup_res[1],
        gateup_res[2],
        down_res[0],
        down_res[1],
        down_res[2],
        norm_res[0],
        norm_res[1],
        norm_res[2],
    )


def solution(mesh):
    return jax.shard_map(
        local,
        mesh=mesh,
        in_specs=(
            P(("dp", "mp"), None),
            P(("dp", "mp"), None),
            P("dp"),
            P("dp"),
            P(("dp", "mp")),
            P("dp", None, "mp"),
            P("mp", "dp"),
            P("dp", None, "mp"),
            P("mp", "dp"),
            P(),
            P("dp", None, "mp"),
            P("mp", "dp"),
            P("dp", None, "mp"),
            P("mp", "dp"),
            P(),
            P("dp", None, "mp"),
            P("mp", "dp"),
            P("dp", None, "mp"),
            P("mp", "dp"),
            P(),
        ),
        out_specs=(
            P(("dp", "mp"), None),
            P(("dp", "mp"), None),
            P("dp", None, "mp"),
            P("dp", None, "mp"),
            P("dp", None, "mp"),
            P("mp", "dp"),
            P("mp", "dp"),
            P("mp", "dp"),
            P("dp", None, "mp"),
            P("dp", None, "mp"),
            P("dp", None, "mp"),
            P("mp", "dp"),
            P("mp", "dp"),
            P("mp", "dp"),
            P(),
            P(),
            P(),
        ),
        check_vma=False,
    )
```

```python
import functools

import jax
import jax.numpy as jnp
from jax import lax
from jax.experimental import pallas as pl
from jax.experimental.pallas import tpu as pltpu
from jax.sharding import PartitionSpec as P

D = 2048
HD = 128
FF = 5461
FF_PAD = 5472
STEP = 5


deep_alpha = 48.0**0.5
norm_eps = 1e-05
masked_score = -1e30
rope_base = 10000.0
beta_one = 0.5
beta_two = 0.5
adam_eps = 1e-08
decay_rate = 0.1


def rope_tables(position, head_dim):
    freqs = rope_base ** (-jnp.arange(0, head_dim, 2, dtype=jnp.float32) / head_dim)
    angles = position.astype(jnp.float32)[:, None] * freqs[None, :]
    cosine, sine = jnp.cos(angles), jnp.sin(angles)
    return (jnp.concatenate([cosine, cosine], -1), jnp.concatenate([-sine, sine], -1))


def turn(values, cosine, sine):
    return values * cosine + pltpu.roll(values, HD // 2, 1) * sine


def dot_nt(left, right):
    return lax.dot_general(
        left, right, (((1,), (1,)), ((), ())), preferred_element_type=jnp.float32
    )


def dot_nn(left, right):
    return lax.dot_general(
        left, right, (((1,), (0,)), ((), ())), preferred_element_type=jnp.float32
    )


def dot_tn(left, right):
    return lax.dot_general(
        left, right, (((0,), (0,)), ((), ())), preferred_element_type=jnp.float32
    )


def soft_rows(info_ref, query, key):
    seq_len = query.shape[0]
    flip = info_ref[2]
    row_at = lax.broadcasted_iota(jnp.int32, (seq_len, seq_len), 0) ^ flip
    col_at = lax.broadcasted_iota(jnp.int32, (seq_len, seq_len), 1) ^ flip
    bound = jnp.where(info_ref[0] > 0, seq_len, info_ref[1])
    visible = (col_at < bound) | (col_at <= row_at)
    scores = jnp.where(visible, dot_nt(query, key) * HD ** (-0.5), masked_score)
    exp_scores = jnp.exp(scores - jnp.max(scores, -1, keepdims=True))
    return exp_scores / jnp.sum(exp_scores, -1, keepdims=True)


def attend_kernel(info_ref, proj_ref, cos_ref, sin_ref, query_ref, key_ref, value_ref, out_ref):
    local_dim = out_ref.shape[1]
    cosine, sine = cos_ref[...], sin_ref[...]
    for start in range(0, local_dim, HD):
        cols = slice(start, start + HD)
        query = turn(proj_ref[:, start : start + HD], cosine, sine).astype(jnp.bfloat16)
        key_at = local_dim + start
        key = turn(proj_ref[:, key_at : key_at + HD], cosine, sine).astype(jnp.bfloat16)
        value_at = 2 * local_dim + start
        value = proj_ref[:, value_at : value_at + HD].astype(jnp.bfloat16)
        soft = soft_rows(info_ref, query, key).astype(jnp.bfloat16)
        query_ref[:, cols] = query
        key_ref[:, cols] = key
        value_ref[:, cols] = value
        out_ref[:, cols] = dot_nn(soft, value).astype(jnp.bfloat16)


def attend_back_kernel(
    info_ref, query_ref, key_ref, value_ref, grad_ref, cos_ref, sin_ref, out_ref
):
    local_dim = grad_ref.shape[1]
    cosine, sine = cos_ref[...], sin_ref[...]
    scale = HD ** (-0.5)
    for start in range(0, local_dim, HD):
        cols = slice(start, start + HD)
        query, key, value = query_ref[:, cols], key_ref[:, cols], value_ref[:, cols]
        grad = grad_ref[:, cols]
        soft = soft_rows(info_ref, query, key)
        grad_soft = dot_nt(grad, value)
        row_dot = jnp.sum(soft * grad_soft, -1, keepdims=True)
        grad_scores = (soft * (grad_soft - row_dot)).astype(jnp.bfloat16)
        value_grad = dot_tn(soft.astype(jnp.bfloat16), grad)
        query_grad = turn(dot_nn(grad_scores, key) * scale, cosine, -sine)
        key_grad = turn(dot_tn(grad_scores, query) * scale, cosine, -sine)
        for index, rows in enumerate((query_grad, key_grad, value_grad)):
            at = index * local_dim + start
            out_ref[:, at : at + HD] = rows.astype(jnp.bfloat16)


def attend_forward(info, proj, cosine, sine):
    seq_len, width = proj.shape
    low = jax.ShapeDtypeStruct((seq_len, width // 3), jnp.bfloat16)
    vmem = pl.BlockSpec(memory_space=pltpu.VMEM)
    return pl.pallas_call(
        attend_kernel,
        out_shape=(low, low, low, low),
        in_specs=[pl.BlockSpec(memory_space=pltpu.SMEM), vmem, vmem, vmem],
        out_specs=(vmem, vmem, vmem, vmem),
        name="attend_forward",
    )(info, proj, cosine, sine)


def attend_backward(info, query, key, value, grad, cosine, sine):
    seq_len, local_dim = query.shape
    vmem = pl.BlockSpec(memory_space=pltpu.VMEM)
    return pl.pallas_call(
        attend_back_kernel,
        out_shape=jax.ShapeDtypeStruct((seq_len, 3 * local_dim), jnp.bfloat16),
        in_specs=[pl.BlockSpec(memory_space=pltpu.SMEM)] + [vmem] * 6,
        out_specs=vmem,
        name="attend_backward",
    )(info, query, key, value, grad, cosine, sine)


def norm_forward(hidden, norm_gain, norm_bias):
    row_mean = jnp.mean(hidden, -1, keepdims=True)
    centred = hidden - row_mean
    variance = jnp.mean(centred * centred, -1, keepdims=True)
    inv_std = lax.rsqrt(variance + norm_eps)
    normed = centred * inv_std
    return (normed * norm_gain + norm_bias, normed, inv_std)


def norm_backward(grad_rows, normed, inv_std, norm_gain):
    grad_normed = grad_rows * norm_gain
    mean_grad = jnp.mean(grad_normed, -1, keepdims=True)
    mean_proj = jnp.mean(grad_normed * normed, -1, keepdims=True)
    grad_in = inv_std * (grad_normed - mean_grad - normed * mean_proj)
    return (grad_in, jnp.sum(grad_rows * normed, 0), jnp.sum(grad_rows, 0))


def adamw(weight, gradient, first_moment, second, step_rate):
    first_new = beta_one * first_moment + (1.0 - beta_one) * gradient
    second_new = beta_two * second + (1.0 - beta_two) * gradient * gradient
    first_hat = first_new / (1.0 - beta_one**STEP)
    second_hat = second_new / (1.0 - beta_two**STEP)
    weight_new = weight - step_rate * (
        first_hat / (jnp.sqrt(second_hat) + adam_eps) + decay_rate * weight
    )
    return (weight_new, first_new, second_new)


def swap(values, axis, bit):
    size = lax.axis_size(axis)
    return lax.ppermute(values, axis, [(at, at ^ bit) for at in range(size)])


def sum_everywhere(values):
    for axis in ("mp", "dp"):
        bit = 1
        while bit < lax.axis_size(axis):
            values = values + swap(values, axis, bit)
            bit *= 2
    return values


def assemble_kernel(order_ref, *refs):
    *parts, out_ref, done = refs
    width = parts[0].shape[1]
    copies = []
    for index, part in enumerate(parts):
        at = pl.multiple_of(order_ref[index] * width, width)
        copies.append(
            pltpu.make_async_copy(part, out_ref.at[:, pl.ds(at, width)], done.at[index])
        )
    for copy in copies:
        copy.start()
    for copy in copies:
        copy.wait()


def gather_columns(part):
    count = lax.axis_size("dp")
    parts = [part] + [
        lax.ppermute(part, "dp", [(at, (at + far) % count) for at in range(count)])
        for far in range(1, count)
    ]
    order = (lax.axis_index("dp") - jnp.arange(count, dtype=jnp.int32)) % count
    anywhere = pl.BlockSpec(memory_space=pl.ANY)
    rows, width = part.shape
    return pl.pallas_call(
        assemble_kernel,
        out_shape=jax.ShapeDtypeStruct((rows, width * count), part.dtype),
        in_specs=[pl.BlockSpec(memory_space=pltpu.SMEM)] + [anywhere] * count,
        out_specs=anywhere,
        scratch_shapes=[pltpu.SemaphoreType.DMA((count,))],
        name="assemble",
    )(order, *parts)


def gather_near(rows):
    half = rows.shape[0] // 2
    near_x, near_y = swap(rows, "mp", 2), swap(rows, "mp", 4)
    far_low, far_high = swap(near_x[:half], "mp", 4), swap(near_y[half:], "mp", 2)
    mates = [swap(part, "mp", 1) for part in (rows, near_x, near_y, far_low, far_high)]
    return [
        jnp.concatenate(parts, 0)
        for parts in (
            (rows, mates[0]),
            (near_x, mates[1]),
            (near_y, mates[2]),
            (far_low, far_high, mates[3], mates[4]),
        )
    ]


def scatter_near(parts):
    own_rows = parts[0].shape[0] // 2
    half = own_rows // 2
    sums = [
        part[:own_rows].astype(jnp.float32)
        + swap(part[own_rows:].astype(jnp.bfloat16), "mp", 1).astype(jnp.float32)
        for part in parts
    ]
    far = sums[3].astype(jnp.bfloat16)
    far_low, far_high = swap(far[:half], "mp", 4), swap(far[half:], "mp", 2)
    x_low = (sums[1][:half] + far_low.astype(jnp.float32)).astype(jnp.bfloat16)
    y_high = (sums[2][half:] + far_high.astype(jnp.float32)).astype(jnp.bfloat16)
    x_high, y_low = sums[1][half:].astype(jnp.bfloat16), sums[2][:half].astype(jnp.bfloat16)
    x_low, x_high = swap(x_low, "mp", 2), swap(x_high, "mp", 2)
    y_low, y_high = swap(y_low, "mp", 4), swap(y_high, "mp", 4)
    across_x = jnp.concatenate([x_low, x_high], 0).astype(jnp.float32)
    across_y = jnp.concatenate([y_low, y_high], 0).astype(jnp.float32)
    return sums[0] + across_x + across_y


def gather_all(rows, seq_count):
    whole = lax.all_gather(rows, "mp", axis=0, tiled=True)
    return jnp.split(whole, seq_count, 0)


def scatter_all(parts):
    whole = jnp.concatenate(parts, 0).astype(jnp.bfloat16)
    return lax.psum_scatter(whole, "mp", scatter_dimension=0, tiled=True).astype(jnp.float32)


def adamw_as(order, weight, gradient, first_moment, second, step_rate, scale):
    turned = [jnp.transpose(rows, order) for rows in (weight, first_moment, second)]
    gradient = gradient.astype(jnp.float32) * scale
    news = adamw(turned[0], gradient, turned[1], turned[2], step_rate)
    back = [order.index(dim) for dim in range(len(order))]
    return tuple(jnp.transpose(rows, back) for rows in news)


def local(
    block_input,
    out_cotangent,
    objective,
    prefix_len,
    target_mask,
    qkv_weight,
    out_weight,
    gateup_weight,
    down_weight,
    norm_params,
    qkv_first,
    out_first,
    gateup_first,
    down_first,
    norm_first,
    qkv_second,
    out_second,
    gateup_second,
    down_second,
    norm_second,
):
    mp_index = lax.axis_index("mp")
    own_rows = block_input.shape[0]
    seq_count = objective.shape[0]
    seq_len = own_rows * lax.axis_size("mp") // seq_count
    shard_rows, _, local_dim = qkv_weight.shape
    local_units = gateup_weight.shape[2]
    seqs = range(seq_count)
    near = lax.axis_size("mp") == 8 and seq_count == 4 and own_rows % 32 == 0
    if near:
        gather_rows, scatter_rows = gather_near, scatter_near
        flip = (mp_index % 2) * own_rows
        seq_at = [(mp_index // 2) ^ seq for seq in seqs]
    else:
        gather_rows = functools.partial(gather_all, seq_count=seq_count)
        scatter_rows = scatter_all
        flip = jnp.zeros((), jnp.int32)
        seq_at = list(seqs)
    infos = [
        jnp.stack([objective[at], prefix_len[at], flip.astype(jnp.int32)]) for at in seq_at
    ]
    cosine, sine = rope_tables(jnp.arange(seq_len, dtype=jnp.int32) ^ flip, HD)

    qkv_low = qkv_weight.astype(jnp.bfloat16).reshape(shard_rows, 3 * local_dim)
    qkv_full = lax.all_gather(qkv_low, "dp", axis=0, tiled=True)
    out_full = gather_columns(out_weight.astype(jnp.bfloat16))
    gateup_low = jnp.transpose(gateup_weight, (1, 2, 0)).astype(jnp.bfloat16)
    gateup_full = lax.all_gather(gateup_low, "dp", axis=2, tiled=True)
    down_full = lax.all_gather(down_weight.astype(jnp.bfloat16), "dp", axis=1, tiled=True)

    mask_f32 = target_mask.astype(jnp.float32)
    target_count = sum_everywhere(jnp.full((8, 128), jnp.sum(mask_f32)))[0, 0]

    inputs = gather_rows(block_input)
    attended, kept = [], []
    for seq in seqs:
        proj = jnp.dot(inputs[seq], qkv_full, preferred_element_type=jnp.float32)
        query, key, value, out = attend_forward(infos[seq], proj, cosine, sine)
        kept.append((query, key, value))
        attended.append(out)
    attended, out_full = lax.optimization_barrier((attended, out_full))
    attn_own = scatter_rows(
        [jnp.dot(rows, out_full, preferred_element_type=jnp.bfloat16) for rows in attended]
    )
    hidden_one = deep_alpha * block_input.astype(jnp.float32) + attn_own
    middle, normed_one, inv_one = norm_forward(hidden_one, norm_params[0], norm_params[1])
    middles = gather_rows(middle.astype(jnp.bfloat16))

    live_units = (mp_index * local_units + jnp.arange(local_units) < FF).astype(jnp.float32)
    gate_ups = [
        jnp.einsum("td,cfd->ctf", rows, gateup_full, preferred_element_type=jnp.float32)
        for rows in middles
    ]
    hiddens = [
        (jax.nn.gelu(gate_up[0]) * gate_up[1] * live_units).astype(jnp.bfloat16)
        for gate_up in gate_ups
    ]
    ffn_own = scatter_rows(
        [jnp.dot(rows, down_full, preferred_element_type=jnp.bfloat16) for rows in hiddens]
    )
    hidden_two = deep_alpha * middle + ffn_own
    output_rows, normed_two, inv_two = norm_forward(hidden_two, norm_params[2], norm_params[3])
    grad_rows = out_cotangent.astype(jnp.float32) * mask_f32[:, None]
    grad_two, gain_two, bias_two = norm_backward(grad_rows, normed_two, inv_two, norm_params[2])

    ffn_backs = gather_rows(grad_two.astype(jnp.bfloat16))
    down_grad = jnp.einsum(
        "tf,td->fd",
        jnp.concatenate(hiddens, 0),
        jnp.concatenate(ffn_backs, 0),
        preferred_element_type=jnp.bfloat16,
    )
    ffn_backs[-1], down_grad = lax.optimization_barrier((ffn_backs[-1], down_grad))
    down_grad = lax.psum_scatter(down_grad, "dp", scatter_dimension=1, tiled=True)
    grad_gateups, middle_parts = [], []
    for seq in seqs:
        gate_act, gelu_pull = jax.vjp(jax.nn.gelu, gate_ups[seq][0])
        grad_hidden = (
            jnp.einsum("td,fd->tf", ffn_backs[seq], down_full, preferred_element_type=jnp.float32)
            * live_units
        )
        grad_gate = gelu_pull(grad_hidden * gate_ups[seq][1])[0]
        grad_up = grad_hidden * gate_act
        grad_gateup = jnp.stack([grad_gate, grad_up], 0).astype(jnp.bfloat16)
        grad_gateups.append(grad_gateup)
        middle_parts.append(
            jnp.einsum(
                "ctf,cfd->td", grad_gateup, gateup_full, preferred_element_type=jnp.bfloat16
            )
        )
    gateup_grad = jnp.einsum(
        "ctf,td->cfd",
        jnp.concatenate(grad_gateups, 1),
        jnp.concatenate(middles, 0),
        preferred_element_type=jnp.bfloat16,
    )
    grad_middle = scatter_rows(middle_parts) + deep_alpha * grad_two
    grad_one, gain_one, bias_one = norm_backward(grad_middle, normed_one, inv_one, norm_params[0])

    grad_one_low, gateup_grad = lax.optimization_barrier(
        (grad_one.astype(jnp.bfloat16), gateup_grad)
    )
    gateup_grad, down_grad = lax.optimization_barrier((gateup_grad, down_grad))
    gateup_grad = lax.psum_scatter(gateup_grad, "dp", scatter_dimension=2, tiled=True)
    attn_backs = gather_rows(grad_one_low)
    grad_projs = []
    for seq in seqs:
        grad_attended = jnp.einsum(
            "td,ed->te", attn_backs[seq], out_full, preferred_element_type=jnp.float32
        ).astype(jnp.bfloat16)
        grad_projs.append(attend_backward(infos[seq], *kept[seq], grad_attended, cosine, sine))
    attended, grad_projs = lax.optimization_barrier((attended, grad_projs))
    attend_grad = jnp.concatenate(
        [
            jnp.einsum("te,td->ed", jnp.concatenate(left, 0), jnp.concatenate(right, 0),
                       preferred_element_type=jnp.bfloat16)
            for left, right in ((attended, attn_backs), (grad_projs, inputs))
        ],
        0,
    )
    grad_projs, attend_grad = lax.optimization_barrier((grad_projs, attend_grad))
    attend_grad, gateup_grad = lax.optimization_barrier((attend_grad, gateup_grad))
    attend_grad = lax.psum_scatter(attend_grad, "dp", scatter_dimension=1, tiled=True)
    input_raw = (
        scatter_rows(
            [
                jnp.einsum("te,de->td", rows, qkv_full, preferred_element_type=jnp.bfloat16)
                for rows in grad_projs
            ]
        )
        + deep_alpha * grad_one
    )
    out_grad = attend_grad[:local_dim]
    qkv_grad = attend_grad[local_dim:].reshape(3, local_dim, shard_rows)
    norm_grad = jnp.stack([gain_one, bias_one, gain_two, bias_two], 0)
    norm_grad, input_raw = lax.optimization_barrier((norm_grad, input_raw))
    norm_grad = sum_everywhere(norm_grad)
    rate_list = (D ** (-0.5), 0.5, D ** (-0.5), (FF_PAD // 64) ** (-0.5), 0.4)
    scale = 1.0 / target_count
    qkv_res = adamw_as(
        (1, 0, 2), qkv_weight, qkv_grad.transpose(0, 2, 1), qkv_first, qkv_second, rate_list[0], scale
    )
    out_res = adamw_as((0, 1), out_weight, out_grad, out_first, out_second, rate_list[1], scale)
    gateup_res = adamw_as(
        (2, 1, 0),
        gateup_weight,
        gateup_grad.transpose(1, 0, 2),
        gateup_first,
        gateup_second,
        rate_list[2],
        scale,
    )
    down_res = adamw_as(
        (0, 1), down_weight, down_grad, down_first, down_second, rate_list[3], scale
    )
    norm_res = adamw(norm_params, norm_grad * scale, norm_first, norm_second, rate_list[4])
    return (
        output_rows.astype(jnp.bfloat16),
        input_raw * scale,
        qkv_res[0],
        qkv_res[1],
        qkv_res[2],
        out_res[0],
        out_res[1],
        out_res[2],
        gateup_res[0],
        gateup_res[1],
        gateup_res[2],
        down_res[0],
        down_res[1],
        down_res[2],
        norm_res[0],
        norm_res[1],
        norm_res[2],
    )


def solution(mesh):
    return jax.shard_map(
        local,
        mesh=mesh,
        in_specs=(
            P(("dp", "mp"), None),
            P(("dp", "mp"), None),
            P("dp"),
            P("dp"),
            P(("dp", "mp")),
            P("dp", None, "mp"),
            P("mp", "dp"),
            P("dp", None, "mp"),
            P("mp", "dp"),
            P(),
            P("dp", None, "mp"),
            P("mp", "dp"),
            P("dp", None, "mp"),
            P("mp", "dp"),
            P(),
            P("dp", None, "mp"),
            P("mp", "dp"),
            P("dp", None, "mp"),
            P("mp", "dp"),
            P(),
        ),
        out_specs=(
            P(("dp", "mp"), None),
            P(("dp", "mp"), None),
            P("dp", None, "mp"),
            P("dp", None, "mp"),
            P("dp", None, "mp"),
            P("mp", "dp"),
            P("mp", "dp"),
            P("mp", "dp"),
            P("dp", None, "mp"),
            P("dp", None, "mp"),
            P("dp", None, "mp"),
            P("mp", "dp"),
            P("mp", "dp"),
            P("mp", "dp"),
            P(),
            P(),
            P(),
        ),
        check_vma=False,
    )
```

```python
import jax
import jax.numpy as jnp
from jax import lax
from jax.experimental import pallas as pl
from jax.experimental.layout import Layout, with_layout_constraint
from jax.experimental.pallas import tpu as pltpu
from jax.sharding import PartitionSpec as P

D = 2048
HD = 128
FF = 5461
FF_PAD = 5472
STEP = 5


deep_alpha = 48.0**0.5
norm_eps = 1e-05
masked_score = -1e30
rope_base = 10000.0
beta_one = 0.5
beta_two = 0.5
adam_eps = 1e-08
decay_rate = 0.1


def rope_tables(position, head_dim):
    freqs = rope_base ** (-jnp.arange(0, head_dim, 2, dtype=jnp.float32) / head_dim)
    angles = position.astype(jnp.float32)[:, None] * freqs[None, :]
    cosine, sine = jnp.cos(angles), jnp.sin(angles)
    return (jnp.concatenate([cosine, cosine], -1), jnp.concatenate([-sine, sine], -1))


def turn(values, cosine, sine):
    return values * cosine + pltpu.roll(values, HD // 2, 1) * sine


def dot_nt(left, right):
    return lax.dot_general(
        left, right, (((1,), (1,)), ((), ())), preferred_element_type=jnp.float32
    )


def dot_nn(left, right):
    return lax.dot_general(
        left, right, (((1,), (0,)), ((), ())), preferred_element_type=jnp.float32
    )


def dot_tn(left, right):
    return lax.dot_general(
        left, right, (((0,), (0,)), ((), ())), preferred_element_type=jnp.float32
    )


def soft_rows(objective_ref, prefix_ref, place_ref, query, key):
    seq_len = query.shape[0]
    seq, flip = pl.program_id(0) ^ place_ref[0], place_ref[1]
    row_at = lax.broadcasted_iota(jnp.int32, (seq_len, seq_len), 0) ^ flip
    col_at = lax.broadcasted_iota(jnp.int32, (seq_len, seq_len), 1) ^ flip
    bound = jnp.where(objective_ref[seq] > 0, seq_len, prefix_ref[seq])
    visible = (col_at < bound) | (col_at <= row_at)
    scores = jnp.where(visible, dot_nt(query, key) * HD ** (-0.5), masked_score)
    exp_scores = jnp.exp(scores - jnp.max(scores, -1, keepdims=True))
    return exp_scores / jnp.sum(exp_scores, -1, keepdims=True)


def attend_kernel(
    objective_ref,
    prefix_ref,
    place_ref,
    proj_ref,
    cos_ref,
    sin_ref,
    query_ref,
    key_ref,
    value_ref,
    out_ref,
):
    local_dim = out_ref.shape[1]
    cosine, sine = cos_ref[...], sin_ref[...]
    for start in range(0, local_dim, HD):
        cols = slice(start, start + HD)
        query = turn(proj_ref[:, start : start + HD], cosine, sine).astype(jnp.bfloat16)
        key_at = local_dim + start
        key = turn(proj_ref[:, key_at : key_at + HD], cosine, sine).astype(jnp.bfloat16)
        value_at = 2 * local_dim + start
        value = proj_ref[:, value_at : value_at + HD].astype(jnp.bfloat16)
        soft = soft_rows(objective_ref, prefix_ref, place_ref, query, key)
        query_ref[:, cols] = query
        key_ref[:, cols] = key
        value_ref[:, cols] = value
        out_ref[:, cols] = dot_nn(soft.astype(jnp.bfloat16), value).astype(jnp.bfloat16)


def attend_back_kernel(
    objective_ref,
    prefix_ref,
    place_ref,
    query_ref,
    key_ref,
    value_ref,
    grad_ref,
    cos_ref,
    sin_ref,
    out_ref,
):
    local_dim = grad_ref.shape[1]
    cosine, sine = cos_ref[...], sin_ref[...]
    scale = HD ** (-0.5)
    for start in range(0, local_dim, HD):
        cols = slice(start, start + HD)
        query, key, value = query_ref[:, cols], key_ref[:, cols], value_ref[:, cols]
        grad = grad_ref[:, cols]
        soft = soft_rows(objective_ref, prefix_ref, place_ref, query, key)
        grad_soft = dot_nt(grad, value)
        row_dot = jnp.sum(soft * grad_soft, -1, keepdims=True)
        grad_scores = (soft * (grad_soft - row_dot)).astype(jnp.bfloat16)
        value_grad = dot_tn(soft.astype(jnp.bfloat16), grad)
        query_grad = turn(dot_nn(grad_scores, key) * scale, cosine, -sine)
        key_grad = turn(dot_tn(grad_scores, query) * scale, cosine, -sine)
        for index, rows in enumerate((query_grad, key_grad, value_grad)):
            at = index * local_dim + start
            out_ref[:, at : at + HD] = rows.astype(jnp.bfloat16)


def seq_specs(seq_len, widths):
    scalars = pl.BlockSpec(memory_space=pltpu.SMEM)
    table = pl.BlockSpec((seq_len, HD), lambda seq: (0, 0))
    rows = [pl.BlockSpec((seq_len, width), lambda seq: (seq, 0)) for width in widths]
    return [scalars] * 3 + rows + [table] * 2


def attend_forward(seq_info, proj, cosine, sine):
    seq_len, (rows, width) = cosine.shape[0], proj.shape
    local_dim = width // 3
    low = jax.ShapeDtypeStruct((rows, local_dim), jnp.bfloat16)
    block = pl.BlockSpec((seq_len, local_dim), lambda seq: (seq, 0))
    return pl.pallas_call(
        attend_kernel,
        grid=(rows // seq_len,),
        out_shape=(low,) * 4,
        in_specs=seq_specs(seq_len, (width,)),
        out_specs=(block,) * 4,
        name="attend_forward",
    )(*seq_info, proj, cosine, sine)


def attend_backward(seq_info, query, key, value, grad, cosine, sine):
    seq_len, (rows, local_dim) = cosine.shape[0], query.shape
    return pl.pallas_call(
        attend_back_kernel,
        grid=(rows // seq_len,),
        out_shape=jax.ShapeDtypeStruct((rows, 3 * local_dim), jnp.bfloat16),
        in_specs=seq_specs(seq_len, (local_dim,) * 4),
        out_specs=pl.BlockSpec((seq_len, 3 * local_dim), lambda seq: (seq, 0)),
        name="attend_backward",
    )(*seq_info, query, key, value, grad, cosine, sine)


def norm_forward(hidden, norm_gain, norm_bias):
    row_mean = jnp.mean(hidden, -1, keepdims=True)
    centred = hidden - row_mean
    variance = jnp.mean(centred * centred, -1, keepdims=True)
    inv_std = lax.rsqrt(variance + norm_eps)
    normed = centred * inv_std
    return (normed * norm_gain + norm_bias, normed, inv_std)


def norm_backward(grad_rows, normed, inv_std, norm_gain):
    grad_normed = grad_rows * norm_gain
    mean_grad = jnp.mean(grad_normed, -1, keepdims=True)
    mean_proj = jnp.mean(grad_normed * normed, -1, keepdims=True)
    grad_in = inv_std * (grad_normed - mean_grad - normed * mean_proj)
    return (grad_in, jnp.sum(grad_rows * normed, 0), jnp.sum(grad_rows, 0))


def adamw(weight, gradient, first_moment, second, step_rate):
    first_new = beta_one * first_moment + (1.0 - beta_one) * gradient
    second_new = beta_two * second + (1.0 - beta_two) * gradient * gradient
    first_hat = first_new / (1.0 - beta_one**STEP)
    second_hat = second_new / (1.0 - beta_two**STEP)
    weight_new = weight - step_rate * (
        first_hat / (jnp.sqrt(second_hat) + adam_eps) + decay_rate * weight
    )
    return (weight_new, first_new, second_new)


def swap(values, axis, bit):
    size = lax.axis_size(axis)
    return lax.ppermute(values, axis, [(at, at ^ bit) for at in range(size)])


def sum_everywhere(values):
    for axis in ("mp", "dp"):
        bit = 1
        while bit < lax.axis_size(axis):
            values = values + swap(values, axis, bit)
            bit *= 2
    return values


def gather_near(rows):
    half = rows.shape[0] // 2
    near_x, near_y = swap(rows, "mp", 2), swap(rows, "mp", 4)
    far_low, far_high = swap(near_x[:half], "mp", 4), swap(near_y[half:], "mp", 2)
    mates = [swap(part, "mp", 1) for part in (rows, near_x, near_y, far_low, far_high)]
    return jnp.concatenate(
        [rows, mates[0], near_x, mates[1], near_y, mates[2], far_low, far_high, mates[3], mates[4]],
        0,
    )


def scatter_near(whole):
    own_rows = whole.shape[0] // 8
    half = own_rows // 2
    blocks = [whole[at * own_rows : (at + 1) * own_rows] for at in range(8)]
    sums = [
        blocks[at].astype(jnp.float32) + swap(blocks[at + 1], "mp", 1).astype(jnp.float32)
        for at in range(0, 8, 2)
    ]
    far = sums[3].astype(jnp.bfloat16)
    far_low, far_high = swap(far[:half], "mp", 4), swap(far[half:], "mp", 2)
    x_low = (sums[1][:half] + far_low.astype(jnp.float32)).astype(jnp.bfloat16)
    y_high = (sums[2][half:] + far_high.astype(jnp.float32)).astype(jnp.bfloat16)
    x_high, y_low = sums[1][half:].astype(jnp.bfloat16), sums[2][:half].astype(jnp.bfloat16)
    x_low, x_high = swap(x_low, "mp", 2), swap(x_high, "mp", 2)
    y_low, y_high = swap(y_low, "mp", 4), swap(y_high, "mp", 4)
    across_x = jnp.concatenate([x_low, x_high], 0).astype(jnp.float32)
    across_y = jnp.concatenate([y_low, y_high], 0).astype(jnp.float32)
    return sums[0] + across_x + across_y


def gather_all(rows):
    return lax.all_gather(rows, "mp", axis=0, tiled=True)


def scatter_all(whole):
    return lax.psum_scatter(whole, "mp", scatter_dimension=0, tiled=True).astype(jnp.float32)


def adamw_as(order, weight, gradient, first_moment, second, step_rate, scale):
    turned = [jnp.transpose(rows, order) for rows in (weight, first_moment, second)]
    rank = len(order)
    gradient = with_layout_constraint(gradient, Layout(major_to_minor=tuple(range(rank))))
    gradient = gradient.astype(jnp.float32) * scale
    news = adamw(turned[0], gradient, turned[1], turned[2], step_rate)
    back = tuple(order.index(dim) for dim in range(rank))
    stored = Layout(major_to_minor=order)
    return tuple(with_layout_constraint(jnp.transpose(rows, back), stored) for rows in news)


def local(
    block_input,
    out_cotangent,
    objective,
    prefix_len,
    target_mask,
    qkv_weight,
    out_weight,
    gateup_weight,
    down_weight,
    norm_params,
    qkv_first,
    out_first,
    gateup_first,
    down_first,
    norm_first,
    qkv_second,
    out_second,
    gateup_second,
    down_second,
    norm_second,
):
    mp_index = lax.axis_index("mp")
    own_rows = block_input.shape[0]
    seq_count = objective.shape[0]
    seq_len = own_rows * lax.axis_size("mp") // seq_count
    shard_rows, _, local_dim = qkv_weight.shape
    local_units = gateup_weight.shape[2]
    near = lax.axis_size("mp") == 8 and seq_count == 4 and own_rows % 32 == 0
    if near:
        gather_rows, scatter_rows = gather_near, scatter_near
        place = jnp.stack([mp_index // 2, (mp_index % 2) * own_rows]).astype(jnp.int32)
    else:
        gather_rows, scatter_rows = gather_all, scatter_all
        place = jnp.zeros((2,), jnp.int32)
    seq_info = (objective, prefix_len, place)
    cosine, sine = rope_tables(jnp.arange(seq_len, dtype=jnp.int32) ^ place[1], HD)

    qkv_low = qkv_weight.astype(jnp.bfloat16).reshape(shard_rows, 3 * local_dim)
    qkv_full = lax.all_gather(qkv_low, "dp", axis=0, tiled=True)
    out_full = lax.all_gather(out_weight.astype(jnp.bfloat16), "dp", axis=1, tiled=True)
    gateup_low = jnp.transpose(gateup_weight, (1, 2, 0)).astype(jnp.bfloat16)
    gateup_full = lax.all_gather(gateup_low, "dp", axis=2, tiled=True)
    down_full = lax.all_gather(down_weight.astype(jnp.bfloat16), "dp", axis=1, tiled=True)

    mask_f32 = target_mask.astype(jnp.float32)
    target_count = sum_everywhere(jnp.full((8, 128), jnp.sum(mask_f32)))[0, 0]

    inputs = gather_rows(block_input)
    proj = jnp.dot(inputs, qkv_full, preferred_element_type=jnp.float32)
    *kept, attended = attend_forward(seq_info, proj, cosine, sine)
    attn_own = scatter_rows(jnp.dot(attended, out_full, preferred_element_type=jnp.bfloat16))
    hidden_one = deep_alpha * block_input.astype(jnp.float32) + attn_own
    middle, normed_one, inv_one = norm_forward(hidden_one, norm_params[0], norm_params[1])
    middle_low = gather_rows(middle.astype(jnp.bfloat16))

    live_units = (mp_index * local_units + jnp.arange(local_units) < FF).astype(jnp.float32)
    gate_up = jnp.einsum(
        "td,cfd->ctf", middle_low, gateup_full, preferred_element_type=jnp.float32
    )
    hidden_low = (jax.nn.gelu(gate_up[0]) * gate_up[1] * live_units).astype(jnp.bfloat16)
    ffn_own = scatter_rows(jnp.dot(hidden_low, down_full, preferred_element_type=jnp.bfloat16))
    hidden_two = deep_alpha * middle + ffn_own
    output_rows, normed_two, inv_two = norm_forward(hidden_two, norm_params[2], norm_params[3])
    grad_rows = out_cotangent.astype(jnp.float32) * mask_f32[:, None]
    grad_two, gain_two, bias_two = norm_backward(grad_rows, normed_two, inv_two, norm_params[2])

    ffn_back = gather_rows(grad_two.astype(jnp.bfloat16))
    down_grad = jnp.einsum("tf,td->fd", hidden_low, ffn_back, preferred_element_type=jnp.bfloat16)
    ffn_back, down_grad = lax.optimization_barrier((ffn_back, down_grad))
    down_grad = lax.psum_scatter(down_grad, "dp", scatter_dimension=1, tiled=True)
    gate_act, gelu_pull = jax.vjp(jax.nn.gelu, gate_up[0])
    grad_hidden = (
        jnp.einsum("td,fd->tf", ffn_back, down_full, preferred_element_type=jnp.float32)
        * live_units
    )
    grad_gate = gelu_pull(grad_hidden * gate_up[1])[0]
    grad_up = grad_hidden * gate_act
    grad_gateup = jnp.stack([grad_gate, grad_up], 0).astype(jnp.bfloat16)
    middle_part = jnp.einsum(
        "ctf,cfd->td", grad_gateup, gateup_full, preferred_element_type=jnp.bfloat16
    )
    middle_low, down_grad = lax.optimization_barrier((middle_low, down_grad))
    gateup_grad = jnp.einsum(
        "ctf,td->cfd", grad_gateup, middle_low, preferred_element_type=jnp.bfloat16
    )
    grad_middle = scatter_rows(middle_part) + deep_alpha * grad_two
    grad_one, gain_one, bias_one = norm_backward(grad_middle, normed_one, inv_one, norm_params[0])

    grad_one_low, gateup_grad = lax.optimization_barrier(
        (grad_one.astype(jnp.bfloat16), gateup_grad)
    )
    gateup_grad = with_layout_constraint(
        lax.psum_scatter(gateup_grad, "dp", scatter_dimension=2, tiled=True),
        Layout(major_to_minor=(0, 1, 2)),
    )
    attn_back = gather_rows(grad_one_low)
    grad_attended = jnp.einsum(
        "td,ed->te", attn_back, out_full, preferred_element_type=jnp.bfloat16
    )
    grad_proj = attend_backward(seq_info, *kept, grad_attended, cosine, sine)
    attended, grad_proj = lax.optimization_barrier((attended, grad_proj))
    attend_grad = jnp.concatenate(
        [
            jnp.einsum("te,td->ed", left, right, preferred_element_type=jnp.bfloat16)
            for left, right in ((attended, attn_back), (grad_proj, inputs))
        ],
        0,
    )
    grad_proj, attend_grad = lax.optimization_barrier((grad_proj, attend_grad))
    attend_grad, gateup_grad = lax.optimization_barrier((attend_grad, gateup_grad))
    attend_grad = lax.psum_scatter(attend_grad, "dp", scatter_dimension=1, tiled=True)
    input_raw = (
        scatter_rows(
            jnp.einsum("te,de->td", grad_proj, qkv_full, preferred_element_type=jnp.bfloat16)
        )
        + deep_alpha * grad_one
    )
    norm_grad = jnp.stack([gain_one, bias_one, gain_two, bias_two], 0)
    norm_grad, input_raw = lax.optimization_barrier((norm_grad, input_raw))
    norm_grad = sum_everywhere(norm_grad)
    rate_list = (D ** (-0.5), 0.5, D ** (-0.5), (FF_PAD // 64) ** (-0.5), 0.4)
    scale = 1.0 / target_count
    gateup_res = adamw_as(
        (2, 1, 0),
        gateup_weight,
        gateup_grad.transpose(1, 0, 2),
        gateup_first,
        gateup_second,
        rate_list[2],
        scale,
    )
    down_res = adamw_as(
        (0, 1), down_weight, down_grad, down_first, down_second, rate_list[3], scale
    )
    attend_grad, gateup_res, down_res = lax.optimization_barrier(
        (attend_grad, gateup_res, down_res)
    )
    out_grad = attend_grad[:local_dim]
    qkv_grad = attend_grad[local_dim:].reshape(3, local_dim, shard_rows)
    qkv_res = adamw_as(
        (1, 0, 2), qkv_weight, qkv_grad.transpose(0, 2, 1), qkv_first, qkv_second, rate_list[0], scale
    )
    out_res = adamw_as((0, 1), out_weight, out_grad, out_first, out_second, rate_list[1], scale)
    norm_res = adamw(norm_params, norm_grad * scale, norm_first, norm_second, rate_list[4])
    return (
        output_rows.astype(jnp.bfloat16),
        input_raw * scale,
        qkv_res[0],
        qkv_res[1],
        qkv_res[2],
        out_res[0],
        out_res[1],
        out_res[2],
        gateup_res[0],
        gateup_res[1],
        gateup_res[2],
        down_res[0],
        down_res[1],
        down_res[2],
        norm_res[0],
        norm_res[1],
        norm_res[2],
    )


def solution(mesh):
    return jax.shard_map(
        local,
        mesh=mesh,
        in_specs=(
            P(("dp", "mp"), None),
            P(("dp", "mp"), None),
            P("dp"),
            P("dp"),
            P(("dp", "mp")),
            P("dp", None, "mp"),
            P("mp", "dp"),
            P("dp", None, "mp"),
            P("mp", "dp"),
            P(),
            P("dp", None, "mp"),
            P("mp", "dp"),
            P("dp", None, "mp"),
            P("mp", "dp"),
            P(),
            P("dp", None, "mp"),
            P("mp", "dp"),
            P("dp", None, "mp"),
            P("mp", "dp"),
            P(),
        ),
        out_specs=(
            P(("dp", "mp"), None),
            P(("dp", "mp"), None),
            P("dp", None, "mp"),
            P("dp", None, "mp"),
            P("dp", None, "mp"),
            P("mp", "dp"),
            P("mp", "dp"),
            P("mp", "dp"),
            P("dp", None, "mp"),
            P("dp", None, "mp"),
            P("dp", None, "mp"),
            P("mp", "dp"),
            P("mp", "dp"),
            P("mp", "dp"),
            P(),
            P(),
            P(),
        ),
        check_vma=False,
    )
```

```python
import jax
import jax.numpy as jnp
from jax import lax
from jax.experimental import pallas as pl
from jax.experimental.layout import Layout, with_layout_constraint
from jax.experimental.pallas import tpu as pltpu
from jax.sharding import PartitionSpec as P

D = 2048
HD = 128
FF = 5461
FF_PAD = 5472
STEP = 5


deep_alpha = 48.0**0.5
norm_eps = 1e-05
masked_score = -1e30
rope_base = 10000.0
beta_one = 0.5
beta_two = 0.5
adam_eps = 1e-08
decay_rate = 0.1


def rope_tables(position, head_dim):
    freqs = rope_base ** (-jnp.arange(0, head_dim, 2, dtype=jnp.float32) / head_dim)
    angles = position.astype(jnp.float32)[:, None] * freqs[None, :]
    cosine, sine = jnp.cos(angles), jnp.sin(angles)
    return (jnp.concatenate([cosine, cosine], -1), jnp.concatenate([-sine, sine], -1))


def turn(values, cosine, sine):
    return values * cosine + pltpu.roll(values, HD // 2, 1) * sine


def dot_nt(left, right):
    return lax.dot_general(
        left, right, (((1,), (1,)), ((), ())), preferred_element_type=jnp.float32
    )


def dot_nn(left, right):
    return lax.dot_general(
        left, right, (((1,), (0,)), ((), ())), preferred_element_type=jnp.float32
    )


def dot_tn(left, right):
    return lax.dot_general(
        left, right, (((0,), (0,)), ((), ())), preferred_element_type=jnp.float32
    )


def soft_rows(objective_ref, prefix_ref, place_ref, query, key):
    seq_len = query.shape[0]
    seq, flip = pl.program_id(0) ^ place_ref[0], place_ref[1]
    row_at = lax.broadcasted_iota(jnp.int32, (seq_len, seq_len), 0) ^ flip
    col_at = lax.broadcasted_iota(jnp.int32, (seq_len, seq_len), 1) ^ flip
    bound = jnp.where(objective_ref[seq] > 0, seq_len, prefix_ref[seq])
    visible = (col_at < bound) | (col_at <= row_at)
    scores = jnp.where(visible, dot_nt(query, key) * HD ** (-0.5), masked_score)
    exp_scores = jnp.exp(scores - jnp.max(scores, -1, keepdims=True))
    return exp_scores / jnp.sum(exp_scores, -1, keepdims=True)


def attend_kernel(
    objective_ref,
    prefix_ref,
    place_ref,
    proj_ref,
    cos_ref,
    sin_ref,
    query_ref,
    key_ref,
    value_ref,
    out_ref,
):
    local_dim = out_ref.shape[1]
    cosine, sine = cos_ref[...], sin_ref[...]
    for start in range(0, local_dim, HD):
        cols = slice(start, start + HD)
        query = turn(proj_ref[:, start : start + HD], cosine, sine).astype(jnp.bfloat16)
        key_at = local_dim + start
        key = turn(proj_ref[:, key_at : key_at + HD], cosine, sine).astype(jnp.bfloat16)
        value_at = 2 * local_dim + start
        value = proj_ref[:, value_at : value_at + HD].astype(jnp.bfloat16)
        soft = soft_rows(objective_ref, prefix_ref, place_ref, query, key)
        query_ref[:, cols] = query
        key_ref[:, cols] = key
        value_ref[:, cols] = value
        out_ref[:, cols] = dot_nn(soft.astype(jnp.bfloat16), value).astype(jnp.bfloat16)


def attend_back_kernel(
    objective_ref,
    prefix_ref,
    place_ref,
    query_ref,
    key_ref,
    value_ref,
    grad_ref,
    cos_ref,
    sin_ref,
    out_ref,
):
    local_dim = grad_ref.shape[1]
    cosine, sine = cos_ref[...], sin_ref[...]
    scale = HD ** (-0.5)
    for start in range(0, local_dim, HD):
        cols = slice(start, start + HD)
        query, key, value = query_ref[:, cols], key_ref[:, cols], value_ref[:, cols]
        grad = grad_ref[:, cols]
        soft = soft_rows(objective_ref, prefix_ref, place_ref, query, key)
        grad_soft = dot_nt(grad, value)
        row_dot = jnp.sum(soft * grad_soft, -1, keepdims=True)
        grad_scores = (soft * (grad_soft - row_dot)).astype(jnp.bfloat16)
        value_grad = dot_tn(soft.astype(jnp.bfloat16), grad)
        query_grad = turn(dot_nn(grad_scores, key) * scale, cosine, -sine)
        key_grad = turn(dot_tn(grad_scores, query) * scale, cosine, -sine)
        for index, rows in enumerate((query_grad, key_grad, value_grad)):
            at = index * local_dim + start
            out_ref[:, at : at + HD] = rows.astype(jnp.bfloat16)


def seq_specs(seq_len, widths):
    scalars = pl.BlockSpec(memory_space=pltpu.SMEM)
    table = pl.BlockSpec((seq_len, HD), lambda seq: (0, 0))
    rows = [pl.BlockSpec((seq_len, width), lambda seq: (seq, 0)) for width in widths]
    return [scalars] * 3 + rows + [table] * 2


def attend_forward(seq_info, proj, cosine, sine):
    seq_len, (rows, width) = cosine.shape[0], proj.shape
    local_dim = width // 3
    low = jax.ShapeDtypeStruct((rows, local_dim), jnp.bfloat16)
    block = pl.BlockSpec((seq_len, local_dim), lambda seq: (seq, 0))
    return pl.pallas_call(
        attend_kernel,
        grid=(rows // seq_len,),
        out_shape=(low,) * 4,
        in_specs=seq_specs(seq_len, (width,)),
        out_specs=(block,) * 4,
        name="attend_forward",
    )(*seq_info, proj, cosine, sine)


def attend_backward(seq_info, query, key, value, grad, cosine, sine):
    seq_len, (rows, local_dim) = cosine.shape[0], query.shape
    return pl.pallas_call(
        attend_back_kernel,
        grid=(rows // seq_len,),
        out_shape=jax.ShapeDtypeStruct((rows, 3 * local_dim), jnp.bfloat16),
        in_specs=seq_specs(seq_len, (local_dim,) * 4),
        out_specs=pl.BlockSpec((seq_len, 3 * local_dim), lambda seq: (seq, 0)),
        name="attend_backward",
    )(*seq_info, query, key, value, grad, cosine, sine)


def norm_forward(hidden, norm_gain, norm_bias):
    row_mean = jnp.mean(hidden, -1, keepdims=True)
    centred = hidden - row_mean
    variance = jnp.mean(centred * centred, -1, keepdims=True)
    inv_std = lax.rsqrt(variance + norm_eps)
    normed = centred * inv_std
    return (normed * norm_gain + norm_bias, normed, inv_std)


def norm_backward(grad_rows, normed, inv_std, norm_gain):
    grad_normed = grad_rows * norm_gain
    mean_grad = jnp.mean(grad_normed, -1, keepdims=True)
    mean_proj = jnp.mean(grad_normed * normed, -1, keepdims=True)
    grad_in = inv_std * (grad_normed - mean_grad - normed * mean_proj)
    return (grad_in, jnp.sum(grad_rows * normed, 0), jnp.sum(grad_rows, 0))


def adamw(weight, gradient, first_moment, second, step_rate):
    first_new = beta_one * first_moment + (1.0 - beta_one) * gradient
    second_new = beta_two * second + (1.0 - beta_two) * gradient * gradient
    first_hat = first_new / (1.0 - beta_one**STEP)
    second_hat = second_new / (1.0 - beta_two**STEP)
    weight_new = weight - step_rate * (
        first_hat / (jnp.sqrt(second_hat) + adam_eps) + decay_rate * weight
    )
    return (weight_new, first_new, second_new)


def swap(values, axis, bit):
    size = lax.axis_size(axis)
    return lax.ppermute(values, axis, [(at, at ^ bit) for at in range(size)])


def sum_everywhere(values):
    for axis in ("mp", "dp"):
        bit = 1
        while bit < lax.axis_size(axis):
            values = values + swap(values, axis, bit)
            bit *= 2
    return values


def gather_near(rows):
    half = rows.shape[0] // 2
    near_x, near_y = swap(rows, "mp", 2), swap(rows, "mp", 4)
    far_low, far_high = swap(near_x[:half], "mp", 4), swap(near_y[half:], "mp", 2)
    mates = [swap(part, "mp", 1) for part in (rows, near_x, near_y, far_low, far_high)]
    return jnp.concatenate(
        [rows, mates[0], near_x, mates[1], near_y, mates[2], far_low, far_high, mates[3], mates[4]],
        0,
    )


def far_first(rows, product, quarters):
    size = rows.shape[0] // 4
    pieces = []
    for first, last in quarters:
        if pieces:
            rows, pieces[0] = lax.optimization_barrier((rows, pieces[0]))
        pieces.insert(0, product(rows[first * size : last * size]))
    return pieces


def scatter_near(pieces):
    blocks = []
    own_rows = sum(piece.shape[0] for piece in pieces) // 8
    half = own_rows // 2
    for piece in pieces:
        blocks += [
            piece[at : at + own_rows] for at in range(0, piece.shape[0], own_rows)
        ]
    sums = [
        blocks[at].astype(jnp.float32) + swap(blocks[at + 1], "mp", 1).astype(jnp.float32)
        for at in range(0, 8, 2)
    ]
    far = sums[3].astype(jnp.bfloat16)
    far_low, far_high = swap(far[:half], "mp", 4), swap(far[half:], "mp", 2)
    x_low = (sums[1][:half] + far_low.astype(jnp.float32)).astype(jnp.bfloat16)
    y_high = (sums[2][half:] + far_high.astype(jnp.float32)).astype(jnp.bfloat16)
    x_high, y_low = sums[1][half:].astype(jnp.bfloat16), sums[2][:half].astype(jnp.bfloat16)
    x_low, x_high = swap(x_low, "mp", 2), swap(x_high, "mp", 2)
    y_low, y_high = swap(y_low, "mp", 4), swap(y_high, "mp", 4)
    across_x = jnp.concatenate([x_low, x_high], 0).astype(jnp.float32)
    across_y = jnp.concatenate([y_low, y_high], 0).astype(jnp.float32)
    return sums[0] + across_x + across_y


def gather_all(rows):
    return lax.all_gather(rows, "mp", axis=0, tiled=True)


def scatter_all(pieces):
    whole = jnp.concatenate(pieces, 0)
    return lax.psum_scatter(whole, "mp", scatter_dimension=0, tiled=True).astype(jnp.float32)


def adamw_as(order, weight, gradient, first_moment, second, step_rate, scale):
    turned = [jnp.transpose(rows, order) for rows in (weight, first_moment, second)]
    rank = len(order)
    gradient = with_layout_constraint(gradient, Layout(major_to_minor=tuple(range(rank))))
    gradient = gradient.astype(jnp.float32) * scale
    news = adamw(turned[0], gradient, turned[1], turned[2], step_rate)
    back = tuple(order.index(dim) for dim in range(rank))
    stored = Layout(major_to_minor=order)
    return tuple(with_layout_constraint(jnp.transpose(rows, back), stored) for rows in news)


def local(
    block_input,
    out_cotangent,
    objective,
    prefix_len,
    target_mask,
    qkv_weight,
    out_weight,
    gateup_weight,
    down_weight,
    norm_params,
    qkv_first,
    out_first,
    gateup_first,
    down_first,
    norm_first,
    qkv_second,
    out_second,
    gateup_second,
    down_second,
    norm_second,
):
    mp_index = lax.axis_index("mp")
    own_rows = block_input.shape[0]
    seq_count = objective.shape[0]
    seq_len = own_rows * lax.axis_size("mp") // seq_count
    shard_rows, _, local_dim = qkv_weight.shape
    local_units = gateup_weight.shape[2]
    near = lax.axis_size("mp") == 8 and seq_count == 4 and own_rows % 32 == 0
    if near:
        gather_rows, scatter_rows = gather_near, scatter_near
        place = jnp.stack([mp_index // 2, (mp_index % 2) * own_rows]).astype(jnp.int32)
    else:
        gather_rows, scatter_rows = gather_all, scatter_all
        place = jnp.zeros((2,), jnp.int32)
    two_pieces, four_pieces = ((3, 4), (0, 3)), ((3, 4), (2, 3), (1, 2), (0, 1))
    seq_info = (objective, prefix_len, place)
    cosine, sine = rope_tables(jnp.arange(seq_len, dtype=jnp.int32) ^ place[1], HD)

    qkv_low = qkv_weight.astype(jnp.bfloat16).reshape(shard_rows, 3 * local_dim)
    qkv_full = lax.all_gather(qkv_low, "dp", axis=0, tiled=True)
    out_full = lax.all_gather(out_weight.astype(jnp.bfloat16), "dp", axis=1, tiled=True)
    gateup_low = with_layout_constraint(
        jnp.transpose(gateup_weight, (1, 2, 0)).astype(jnp.bfloat16),
        Layout(major_to_minor=(0, 1, 2)),
    )
    gateup_full = lax.all_gather(gateup_low, "dp", axis=2, tiled=True)
    down_full = lax.all_gather(down_weight.astype(jnp.bfloat16), "dp", axis=1, tiled=True)

    mask_f32 = target_mask.astype(jnp.float32)
    target_count = sum_everywhere(jnp.full((8, 128), jnp.sum(mask_f32)))[0, 0]

    cosine, target_count = lax.optimization_barrier((cosine, target_count))

    inputs = gather_rows(block_input)
    proj = jnp.dot(inputs, qkv_full, preferred_element_type=jnp.float32)
    *kept, attended = attend_forward(seq_info, proj, cosine, sine)
    attn_own = scatter_rows(
        far_first(
            attended,
            lambda rows: jnp.dot(rows, out_full, preferred_element_type=jnp.bfloat16),
            two_pieces,
        )
    )
    hidden_one = deep_alpha * block_input.astype(jnp.float32) + attn_own
    middle, normed_one, inv_one = norm_forward(hidden_one, norm_params[0], norm_params[1])
    middle_low = gather_rows(middle.astype(jnp.bfloat16))

    live_units = (mp_index * local_units + jnp.arange(local_units) < FF).astype(jnp.float32)
    gate_up = jnp.einsum(
        "td,cfd->ctf", middle_low, gateup_full, preferred_element_type=jnp.float32
    )
    hidden_low = (jax.nn.gelu(gate_up[0]) * gate_up[1] * live_units).astype(jnp.bfloat16)
    ffn_own = scatter_rows(
        far_first(
            hidden_low,
            lambda rows: jnp.dot(rows, down_full, preferred_element_type=jnp.bfloat16),
            two_pieces,
        )
    )
    hidden_two = deep_alpha * middle + ffn_own
    output_rows, normed_two, inv_two = norm_forward(hidden_two, norm_params[2], norm_params[3])
    grad_rows = out_cotangent.astype(jnp.float32) * mask_f32[:, None]
    grad_two, gain_two, bias_two = norm_backward(grad_rows, normed_two, inv_two, norm_params[2])

    ffn_back = gather_rows(grad_two.astype(jnp.bfloat16))
    down_grad = jnp.einsum("tf,td->fd", hidden_low, ffn_back, preferred_element_type=jnp.bfloat16)
    ffn_back, down_grad = lax.optimization_barrier((ffn_back, down_grad))
    down_grad = lax.psum_scatter(down_grad, "dp", scatter_dimension=1, tiled=True)
    quarter = ffn_back.shape[0] // 4
    middle_parts, grad_gateups = [], []
    for first, last in four_pieces:
        at = slice(first * quarter, last * quarter)
        if middle_parts:
            ffn_back, middle_parts[0] = lax.optimization_barrier((ffn_back, middle_parts[0]))
        gate_act, gelu_pull = jax.vjp(jax.nn.gelu, gate_up[0, at])
        grad_hidden = (
            jnp.einsum("td,fd->tf", ffn_back[at], down_full, preferred_element_type=jnp.float32)
            * live_units
        )
        grad_gate = gelu_pull(grad_hidden * gate_up[1, at])[0]
        grad_gateup = jnp.stack([grad_gate, grad_hidden * gate_act], 0).astype(jnp.bfloat16)
        grad_gateups.insert(0, grad_gateup)
        middle_parts.insert(
            0,
            jnp.einsum(
                "ctf,cfd->td", grad_gateup, gateup_full, preferred_element_type=jnp.bfloat16
            ),
        )
    gateup_grad = jnp.einsum(
        "ctf,td->cfd",
        jnp.concatenate(grad_gateups, 1),
        middle_low,
        preferred_element_type=jnp.bfloat16,
    )
    gateup_grad, down_grad = lax.optimization_barrier((gateup_grad, down_grad))
    grad_middle = scatter_rows(middle_parts) + deep_alpha * grad_two
    grad_one, gain_one, bias_one = norm_backward(grad_middle, normed_one, inv_one, norm_params[0])

    grad_one_low, gateup_grad = lax.optimization_barrier(
        (grad_one.astype(jnp.bfloat16), gateup_grad)
    )
    gateup_grad = with_layout_constraint(
        lax.psum_scatter(gateup_grad, "dp", scatter_dimension=2, tiled=True),
        Layout(major_to_minor=(0, 1, 2)),
    )
    attn_back = gather_rows(grad_one_low)
    grad_attended = jnp.einsum(
        "td,ed->te", attn_back, out_full, preferred_element_type=jnp.bfloat16
    )
    grad_proj = attend_backward(seq_info, *kept, grad_attended, cosine, sine)
    attended, grad_proj = lax.optimization_barrier((attended, grad_proj))
    attend_grad = jnp.concatenate(
        [
            jnp.einsum("te,td->ed", left, right, preferred_element_type=jnp.bfloat16)
            for left, right in ((attended, attn_back), (grad_proj, inputs))
        ],
        0,
    )
    grad_proj, attend_grad = lax.optimization_barrier((grad_proj, attend_grad))
    attend_grad, gateup_grad = lax.optimization_barrier((attend_grad, gateup_grad))
    attend_grad = lax.psum_scatter(attend_grad, "dp", scatter_dimension=1, tiled=True)
    input_raw = (
        scatter_rows(
            far_first(
                grad_proj,
                lambda rows: jnp.einsum(
                    "te,de->td", rows, qkv_full, preferred_element_type=jnp.bfloat16
                ),
                two_pieces,
            )
        )
        + deep_alpha * grad_one
    )
    norm_grad = jnp.stack([gain_one, bias_one, gain_two, bias_two], 0)
    norm_grad, input_raw = lax.optimization_barrier((norm_grad, input_raw))
    norm_grad = sum_everywhere(norm_grad)
    rate_list = (D ** (-0.5), 0.5, D ** (-0.5), (FF_PAD // 64) ** (-0.5), 0.4)
    scale = 1.0 / target_count
    gateup_res = adamw_as(
        (2, 1, 0),
        gateup_weight,
        gateup_grad.transpose(1, 0, 2),
        gateup_first,
        gateup_second,
        rate_list[2],
        scale,
    )
    down_res = adamw_as(
        (0, 1), down_weight, down_grad, down_first, down_second, rate_list[3], scale
    )
    attend_grad, gateup_res, down_res = lax.optimization_barrier(
        (attend_grad, gateup_res, down_res)
    )
    out_grad = attend_grad[:local_dim]
    qkv_grad = attend_grad[local_dim:].reshape(3, local_dim, shard_rows)
    qkv_res = adamw_as(
        (1, 0, 2), qkv_weight, qkv_grad.transpose(0, 2, 1), qkv_first, qkv_second, rate_list[0], scale
    )
    out_res = adamw_as((0, 1), out_weight, out_grad, out_first, out_second, rate_list[1], scale)
    norm_res = adamw(norm_params, norm_grad * scale, norm_first, norm_second, rate_list[4])
    return (
        output_rows.astype(jnp.bfloat16),
        input_raw * scale,
        qkv_res[0],
        qkv_res[1],
        qkv_res[2],
        out_res[0],
        out_res[1],
        out_res[2],
        gateup_res[0],
        gateup_res[1],
        gateup_res[2],
        down_res[0],
        down_res[1],
        down_res[2],
        norm_res[0],
        norm_res[1],
        norm_res[2],
    )


def solution(mesh):
    return jax.shard_map(
        local,
        mesh=mesh,
        in_specs=(
            P(("dp", "mp"), None),
            P(("dp", "mp"), None),
            P("dp"),
            P("dp"),
            P(("dp", "mp")),
            P("dp", None, "mp"),
            P("mp", "dp"),
            P("dp", None, "mp"),
            P("mp", "dp"),
            P(),
            P("dp", None, "mp"),
            P("mp", "dp"),
            P("dp", None, "mp"),
            P("mp", "dp"),
            P(),
            P("dp", None, "mp"),
            P("mp", "dp"),
            P("dp", None, "mp"),
            P("mp", "dp"),
            P(),
        ),
        out_specs=(
            P(("dp", "mp"), None),
            P(("dp", "mp"), None),
            P("dp", None, "mp"),
            P("dp", None, "mp"),
            P("dp", None, "mp"),
            P("mp", "dp"),
            P("mp", "dp"),
            P("mp", "dp"),
            P("dp", None, "mp"),
            P("dp", None, "mp"),
            P("dp", None, "mp"),
            P("mp", "dp"),
            P("mp", "dp"),
            P("mp", "dp"),
            P(),
            P(),
            P(),
        ),
        check_vma=False,
    )
```

```python
import jax
import jax.numpy as jnp
from jax import lax
from jax.experimental import pallas as pl
from jax.experimental.layout import Layout, with_layout_constraint
from jax.experimental.pallas import tpu as pltpu
from jax.sharding import PartitionSpec as P

D = 2048
HD = 128
FF = 5461
FF_PAD = 5472
STEP = 5


deep_alpha = 48.0**0.5
norm_eps = 1e-05
masked_score = -1e30
rope_base = 10000.0
beta_one = 0.5
beta_two = 0.5
adam_eps = 1e-08
decay_rate = 0.1


def rope_tables(position, head_dim):
    freqs = rope_base ** (-jnp.arange(0, head_dim, 2, dtype=jnp.float32) / head_dim)
    angles = position.astype(jnp.float32)[:, None] * freqs[None, :]
    cosine, sine = jnp.cos(angles), jnp.sin(angles)
    return (jnp.concatenate([cosine, cosine], -1), jnp.concatenate([-sine, sine], -1))


def turn(values, cosine, sine):
    return values * cosine + pltpu.roll(values, HD // 2, 1) * sine


def dot_nt(left, right):
    return lax.dot_general(
        left, right, (((1,), (1,)), ((), ())), preferred_element_type=jnp.float32
    )


def dot_nn(left, right):
    return lax.dot_general(
        left, right, (((1,), (0,)), ((), ())), preferred_element_type=jnp.float32
    )


def dot_tn(left, right):
    return lax.dot_general(
        left, right, (((0,), (0,)), ((), ())), preferred_element_type=jnp.float32
    )


def soft_rows(objective_ref, prefix_ref, place_ref, query, key):
    seq_len = query.shape[0]
    seq, flip = pl.program_id(0) ^ place_ref[0], place_ref[1]
    row_at = lax.broadcasted_iota(jnp.int32, (seq_len, seq_len), 0) ^ flip
    col_at = lax.broadcasted_iota(jnp.int32, (seq_len, seq_len), 1) ^ flip
    bound = jnp.where(objective_ref[seq] > 0, seq_len, prefix_ref[seq])
    visible = (col_at < bound) | (col_at <= row_at)
    scores = jnp.where(visible, dot_nt(query, key) * HD ** (-0.5), masked_score)
    exp_scores = jnp.exp(scores - jnp.max(scores, -1, keepdims=True))
    return exp_scores / jnp.sum(exp_scores, -1, keepdims=True)


def attend_kernel(
    objective_ref,
    prefix_ref,
    place_ref,
    proj_ref,
    cos_ref,
    sin_ref,
    query_ref,
    key_ref,
    value_ref,
    out_ref,
):
    local_dim = out_ref.shape[1]
    cosine, sine = cos_ref[...], sin_ref[...]
    for start in range(0, local_dim, HD):
        cols = slice(start, start + HD)
        query = turn(proj_ref[:, start : start + HD], cosine, sine).astype(jnp.bfloat16)
        key_at = local_dim + start
        key = turn(proj_ref[:, key_at : key_at + HD], cosine, sine).astype(jnp.bfloat16)
        value_at = 2 * local_dim + start
        value = proj_ref[:, value_at : value_at + HD].astype(jnp.bfloat16)
        soft = soft_rows(objective_ref, prefix_ref, place_ref, query, key)
        query_ref[:, cols] = query
        key_ref[:, cols] = key
        value_ref[:, cols] = value
        out_ref[:, cols] = dot_nn(soft.astype(jnp.bfloat16), value).astype(jnp.bfloat16)


def attend_back_kernel(
    objective_ref,
    prefix_ref,
    place_ref,
    query_ref,
    key_ref,
    value_ref,
    grad_ref,
    cos_ref,
    sin_ref,
    out_ref,
):
    local_dim = grad_ref.shape[1]
    cosine, sine = cos_ref[...], sin_ref[...]
    scale = HD ** (-0.5)
    for start in range(0, local_dim, HD):
        cols = slice(start, start + HD)
        query, key, value = query_ref[:, cols], key_ref[:, cols], value_ref[:, cols]
        grad = grad_ref[:, cols]
        soft = soft_rows(objective_ref, prefix_ref, place_ref, query, key)
        grad_soft = dot_nt(grad, value)
        row_dot = jnp.sum(soft * grad_soft, -1, keepdims=True)
        grad_scores = (soft * (grad_soft - row_dot)).astype(jnp.bfloat16)
        value_grad = dot_tn(soft.astype(jnp.bfloat16), grad)
        query_grad = turn(dot_nn(grad_scores, key) * scale, cosine, -sine)
        key_grad = turn(dot_tn(grad_scores, query) * scale, cosine, -sine)
        for index, rows in enumerate((query_grad, key_grad, value_grad)):
            at = index * local_dim + start
            out_ref[:, at : at + HD] = rows.astype(jnp.bfloat16)


def seq_specs(seq_len, widths):
    scalars = pl.BlockSpec(memory_space=pltpu.SMEM)
    table = pl.BlockSpec((seq_len, HD), lambda seq: (0, 0))
    rows = [pl.BlockSpec((seq_len, width), lambda seq: (seq, 0)) for width in widths]
    return [scalars] * 3 + rows + [table] * 2


def attend_forward(seq_info, proj, cosine, sine):
    seq_len, (rows, width) = cosine.shape[0], proj.shape
    local_dim = width // 3
    low = jax.ShapeDtypeStruct((rows, local_dim), jnp.bfloat16)
    block = pl.BlockSpec((seq_len, local_dim), lambda seq: (seq, 0))
    return pl.pallas_call(
        attend_kernel,
        grid=(rows // seq_len,),
        out_shape=(low,) * 4,
        in_specs=seq_specs(seq_len, (width,)),
        out_specs=(block,) * 4,
        name="attend_forward",
    )(*seq_info, proj, cosine, sine)


def attend_backward(seq_info, query, key, value, grad, cosine, sine):
    seq_len, (rows, local_dim) = cosine.shape[0], query.shape
    return pl.pallas_call(
        attend_back_kernel,
        grid=(rows // seq_len,),
        out_shape=jax.ShapeDtypeStruct((rows, 3 * local_dim), jnp.bfloat16),
        in_specs=seq_specs(seq_len, (local_dim,) * 4),
        out_specs=pl.BlockSpec((seq_len, 3 * local_dim), lambda seq: (seq, 0)),
        name="attend_backward",
    )(*seq_info, query, key, value, grad, cosine, sine)


def norm_forward(hidden, norm_gain, norm_bias):
    row_mean = jnp.mean(hidden, -1, keepdims=True)
    centred = hidden - row_mean
    variance = jnp.mean(centred * centred, -1, keepdims=True)
    inv_std = lax.rsqrt(variance + norm_eps)
    normed = centred * inv_std
    return (normed * norm_gain + norm_bias, normed, inv_std)


def norm_backward(grad_rows, normed, inv_std, norm_gain):
    grad_normed = grad_rows * norm_gain
    mean_grad = jnp.mean(grad_normed, -1, keepdims=True)
    mean_proj = jnp.mean(grad_normed * normed, -1, keepdims=True)
    grad_in = inv_std * (grad_normed - mean_grad - normed * mean_proj)
    return (grad_in, jnp.sum(grad_rows * normed, 0), jnp.sum(grad_rows, 0))


def adamw(weight, gradient, first_moment, second, step_rate):
    first_new = beta_one * first_moment + (1.0 - beta_one) * gradient
    second_new = beta_two * second + (1.0 - beta_two) * gradient * gradient
    first_hat = first_new / (1.0 - beta_one**STEP)
    second_hat = second_new / (1.0 - beta_two**STEP)
    weight_new = weight - step_rate * (
        first_hat / (jnp.sqrt(second_hat) + adam_eps) + decay_rate * weight
    )
    return (weight_new, first_new, second_new)


def swap(values, axis, bit):
    size = lax.axis_size(axis)
    return lax.ppermute(values, axis, [(at, at ^ bit) for at in range(size)])


def sum_everywhere(values):
    for axis in ("mp", "dp"):
        bit = 1
        while bit < lax.axis_size(axis):
            values = values + swap(values, axis, bit)
            bit *= 2
    return values


def gather_near(rows, ahead=None):
    half = rows.shape[0] // 2
    near_x, near_y = swap(rows, "mp", 2), swap(rows, "mp", 4)
    if ahead is not None:
        near_x, near_y, ahead = lax.optimization_barrier((near_x, near_y, ahead))
    far_low, far_high = swap(near_x[:half], "mp", 4), swap(near_y[half:], "mp", 2)
    mates = [swap(part, "mp", 1) for part in (rows, near_x, near_y, far_low, far_high)]
    whole = jnp.concatenate(
        [rows, mates[0], near_x, mates[1], near_y, mates[2], far_low, far_high, mates[3], mates[4]],
        0,
    )
    return whole if ahead is None else (whole, ahead)


def far_first(rows, product, quarters):
    size = rows.shape[0] // 4
    pieces = []
    for first, last in quarters:
        if pieces:
            rows, pieces[0] = lax.optimization_barrier((rows, pieces[0]))
        pieces.insert(0, product(rows[first * size : last * size]))
    return pieces


def scatter_near(pieces):
    blocks = []
    own_rows = sum(piece.shape[0] for piece in pieces) // 8
    half = own_rows // 2
    for piece in pieces:
        blocks += [
            piece[at : at + own_rows] for at in range(0, piece.shape[0], own_rows)
        ]
    sums = [
        blocks[at].astype(jnp.float32) + swap(blocks[at + 1], "mp", 1).astype(jnp.float32)
        for at in range(0, 8, 2)
    ]
    far = sums[3].astype(jnp.bfloat16)
    far_low, far_high = swap(far[:half], "mp", 4), swap(far[half:], "mp", 2)
    x_low = (sums[1][:half] + far_low.astype(jnp.float32)).astype(jnp.bfloat16)
    y_high = (sums[2][half:] + far_high.astype(jnp.float32)).astype(jnp.bfloat16)
    x_high, y_low = sums[1][half:].astype(jnp.bfloat16), sums[2][:half].astype(jnp.bfloat16)
    x_low, x_high = swap(x_low, "mp", 2), swap(x_high, "mp", 2)
    y_low, y_high = swap(y_low, "mp", 4), swap(y_high, "mp", 4)
    across_x = jnp.concatenate([x_low, x_high], 0).astype(jnp.float32)
    across_y = jnp.concatenate([y_low, y_high], 0).astype(jnp.float32)
    return sums[0] + across_x + across_y


def core_sum(piece):
    half = piece.shape[0] // 2
    mate = swap(piece[half:], "mp", 1)
    return piece[:half].astype(jnp.float32) + mate.astype(jnp.float32)


def scatter_beside(rows, product):
    far = product(rows, 3)
    rows, far = lax.optimization_barrier((rows, far))
    near_x = product(rows, 1)
    far = core_sum(far).astype(jnp.bfloat16)
    rows, far, near_x = lax.optimization_barrier((rows, far, near_x))
    half = far.shape[0] // 2
    far_low, far_high = swap(far[:half], "mp", 4), swap(far[half:], "mp", 2)
    near_y, far_low, far_high = lax.optimization_barrier((product(rows, 2), far_low, far_high))
    near_x, near_y = core_sum(near_x), core_sum(near_y)
    low, high = slice(0, half), slice(half, 2 * half)
    x_low = (near_x[low] + far_low.astype(jnp.float32)).astype(jnp.bfloat16)
    y_high = (near_y[high] + far_high.astype(jnp.float32)).astype(jnp.bfloat16)
    rows, x_low, y_high = lax.optimization_barrier((rows, x_low, y_high))
    x_high, y_low = near_x[high].astype(jnp.bfloat16), near_y[low].astype(jnp.bfloat16)
    across_x = jnp.concatenate([swap(x_low, "mp", 2), swap(x_high, "mp", 2)], 0)
    across_y = jnp.concatenate([swap(y_low, "mp", 4), swap(y_high, "mp", 4)], 0)
    own, across_x, across_y = lax.optimization_barrier((product(rows, 0), across_x, across_y))
    own = core_sum(own)
    return own + across_x.astype(jnp.float32) + across_y.astype(jnp.float32)


def gather_all(rows, ahead=None):
    whole = lax.all_gather(rows, "mp", axis=0, tiled=True)
    return whole if ahead is None else (whole, ahead)


def scatter_all(pieces):
    whole = jnp.concatenate(pieces, 0)
    return lax.psum_scatter(whole, "mp", scatter_dimension=0, tiled=True).astype(jnp.float32)


def adamw_as(order, weight, gradient, first_moment, second, step_rate, scale):
    turned = [jnp.transpose(rows, order) for rows in (weight, first_moment, second)]
    rank = len(order)
    gradient = with_layout_constraint(gradient, Layout(major_to_minor=tuple(range(rank))))
    gradient = gradient.astype(jnp.float32) * scale
    news = adamw(turned[0], gradient, turned[1], turned[2], step_rate)
    back = tuple(order.index(dim) for dim in range(rank))
    stored = Layout(major_to_minor=order)
    return tuple(with_layout_constraint(jnp.transpose(rows, back), stored) for rows in news)


def local(
    block_input,
    out_cotangent,
    objective,
    prefix_len,
    target_mask,
    qkv_weight,
    out_weight,
    gateup_weight,
    down_weight,
    norm_params,
    qkv_first,
    out_first,
    gateup_first,
    down_first,
    norm_first,
    qkv_second,
    out_second,
    gateup_second,
    down_second,
    norm_second,
):
    mp_index = lax.axis_index("mp")
    own_rows = block_input.shape[0]
    seq_count = objective.shape[0]
    seq_len = own_rows * lax.axis_size("mp") // seq_count
    shard_rows, _, local_dim = qkv_weight.shape
    local_units = gateup_weight.shape[2]
    near = lax.axis_size("mp") == 8 and seq_count == 4 and own_rows % 32 == 0
    if near:
        gather_rows, scatter_rows = gather_near, scatter_near
        place = jnp.stack([mp_index // 2, (mp_index % 2) * own_rows]).astype(jnp.int32)
    else:
        gather_rows, scatter_rows = gather_all, scatter_all
        place = jnp.zeros((2,), jnp.int32)
    two_pieces = ((3, 4), (0, 3))
    seq_info = (objective, prefix_len, place)
    cosine, sine = rope_tables(jnp.arange(seq_len, dtype=jnp.int32) ^ place[1], HD)

    qkv_low = qkv_weight.astype(jnp.bfloat16).reshape(shard_rows, 3 * local_dim)
    attend_low = jnp.concatenate([qkv_low, out_weight.T.astype(jnp.bfloat16)], 1)
    attend_full = lax.all_gather(attend_low, "dp", axis=0, tiled=True)
    qkv_full, out_full = attend_full[:, : 3 * local_dim], attend_full[:, 3 * local_dim :]
    gateup_low = with_layout_constraint(
        jnp.transpose(gateup_weight, (1, 2, 0)).astype(jnp.bfloat16),
        Layout(major_to_minor=(0, 1, 2)),
    )
    gateup_full = lax.all_gather(gateup_low, "dp", axis=2, tiled=True)
    down_full = lax.all_gather(down_weight.astype(jnp.bfloat16), "dp", axis=1, tiled=True)

    mask_f32 = target_mask.astype(jnp.float32)
    target_count = sum_everywhere(jnp.full((8, 128), jnp.sum(mask_f32)))[0, 0]

    cosine, target_count = lax.optimization_barrier((cosine, target_count))

    inputs = gather_rows(block_input)
    proj = jnp.dot(inputs, qkv_full, preferred_element_type=jnp.float32)
    *kept, attended = attend_forward(seq_info, proj, cosine, sine)
    attn_own = scatter_rows(
        far_first(
            attended,
            lambda rows: jnp.einsum(
                "te,de->td", rows, out_full, preferred_element_type=jnp.bfloat16
            ),
            two_pieces,
        )
    )
    hidden_one = deep_alpha * block_input.astype(jnp.float32) + attn_own
    middle, normed_one, inv_one = norm_forward(hidden_one, norm_params[0], norm_params[1])
    middle_low = gather_rows(middle.astype(jnp.bfloat16))

    live_units = (mp_index * local_units + jnp.arange(local_units) < FF).astype(jnp.float32)
    gate_up = jnp.einsum(
        "td,cfd->ctf", middle_low, gateup_full, preferred_element_type=jnp.float32
    )
    hidden_low = (jax.nn.gelu(gate_up[0]) * gate_up[1] * live_units).astype(jnp.bfloat16)
    ffn_own = scatter_rows(
        far_first(
            hidden_low,
            lambda rows: jnp.dot(rows, down_full, preferred_element_type=jnp.bfloat16),
            two_pieces,
        )
    )
    hidden_two = deep_alpha * middle + ffn_own
    output_rows, normed_two, inv_two = norm_forward(hidden_two, norm_params[2], norm_params[3])
    grad_rows = out_cotangent.astype(jnp.float32) * mask_f32[:, None]
    grad_two, gain_two, bias_two = norm_backward(grad_rows, normed_two, inv_two, norm_params[2])

    ffn_back = gather_rows(grad_two.astype(jnp.bfloat16))
    down_grad = jnp.einsum("tf,td->fd", hidden_low, ffn_back, preferred_element_type=jnp.bfloat16)
    ffn_back, down_grad = lax.optimization_barrier((ffn_back, down_grad))
    down_grad = lax.psum_scatter(down_grad, "dp", scatter_dimension=1, tiled=True)
    quarter = ffn_back.shape[0] // 4
    grad_gateups = [None] * 4

    def back_quarter(rows, index):
        at = slice(index * quarter, (index + 1) * quarter)
        gate_act, gelu_pull = jax.vjp(jax.nn.gelu, gate_up[0, at])
        grad_hidden = (
            jnp.einsum("td,fd->tf", rows[at], down_full, preferred_element_type=jnp.float32)
            * live_units
        )
        grad_gate = gelu_pull(grad_hidden * gate_up[1, at])[0]
        grads = jnp.stack([grad_gate, grad_hidden * gate_act], 0).astype(jnp.bfloat16)
        grad_gateups[index] = grads
        return jnp.einsum("ctf,cfd->td", grads, gateup_full, preferred_element_type=jnp.bfloat16)

    if near:
        grad_middle = scatter_beside(ffn_back, back_quarter)
    else:
        grad_middle = scatter_all([back_quarter(ffn_back, index) for index in range(4)])
    grad_middle = grad_middle + deep_alpha * grad_two
    middle_low, down_grad = lax.optimization_barrier((middle_low, down_grad))
    gateup_grad = jnp.einsum(
        "ctf,td->cfd",
        jnp.concatenate(grad_gateups, 1),
        middle_low,
        preferred_element_type=jnp.bfloat16,
    )
    grad_one, gain_one, bias_one = norm_backward(grad_middle, normed_one, inv_one, norm_params[0])

    attn_back, gateup_grad = gather_rows(grad_one.astype(jnp.bfloat16), gateup_grad)
    gateup_grad = with_layout_constraint(
        lax.psum_scatter(gateup_grad, "dp", scatter_dimension=2, tiled=True),
        Layout(major_to_minor=(0, 1, 2)),
    )
    grad_attended = jnp.einsum(
        "td,de->te", attn_back, out_full, preferred_element_type=jnp.bfloat16
    )
    grad_proj = attend_backward(seq_info, *kept, grad_attended, cosine, sine)
    attended, grad_proj = lax.optimization_barrier((attended, grad_proj))
    attend_grad = jnp.concatenate(
        [
            jnp.einsum("te,td->ed", left, right, preferred_element_type=jnp.bfloat16)
            for left, right in ((attended, attn_back), (grad_proj, inputs))
        ],
        0,
    )
    grad_proj, attend_grad = lax.optimization_barrier((grad_proj, attend_grad))
    attend_grad, gateup_grad = lax.optimization_barrier((attend_grad, gateup_grad))
    attend_grad = lax.psum_scatter(attend_grad, "dp", scatter_dimension=1, tiled=True)
    input_raw = (
        scatter_rows(
            far_first(
                grad_proj,
                lambda rows: jnp.einsum(
                    "te,de->td", rows, qkv_full, preferred_element_type=jnp.bfloat16
                ),
                two_pieces,
            )
        )
        + deep_alpha * grad_one
    )
    norm_grad = jnp.stack([gain_one, bias_one, gain_two, bias_two], 0)
    norm_grad, input_raw = lax.optimization_barrier((norm_grad, input_raw))
    norm_grad = sum_everywhere(norm_grad)
    rate_list = (D ** (-0.5), 0.5, D ** (-0.5), (FF_PAD // 64) ** (-0.5), 0.4)
    scale = 1.0 / target_count
    gateup_res = adamw_as(
        (2, 1, 0),
        gateup_weight,
        gateup_grad.transpose(1, 0, 2),
        gateup_first,
        gateup_second,
        rate_list[2],
        scale,
    )
    down_res = adamw_as(
        (0, 1), down_weight, down_grad, down_first, down_second, rate_list[3], scale
    )
    attend_grad, gateup_res, down_res = lax.optimization_barrier(
        (attend_grad, gateup_res, down_res)
    )
    out_grad = attend_grad[:local_dim]
    qkv_grad = attend_grad[local_dim:].reshape(3, local_dim, shard_rows)
    qkv_res = adamw_as(
        (1, 0, 2), qkv_weight, qkv_grad.transpose(0, 2, 1), qkv_first, qkv_second, rate_list[0], scale
    )
    out_res = adamw_as((0, 1), out_weight, out_grad, out_first, out_second, rate_list[1], scale)
    norm_res = adamw(norm_params, norm_grad * scale, norm_first, norm_second, rate_list[4])
    return (
        output_rows.astype(jnp.bfloat16),
        input_raw * scale,
        qkv_res[0],
        qkv_res[1],
        qkv_res[2],
        out_res[0],
        out_res[1],
        out_res[2],
        gateup_res[0],
        gateup_res[1],
        gateup_res[2],
        down_res[0],
        down_res[1],
        down_res[2],
        norm_res[0],
        norm_res[1],
        norm_res[2],
    )


def solution(mesh):
    return jax.shard_map(
        local,
        mesh=mesh,
        in_specs=(
            P(("dp", "mp"), None),
            P(("dp", "mp"), None),
            P("dp"),
            P("dp"),
            P(("dp", "mp")),
            P("dp", None, "mp"),
            P("mp", "dp"),
            P("dp", None, "mp"),
            P("mp", "dp"),
            P(),
            P("dp", None, "mp"),
            P("mp", "dp"),
            P("dp", None, "mp"),
            P("mp", "dp"),
            P(),
            P("dp", None, "mp"),
            P("mp", "dp"),
            P("dp", None, "mp"),
            P("mp", "dp"),
            P(),
        ),
        out_specs=(
            P(("dp", "mp"), None),
            P(("dp", "mp"), None),
            P("dp", None, "mp"),
            P("dp", None, "mp"),
            P("dp", None, "mp"),
            P("mp", "dp"),
            P("mp", "dp"),
            P("mp", "dp"),
            P("dp", None, "mp"),
            P("dp", None, "mp"),
            P("dp", None, "mp"),
            P("mp", "dp"),
            P("mp", "dp"),
            P("mp", "dp"),
            P(),
            P(),
            P(),
        ),
        check_vma=False,
    )
```

```python
import jax
import jax.numpy as jnp
from jax import lax
from jax.experimental import pallas as pl
from jax.experimental.layout import Layout, with_layout_constraint
from jax.experimental.pallas import tpu as pltpu
from jax.sharding import PartitionSpec as P

D = 2048
HD = 128
FF = 5461
FF_PAD = 5472
STEP = 5


deep_alpha = 48.0**0.5
norm_eps = 1e-05
masked_score = -1e30
rope_base = 10000.0
beta_one = 0.5
beta_two = 0.5
adam_eps = 1e-08
decay_rate = 0.1


def rope_tables(position, head_dim):
    freqs = rope_base ** (-jnp.arange(0, head_dim, 2, dtype=jnp.float32) / head_dim)
    angles = position.astype(jnp.float32)[:, None] * freqs[None, :]
    cosine, sine = jnp.cos(angles), jnp.sin(angles)
    return (jnp.concatenate([cosine, cosine], -1), jnp.concatenate([-sine, sine], -1))


def turn(values, cosine, sine):
    return values * cosine + pltpu.roll(values, HD // 2, 1) * sine


def dot_nt(left, right):
    return lax.dot_general(
        left, right, (((1,), (1,)), ((), ())), preferred_element_type=jnp.float32
    )


def dot_nn(left, right):
    return lax.dot_general(
        left, right, (((1,), (0,)), ((), ())), preferred_element_type=jnp.float32
    )


def dot_tn(left, right):
    return lax.dot_general(
        left, right, (((0,), (0,)), ((), ())), preferred_element_type=jnp.float32
    )


def soft_rows(objective_ref, prefix_ref, place_ref, query, key):
    seq_len = query.shape[0]
    seq, flip = pl.program_id(0) ^ place_ref[0], place_ref[1]
    row_at = lax.broadcasted_iota(jnp.int32, (seq_len, seq_len), 0) ^ flip
    col_at = lax.broadcasted_iota(jnp.int32, (seq_len, seq_len), 1) ^ flip
    bound = jnp.where(objective_ref[seq] > 0, seq_len, prefix_ref[seq])
    visible = (col_at < bound) | (col_at <= row_at)
    scores = jnp.where(visible, dot_nt(query, key) * HD ** (-0.5), masked_score)
    exp_scores = jnp.exp(scores - jnp.max(scores, -1, keepdims=True))
    return exp_scores / jnp.sum(exp_scores, -1, keepdims=True)


def attend_kernel(
    objective_ref,
    prefix_ref,
    place_ref,
    proj_ref,
    cos_ref,
    sin_ref,
    query_ref,
    key_ref,
    value_ref,
    out_ref,
):
    local_dim = out_ref.shape[1]
    cosine, sine = cos_ref[...], sin_ref[...]
    for start in range(0, local_dim, HD):
        cols = slice(start, start + HD)
        query = turn(proj_ref[:, start : start + HD], cosine, sine).astype(jnp.bfloat16)
        key_at = local_dim + start
        key = turn(proj_ref[:, key_at : key_at + HD], cosine, sine).astype(jnp.bfloat16)
        value_at = 2 * local_dim + start
        value = proj_ref[:, value_at : value_at + HD].astype(jnp.bfloat16)
        soft = soft_rows(objective_ref, prefix_ref, place_ref, query, key)
        query_ref[:, cols] = query
        key_ref[:, cols] = key
        value_ref[:, cols] = value
        out_ref[:, cols] = dot_nn(soft.astype(jnp.bfloat16), value).astype(jnp.bfloat16)


def attend_back_kernel(
    objective_ref,
    prefix_ref,
    place_ref,
    query_ref,
    key_ref,
    value_ref,
    grad_ref,
    cos_ref,
    sin_ref,
    out_ref,
):
    local_dim = grad_ref.shape[1]
    cosine, sine = cos_ref[...], sin_ref[...]
    scale = HD ** (-0.5)
    for start in range(0, local_dim, HD):
        cols = slice(start, start + HD)
        query, key, value = query_ref[:, cols], key_ref[:, cols], value_ref[:, cols]
        grad = grad_ref[:, cols]
        soft = soft_rows(objective_ref, prefix_ref, place_ref, query, key)
        grad_soft = dot_nt(grad, value)
        row_dot = jnp.sum(soft * grad_soft, -1, keepdims=True)
        grad_scores = (soft * (grad_soft - row_dot)).astype(jnp.bfloat16)
        value_grad = dot_tn(soft.astype(jnp.bfloat16), grad)
        query_grad = turn(dot_nn(grad_scores, key) * scale, cosine, -sine)
        key_grad = turn(dot_tn(grad_scores, query) * scale, cosine, -sine)
        for index, rows in enumerate((query_grad, key_grad, value_grad)):
            at = index * local_dim + start
            out_ref[:, at : at + HD] = rows.astype(jnp.bfloat16)


def seq_specs(seq_len, widths):
    scalars = pl.BlockSpec(memory_space=pltpu.SMEM)
    table = pl.BlockSpec((seq_len, HD), lambda seq: (0, 0))
    rows = [pl.BlockSpec((seq_len, width), lambda seq: (seq, 0)) for width in widths]
    return [scalars] * 3 + rows + [table] * 2


def attend_forward(seq_info, proj, cosine, sine):
    seq_len, (rows, width) = cosine.shape[0], proj.shape
    local_dim = width // 3
    low = jax.ShapeDtypeStruct((rows, local_dim), jnp.bfloat16)
    block = pl.BlockSpec((seq_len, local_dim), lambda seq: (seq, 0))
    return pl.pallas_call(
        attend_kernel,
        grid=(rows // seq_len,),
        out_shape=(low,) * 4,
        in_specs=seq_specs(seq_len, (width,)),
        out_specs=(block,) * 4,
        name="attend_forward",
    )(*seq_info, proj, cosine, sine)


def attend_backward(seq_info, query, key, value, grad, cosine, sine):
    seq_len, (rows, local_dim) = cosine.shape[0], query.shape
    return pl.pallas_call(
        attend_back_kernel,
        grid=(rows // seq_len,),
        out_shape=jax.ShapeDtypeStruct((rows, 3 * local_dim), jnp.bfloat16),
        in_specs=seq_specs(seq_len, (local_dim,) * 4),
        out_specs=pl.BlockSpec((seq_len, 3 * local_dim), lambda seq: (seq, 0)),
        name="attend_backward",
    )(*seq_info, query, key, value, grad, cosine, sine)


def norm_forward(hidden, norm_gain, norm_bias):
    row_mean = jnp.mean(hidden, -1, keepdims=True)
    centred = hidden - row_mean
    variance = jnp.mean(centred * centred, -1, keepdims=True)
    inv_std = lax.rsqrt(variance + norm_eps)
    normed = centred * inv_std
    return (normed * norm_gain + norm_bias, normed, inv_std)


def norm_backward(grad_rows, normed, inv_std, norm_gain):
    grad_normed = grad_rows * norm_gain
    mean_grad = jnp.mean(grad_normed, -1, keepdims=True)
    mean_proj = jnp.mean(grad_normed * normed, -1, keepdims=True)
    grad_in = inv_std * (grad_normed - mean_grad - normed * mean_proj)
    return (grad_in, jnp.sum(grad_rows * normed, 0), jnp.sum(grad_rows, 0))


def adamw(weight, gradient, first_moment, second, step_rate):
    first_new = beta_one * first_moment + (1.0 - beta_one) * gradient
    second_new = beta_two * second + (1.0 - beta_two) * gradient * gradient
    first_hat = first_new / (1.0 - beta_one**STEP)
    second_hat = second_new / (1.0 - beta_two**STEP)
    weight_new = weight - step_rate * (
        first_hat / (jnp.sqrt(second_hat) + adam_eps) + decay_rate * weight
    )
    return (weight_new, first_new, second_new)


def swap(values, axis, bit):
    size = lax.axis_size(axis)
    return lax.ppermute(values, axis, [(at, at ^ bit) for at in range(size)])


def sum_everywhere(values):
    for axis in ("mp", "dp"):
        bit = 1
        while bit < lax.axis_size(axis):
            values = values + swap(values, axis, bit)
            bit *= 2
    return values


def gather_near(rows, ahead=None):
    half = rows.shape[0] // 2
    near_x, near_y = swap(rows, "mp", 2), swap(rows, "mp", 4)
    if ahead is not None:
        near_x, near_y, ahead = lax.optimization_barrier((near_x, near_y, ahead))
    far_low, far_high = swap(near_x[:half], "mp", 4), swap(near_y[half:], "mp", 2)
    mates = [swap(part, "mp", 1) for part in (rows, near_x, near_y, far_low, far_high)]
    whole = jnp.concatenate(
        [rows, mates[0], near_x, mates[1], near_y, mates[2], far_low, far_high, mates[3], mates[4]],
        0,
    )
    return whole if ahead is None else (whole, ahead)


def far_first(rows, product, quarters):
    size = rows.shape[0] // 4
    pieces = []
    for first, last in quarters:
        if pieces:
            rows, pieces[0] = lax.optimization_barrier((rows, pieces[0]))
        pieces.insert(0, product(rows[first * size : last * size]))
    return pieces


def scatter_near(pieces, ahead=None):
    blocks = []
    own_rows = sum(piece.shape[0] for piece in pieces) // 8
    half = own_rows // 2
    for piece in pieces:
        blocks += [
            piece[at : at + own_rows] for at in range(0, piece.shape[0], own_rows)
        ]
    sums = [
        blocks[at].astype(jnp.float32) + swap(blocks[at + 1], "mp", 1).astype(jnp.float32)
        for at in range(0, 8, 2)
    ]
    far = sums[3].astype(jnp.bfloat16)
    far_low, far_high = swap(far[:half], "mp", 4), swap(far[half:], "mp", 2)
    if ahead is not None:
        far_low, far_high, ahead = lax.optimization_barrier((far_low, far_high, ahead))
    x_low = (sums[1][:half] + far_low.astype(jnp.float32)).astype(jnp.bfloat16)
    y_high = (sums[2][half:] + far_high.astype(jnp.float32)).astype(jnp.bfloat16)
    x_high, y_low = sums[1][half:].astype(jnp.bfloat16), sums[2][:half].astype(jnp.bfloat16)
    x_low, x_high = swap(x_low, "mp", 2), swap(x_high, "mp", 2)
    y_low, y_high = swap(y_low, "mp", 4), swap(y_high, "mp", 4)
    across_x = jnp.concatenate([x_low, x_high], 0).astype(jnp.float32)
    across_y = jnp.concatenate([y_low, y_high], 0).astype(jnp.float32)
    total = sums[0] + across_x + across_y
    return total if ahead is None else (total, ahead)


def core_sum(piece):
    half = piece.shape[0] // 2
    mate = swap(piece[half:], "mp", 1)
    return piece[:half].astype(jnp.float32) + mate.astype(jnp.float32)


def scatter_beside(rows, product, last=None):
    far = product(rows, 3)
    rows, far = lax.optimization_barrier((rows, far))
    near_x = product(rows, 1)
    far = core_sum(far).astype(jnp.bfloat16)
    rows, far, near_x = lax.optimization_barrier((rows, far, near_x))
    half = far.shape[0] // 2
    far_low, far_high = swap(far[:half], "mp", 4), swap(far[half:], "mp", 2)
    near_y, far_low, far_high = lax.optimization_barrier((product(rows, 2), far_low, far_high))
    near_x, near_y = core_sum(near_x), core_sum(near_y)
    low, high = slice(0, half), slice(half, 2 * half)
    x_low = (near_x[low] + far_low.astype(jnp.float32)).astype(jnp.bfloat16)
    y_high = (near_y[high] + far_high.astype(jnp.float32)).astype(jnp.bfloat16)
    rows, x_low, y_high = lax.optimization_barrier((rows, x_low, y_high))
    x_high, y_low = near_x[high].astype(jnp.bfloat16), near_y[low].astype(jnp.bfloat16)
    across = [swap(x_low, "mp", 2), swap(x_high, "mp", 2), swap(y_low, "mp", 4), swap(y_high, "mp", 4)]
    own = product(rows, 0)
    ahead = () if last is None else last()
    own, across, ahead = lax.optimization_barrier((own, across, ahead))
    across_x, across_y = jnp.concatenate(across[:2], 0), jnp.concatenate(across[2:], 0)
    own = core_sum(own)
    total = own + across_x.astype(jnp.float32) + across_y.astype(jnp.float32)
    return total if last is None else (total, ahead)


def gather_all(rows, ahead=None):
    whole = lax.all_gather(rows, "mp", axis=0, tiled=True)
    return whole if ahead is None else (whole, ahead)


def scatter_all(pieces, ahead=None):
    whole = jnp.concatenate(pieces, 0)
    total = lax.psum_scatter(whole, "mp", scatter_dimension=0, tiled=True).astype(jnp.float32)
    return total if ahead is None else (total, ahead)


def adamw_as(order, weight, gradient, first_moment, second, step_rate, scale):
    turned = [jnp.transpose(rows, order) for rows in (weight, first_moment, second)]
    rank = len(order)
    gradient = with_layout_constraint(gradient, Layout(major_to_minor=tuple(range(rank))))
    gradient = gradient.astype(jnp.float32) * scale
    news = adamw(turned[0], gradient, turned[1], turned[2], step_rate)
    back = tuple(order.index(dim) for dim in range(rank))
    stored = Layout(major_to_minor=order)
    return tuple(with_layout_constraint(jnp.transpose(rows, back), stored) for rows in news)


def local(
    block_input,
    out_cotangent,
    objective,
    prefix_len,
    target_mask,
    qkv_weight,
    out_weight,
    gateup_weight,
    down_weight,
    norm_params,
    qkv_first,
    out_first,
    gateup_first,
    down_first,
    norm_first,
    qkv_second,
    out_second,
    gateup_second,
    down_second,
    norm_second,
):
    mp_index = lax.axis_index("mp")
    own_rows = block_input.shape[0]
    seq_count = objective.shape[0]
    seq_len = own_rows * lax.axis_size("mp") // seq_count
    shard_rows, _, local_dim = qkv_weight.shape
    local_units = gateup_weight.shape[2]
    near = lax.axis_size("mp") == 8 and seq_count == 4 and own_rows % 32 == 0
    if near:
        gather_rows, scatter_rows = gather_near, scatter_near
        place = jnp.stack([mp_index // 2, (mp_index % 2) * own_rows]).astype(jnp.int32)
    else:
        gather_rows, scatter_rows = gather_all, scatter_all
        place = jnp.zeros((2,), jnp.int32)
    two_pieces = ((3, 4), (0, 3))
    seq_info = (objective, prefix_len, place)
    cosine, sine = rope_tables(jnp.arange(seq_len, dtype=jnp.int32) ^ place[1], HD)

    qkv_low = qkv_weight.astype(jnp.bfloat16).reshape(shard_rows, 3 * local_dim)
    attend_low = jnp.concatenate([qkv_low, out_weight.T.astype(jnp.bfloat16)], 1)
    attend_full = lax.all_gather(attend_low, "dp", axis=0, tiled=True)
    qkv_full, out_full = attend_full[:, : 3 * local_dim], attend_full[:, 3 * local_dim :]
    gateup_low = with_layout_constraint(
        jnp.transpose(gateup_weight, (1, 2, 0)).astype(jnp.bfloat16),
        Layout(major_to_minor=(0, 1, 2)),
    )
    gateup_full = lax.all_gather(gateup_low, "dp", axis=2, tiled=True)
    down_full = lax.all_gather(down_weight.astype(jnp.bfloat16), "dp", axis=1, tiled=True)

    mask_f32 = target_mask.astype(jnp.float32)
    target_count = sum_everywhere(jnp.full((8, 128), jnp.sum(mask_f32)))[0, 0]

    cosine, target_count = lax.optimization_barrier((cosine, target_count))

    inputs = gather_rows(block_input)
    proj = jnp.dot(inputs, qkv_full, preferred_element_type=jnp.float32)
    *kept, attended = attend_forward(seq_info, proj, cosine, sine)
    attn_own = scatter_rows(
        far_first(
            attended,
            lambda rows: jnp.einsum(
                "te,de->td", rows, out_full, preferred_element_type=jnp.bfloat16
            ),
            two_pieces,
        )
    )
    hidden_one = deep_alpha * block_input.astype(jnp.float32) + attn_own
    middle, normed_one, inv_one = norm_forward(hidden_one, norm_params[0], norm_params[1])
    middle_low = gather_rows(middle.astype(jnp.bfloat16))

    live_units = (mp_index * local_units + jnp.arange(local_units) < FF).astype(jnp.float32)
    gate_up = jnp.einsum(
        "td,cfd->ctf", middle_low, gateup_full, preferred_element_type=jnp.float32
    )
    hidden_low = (jax.nn.gelu(gate_up[0]) * gate_up[1] * live_units).astype(jnp.bfloat16)
    quarter = hidden_low.shape[0] // 4

    def down_quarter(rows, index):
        rows = rows[index * quarter : (index + 1) * quarter]
        return jnp.dot(rows, down_full, preferred_element_type=jnp.bfloat16)

    if near:
        ffn_own = scatter_beside(hidden_low, down_quarter)
    else:
        ffn_own = scatter_all([down_quarter(hidden_low, index) for index in range(4)])
    hidden_two = deep_alpha * middle + ffn_own
    output_rows, normed_two, inv_two = norm_forward(hidden_two, norm_params[2], norm_params[3])
    grad_rows = out_cotangent.astype(jnp.float32) * mask_f32[:, None]
    grad_two, gain_two, bias_two = norm_backward(grad_rows, normed_two, inv_two, norm_params[2])

    ffn_back = gather_rows(grad_two.astype(jnp.bfloat16))
    down_grad = jnp.einsum("tf,td->fd", hidden_low, ffn_back, preferred_element_type=jnp.bfloat16)
    ffn_back, down_grad = lax.optimization_barrier((ffn_back, down_grad))
    down_grad = lax.psum_scatter(down_grad, "dp", scatter_dimension=1, tiled=True)
    grad_gateups = [None] * 4

    def back_quarter(rows, index):
        at = slice(index * quarter, (index + 1) * quarter)
        gate_act, gelu_pull = jax.vjp(jax.nn.gelu, gate_up[0, at])
        grad_hidden = (
            jnp.einsum("td,fd->tf", rows[at], down_full, preferred_element_type=jnp.float32)
            * live_units
        )
        grad_gate = gelu_pull(grad_hidden * gate_up[1, at])[0]
        grads = jnp.stack([grad_gate, grad_hidden * gate_act], 0).astype(jnp.bfloat16)
        grad_gateups[index] = grads
        return jnp.einsum("ctf,cfd->td", grads, gateup_full, preferred_element_type=jnp.bfloat16)

    middle_low, down_grad = lax.optimization_barrier((middle_low, down_grad))

    def gateup_product():
        return jnp.einsum(
            "ctf,td->cfd",
            jnp.concatenate(grad_gateups, 1),
            middle_low,
            preferred_element_type=jnp.bfloat16,
        )

    if near:
        grad_middle, gateup_grad = scatter_beside(ffn_back, back_quarter, gateup_product)
    else:
        grad_middle = scatter_all([back_quarter(ffn_back, index) for index in range(4)])
        gateup_grad = gateup_product()
    grad_middle = grad_middle + deep_alpha * grad_two
    grad_one, gain_one, bias_one = norm_backward(grad_middle, normed_one, inv_one, norm_params[0])

    rate_list = (D ** (-0.5), 0.5, D ** (-0.5), (FF_PAD // 64) ** (-0.5), 0.4)
    scale = 1.0 / target_count
    down_res = adamw_as(
        (0, 1), down_weight, down_grad, down_first, down_second, rate_list[3], scale
    )
    attn_back, down_res = gather_rows(grad_one.astype(jnp.bfloat16), down_res)
    gateup_grad = with_layout_constraint(
        lax.psum_scatter(gateup_grad, "dp", scatter_dimension=2, tiled=True),
        Layout(major_to_minor=(0, 1, 2)),
    )
    grad_attended = jnp.einsum(
        "td,de->te", attn_back, out_full, preferred_element_type=jnp.bfloat16
    )
    grad_proj = attend_backward(seq_info, *kept, grad_attended, cosine, sine)
    attended, grad_proj = lax.optimization_barrier((attended, grad_proj))
    attend_grad = jnp.concatenate(
        [
            jnp.einsum("te,td->ed", left, right, preferred_element_type=jnp.bfloat16)
            for left, right in ((attended, attn_back), (grad_proj, inputs))
        ],
        0,
    )
    grad_proj, attend_grad = lax.optimization_barrier((grad_proj, attend_grad))
    attend_grad, gateup_grad = lax.optimization_barrier((attend_grad, gateup_grad))
    attend_grad = lax.psum_scatter(attend_grad, "dp", scatter_dimension=1, tiled=True)
    gateup_res = adamw_as(
        (2, 1, 0),
        gateup_weight,
        gateup_grad.transpose(1, 0, 2),
        gateup_first,
        gateup_second,
        rate_list[2],
        scale,
    )
    input_raw, gateup_res = scatter_rows(
        far_first(
            grad_proj,
            lambda rows: jnp.einsum(
                "te,de->td", rows, qkv_full, preferred_element_type=jnp.bfloat16
            ),
            two_pieces,
        ),
        gateup_res,
    )
    input_raw = input_raw + deep_alpha * grad_one
    norm_grad = jnp.stack([gain_one, bias_one, gain_two, bias_two], 0)
    norm_grad, input_raw = lax.optimization_barrier((norm_grad, input_raw))
    norm_grad = sum_everywhere(norm_grad)
    out_grad = attend_grad[:local_dim]
    qkv_grad = attend_grad[local_dim:].reshape(3, local_dim, shard_rows)
    qkv_res = adamw_as(
        (1, 0, 2), qkv_weight, qkv_grad.transpose(0, 2, 1), qkv_first, qkv_second, rate_list[0], scale
    )
    out_res = adamw_as((0, 1), out_weight, out_grad, out_first, out_second, rate_list[1], scale)
    norm_res = adamw(norm_params, norm_grad * scale, norm_first, norm_second, rate_list[4])
    return (
        output_rows.astype(jnp.bfloat16),
        input_raw * scale,
        qkv_res[0],
        qkv_res[1],
        qkv_res[2],
        out_res[0],
        out_res[1],
        out_res[2],
        gateup_res[0],
        gateup_res[1],
        gateup_res[2],
        down_res[0],
        down_res[1],
        down_res[2],
        norm_res[0],
        norm_res[1],
        norm_res[2],
    )


def solution(mesh):
    return jax.shard_map(
        local,
        mesh=mesh,
        in_specs=(
            P(("dp", "mp"), None),
            P(("dp", "mp"), None),
            P("dp"),
            P("dp"),
            P(("dp", "mp")),
            P("dp", None, "mp"),
            P("mp", "dp"),
            P("dp", None, "mp"),
            P("mp", "dp"),
            P(),
            P("dp", None, "mp"),
            P("mp", "dp"),
            P("dp", None, "mp"),
            P("mp", "dp"),
            P(),
            P("dp", None, "mp"),
            P("mp", "dp"),
            P("dp", None, "mp"),
            P("mp", "dp"),
            P(),
        ),
        out_specs=(
            P(("dp", "mp"), None),
            P(("dp", "mp"), None),
            P("dp", None, "mp"),
            P("dp", None, "mp"),
            P("dp", None, "mp"),
            P("mp", "dp"),
            P("mp", "dp"),
            P("mp", "dp"),
            P("dp", None, "mp"),
            P("dp", None, "mp"),
            P("dp", None, "mp"),
            P("mp", "dp"),
            P("mp", "dp"),
            P("mp", "dp"),
            P(),
            P(),
            P(),
        ),
        check_vma=False,
    )
```

```python
import jax
import jax.numpy as jnp
from jax import lax
from jax.experimental import pallas as pl
from jax.experimental.layout import Layout, with_layout_constraint
from jax.experimental.pallas import tpu as pltpu
from jax.sharding import PartitionSpec as P

D = 2048
HD = 128
FF = 5461
FF_PAD = 5472
STEP = 5


deep_alpha = 48.0**0.5
norm_eps = 1e-05
masked_score = -1e30
rope_base = 10000.0
beta_one = 0.5
beta_two = 0.5
adam_eps = 1e-08
decay_rate = 0.1


def rope_tables(position, head_dim):
    freqs = rope_base ** (-jnp.arange(0, head_dim, 2, dtype=jnp.float32) / head_dim)
    angles = position.astype(jnp.float32)[:, None] * freqs[None, :]
    cosine, sine = jnp.cos(angles), jnp.sin(angles)
    return (jnp.concatenate([cosine, cosine], -1), jnp.concatenate([-sine, sine], -1))


def turn(values, cosine, sine):
    return values * cosine + pltpu.roll(values, HD // 2, 1) * sine


def dot_nt(left, right):
    return lax.dot_general(
        left, right, (((1,), (1,)), ((), ())), preferred_element_type=jnp.float32
    )


def dot_nn(left, right):
    return lax.dot_general(
        left, right, (((1,), (0,)), ((), ())), preferred_element_type=jnp.float32
    )


def dot_tn(left, right):
    return lax.dot_general(
        left, right, (((0,), (0,)), ((), ())), preferred_element_type=jnp.float32
    )


def soft_rows(objective_ref, prefix_ref, place_ref, query, key):
    seq_len = query.shape[0]
    seq, flip = pl.program_id(0) ^ place_ref[0], place_ref[1]
    row_at = lax.broadcasted_iota(jnp.int32, (seq_len, seq_len), 0) ^ flip
    col_at = lax.broadcasted_iota(jnp.int32, (seq_len, seq_len), 1) ^ flip
    bound = jnp.where(objective_ref[seq] > 0, seq_len, prefix_ref[seq])
    visible = (col_at < bound) | (col_at <= row_at)
    scores = jnp.where(visible, dot_nt(query, key) * HD ** (-0.5), masked_score)
    exp_scores = jnp.exp(scores - jnp.max(scores, -1, keepdims=True))
    return exp_scores / jnp.sum(exp_scores, -1, keepdims=True)


def attend_kernel(
    objective_ref,
    prefix_ref,
    place_ref,
    proj_ref,
    cos_ref,
    sin_ref,
    query_ref,
    key_ref,
    value_ref,
    out_ref,
):
    local_dim = out_ref.shape[1]
    cosine, sine = cos_ref[...], sin_ref[...]
    for start in range(0, local_dim, HD):
        cols = slice(start, start + HD)
        query = turn(proj_ref[:, start : start + HD], cosine, sine).astype(jnp.bfloat16)
        key_at = local_dim + start
        key = turn(proj_ref[:, key_at : key_at + HD], cosine, sine).astype(jnp.bfloat16)
        value_at = 2 * local_dim + start
        value = proj_ref[:, value_at : value_at + HD].astype(jnp.bfloat16)
        soft = soft_rows(objective_ref, prefix_ref, place_ref, query, key)
        query_ref[:, cols] = query
        key_ref[:, cols] = key
        value_ref[:, cols] = value
        out_ref[:, cols] = dot_nn(soft.astype(jnp.bfloat16), value).astype(jnp.bfloat16)


def attend_back_kernel(
    objective_ref,
    prefix_ref,
    place_ref,
    query_ref,
    key_ref,
    value_ref,
    grad_ref,
    cos_ref,
    sin_ref,
    out_ref,
):
    local_dim = grad_ref.shape[1]
    cosine, sine = cos_ref[...], sin_ref[...]
    scale = HD ** (-0.5)
    for start in range(0, local_dim, HD):
        cols = slice(start, start + HD)
        query, key, value = query_ref[:, cols], key_ref[:, cols], value_ref[:, cols]
        grad = grad_ref[:, cols]
        soft = soft_rows(objective_ref, prefix_ref, place_ref, query, key)
        grad_soft = dot_nt(grad, value)
        row_dot = jnp.sum(soft * grad_soft, -1, keepdims=True)
        grad_scores = (soft * (grad_soft - row_dot)).astype(jnp.bfloat16)
        value_grad = dot_tn(soft.astype(jnp.bfloat16), grad)
        query_grad = turn(dot_nn(grad_scores, key) * scale, cosine, -sine)
        key_grad = turn(dot_tn(grad_scores, query) * scale, cosine, -sine)
        for index, rows in enumerate((query_grad, key_grad, value_grad)):
            at = index * local_dim + start
            out_ref[:, at : at + HD] = rows.astype(jnp.bfloat16)


def seq_specs(seq_len, widths):
    scalars = pl.BlockSpec(memory_space=pltpu.SMEM)
    table = pl.BlockSpec((seq_len, HD), lambda seq: (0, 0))
    rows = [pl.BlockSpec((seq_len, width), lambda seq: (seq, 0)) for width in widths]
    return [scalars] * 3 + rows + [table] * 2


def attend_forward(seq_info, proj, cosine, sine):
    seq_len, (rows, width) = cosine.shape[0], proj.shape
    local_dim = width // 3
    low = jax.ShapeDtypeStruct((rows, local_dim), jnp.bfloat16)
    block = pl.BlockSpec((seq_len, local_dim), lambda seq: (seq, 0))
    return pl.pallas_call(
        attend_kernel,
        grid=(rows // seq_len,),
        out_shape=(low,) * 4,
        in_specs=seq_specs(seq_len, (width,)),
        out_specs=(block,) * 4,
        name="attend_forward",
    )(*seq_info, proj, cosine, sine)


def attend_backward(seq_info, query, key, value, grad, cosine, sine):
    seq_len, (rows, local_dim) = cosine.shape[0], query.shape
    return pl.pallas_call(
        attend_back_kernel,
        grid=(rows // seq_len,),
        out_shape=jax.ShapeDtypeStruct((rows, 3 * local_dim), jnp.bfloat16),
        in_specs=seq_specs(seq_len, (local_dim,) * 4),
        out_specs=pl.BlockSpec((seq_len, 3 * local_dim), lambda seq: (seq, 0)),
        name="attend_backward",
    )(*seq_info, query, key, value, grad, cosine, sine)


def norm_forward(hidden, norm_gain, norm_bias):
    row_mean = jnp.mean(hidden, -1, keepdims=True)
    centred = hidden - row_mean
    variance = jnp.mean(centred * centred, -1, keepdims=True)
    inv_std = lax.rsqrt(variance + norm_eps)
    normed = centred * inv_std
    return (normed * norm_gain + norm_bias, normed, inv_std)


def norm_backward(grad_rows, normed, inv_std, norm_gain):
    grad_normed = grad_rows * norm_gain
    mean_grad = jnp.mean(grad_normed, -1, keepdims=True)
    mean_proj = jnp.mean(grad_normed * normed, -1, keepdims=True)
    grad_in = inv_std * (grad_normed - mean_grad - normed * mean_proj)
    return (grad_in, jnp.sum(grad_rows * normed, 0), jnp.sum(grad_rows, 0))


def adamw(weight, gradient, first_moment, second, step_rate):
    first_new = beta_one * first_moment + (1.0 - beta_one) * gradient
    second_new = beta_two * second + (1.0 - beta_two) * gradient * gradient
    first_hat = first_new / (1.0 - beta_one**STEP)
    second_hat = second_new / (1.0 - beta_two**STEP)
    weight_new = weight - step_rate * (
        first_hat / (jnp.sqrt(second_hat) + adam_eps) + decay_rate * weight
    )
    return (weight_new, first_new, second_new)


def swap(values, axis, bit):
    size = lax.axis_size(axis)
    return lax.ppermute(values, axis, [(at, at ^ bit) for at in range(size)])


def sum_everywhere(values):
    for axis in ("mp", "dp"):
        bit = 1
        while bit < lax.axis_size(axis):
            values = values + swap(values, axis, bit)
            bit *= 2
    return values


def gather_near(rows, ahead=None):
    half = rows.shape[0] // 2
    near_x, near_y = swap(rows, "mp", 2), swap(rows, "mp", 4)
    if ahead is not None:
        near_x, near_y, ahead = lax.optimization_barrier((near_x, near_y, ahead))
    far_low, far_high = swap(near_x[:half], "mp", 4), swap(near_y[half:], "mp", 2)
    mates = [swap(part, "mp", 1) for part in (rows, near_x, near_y, far_low, far_high)]
    whole = jnp.concatenate(
        [rows, mates[0], near_x, mates[1], near_y, mates[2], far_low, far_high, mates[3], mates[4]],
        0,
    )
    return whole if ahead is None else (whole, ahead)


def far_first(rows, product, quarters):
    size = rows.shape[0] // 4
    pieces = []
    for first, last in quarters:
        if pieces:
            rows, pieces[0] = lax.optimization_barrier((rows, pieces[0]))
        pieces.insert(0, product(rows[first * size : last * size]))
    return pieces


def scatter_near(pieces, ahead=None):
    blocks = []
    own_rows = sum(piece.shape[0] for piece in pieces) // 8
    half = own_rows // 2
    for piece in pieces:
        blocks += [
            piece[at : at + own_rows] for at in range(0, piece.shape[0], own_rows)
        ]
    sums = [
        blocks[at].astype(jnp.float32) + swap(blocks[at + 1], "mp", 1).astype(jnp.float32)
        for at in range(0, 8, 2)
    ]
    far = sums[3].astype(jnp.bfloat16)
    far_low, far_high = swap(far[:half], "mp", 4), swap(far[half:], "mp", 2)
    if ahead is not None:
        far_low, far_high, ahead = lax.optimization_barrier((far_low, far_high, ahead))
    x_low = (sums[1][:half] + far_low.astype(jnp.float32)).astype(jnp.bfloat16)
    y_high = (sums[2][half:] + far_high.astype(jnp.float32)).astype(jnp.bfloat16)
    x_high, y_low = sums[1][half:].astype(jnp.bfloat16), sums[2][:half].astype(jnp.bfloat16)
    x_low, x_high = swap(x_low, "mp", 2), swap(x_high, "mp", 2)
    y_low, y_high = swap(y_low, "mp", 4), swap(y_high, "mp", 4)
    across_x = jnp.concatenate([x_low, x_high], 0).astype(jnp.float32)
    across_y = jnp.concatenate([y_low, y_high], 0).astype(jnp.float32)
    total = sums[0] + across_x + across_y
    return total if ahead is None else (total, ahead)


def core_sum(piece):
    half = piece.shape[0] // 2
    mate = swap(piece[half:], "mp", 1)
    return piece[:half].astype(jnp.float32) + mate.astype(jnp.float32)


def scatter_beside(own, rows, product, last):
    far = product(rows, 3)
    rows, far = lax.optimization_barrier((rows, far))
    near_x = product(rows, 1)
    far, own = core_sum(far).astype(jnp.bfloat16), core_sum(own)
    rows, far, own, near_x = lax.optimization_barrier((rows, far, own, near_x))
    half = far.shape[0] // 2
    far_low, far_high = swap(far[:half], "mp", 4), swap(far[half:], "mp", 2)
    near_y, far_low, far_high = lax.optimization_barrier((product(rows, 2), far_low, far_high))
    near_x, near_y = core_sum(near_x), core_sum(near_y)
    low, high = slice(0, half), slice(half, 2 * half)
    x_low = (near_x[low] + far_low.astype(jnp.float32)).astype(jnp.bfloat16)
    y_high = (near_y[high] + far_high.astype(jnp.float32)).astype(jnp.bfloat16)
    x_high, y_low = near_x[high].astype(jnp.bfloat16), near_y[low].astype(jnp.bfloat16)
    across = [swap(x_low, "mp", 2), swap(x_high, "mp", 2), swap(y_low, "mp", 4), swap(y_high, "mp", 4)]
    across, ahead = lax.optimization_barrier((across, last()))
    across_x, across_y = jnp.concatenate(across[:2], 0), jnp.concatenate(across[2:], 0)
    return own + across_x.astype(jnp.float32) + across_y.astype(jnp.float32), ahead


def gather_beside(rows, product):
    half = rows.shape[0] // 2
    near_x, near_y, mate = swap(rows, "mp", 2), swap(rows, "mp", 4), swap(rows, "mp", 1)
    own = product(jnp.concatenate([rows, mate], 0), 0)
    near_x, near_y, own = lax.optimization_barrier((near_x, near_y, own))
    far_low, far_high = swap(near_x[:half], "mp", 4), swap(near_y[half:], "mp", 2)
    mates = [swap(part, "mp", 1) for part in (near_x, near_y, far_low, far_high)]
    whole = jnp.concatenate(
        [rows, mate, near_x, mates[0], near_y, mates[1], far_low, far_high, *mates[2:]], 0
    )
    return whole, own


def gather_all(rows, ahead=None):
    whole = lax.all_gather(rows, "mp", axis=0, tiled=True)
    return whole if ahead is None else (whole, ahead)


def scatter_all(pieces, ahead=None):
    whole = jnp.concatenate(pieces, 0)
    total = lax.psum_scatter(whole, "mp", scatter_dimension=0, tiled=True).astype(jnp.float32)
    return total if ahead is None else (total, ahead)


def adamw_as(order, weight, gradient, first_moment, second, step_rate, scale):
    turned = [jnp.transpose(rows, order) for rows in (weight, first_moment, second)]
    rank = len(order)
    gradient = with_layout_constraint(gradient, Layout(major_to_minor=tuple(range(rank))))
    gradient = gradient.astype(jnp.float32) * scale
    news = adamw(turned[0], gradient, turned[1], turned[2], step_rate)
    back = tuple(order.index(dim) for dim in range(rank))
    stored = Layout(major_to_minor=order)
    return tuple(with_layout_constraint(jnp.transpose(rows, back), stored) for rows in news)


def local(
    block_input,
    out_cotangent,
    objective,
    prefix_len,
    target_mask,
    qkv_weight,
    out_weight,
    gateup_weight,
    down_weight,
    norm_params,
    qkv_first,
    out_first,
    gateup_first,
    down_first,
    norm_first,
    qkv_second,
    out_second,
    gateup_second,
    down_second,
    norm_second,
):
    mp_index = lax.axis_index("mp")
    own_rows = block_input.shape[0]
    seq_count = objective.shape[0]
    seq_len = own_rows * lax.axis_size("mp") // seq_count
    shard_rows, _, local_dim = qkv_weight.shape
    local_units = gateup_weight.shape[2]
    near = lax.axis_size("mp") == 8 and seq_count == 4 and own_rows % 32 == 0
    if near:
        gather_rows, scatter_rows = gather_near, scatter_near
        place = jnp.stack([mp_index // 2, (mp_index % 2) * own_rows]).astype(jnp.int32)
    else:
        gather_rows, scatter_rows = gather_all, scatter_all
        place = jnp.zeros((2,), jnp.int32)
    two_pieces = ((3, 4), (0, 3))
    seq_info = (objective, prefix_len, place)
    cosine, sine = rope_tables(jnp.arange(seq_len, dtype=jnp.int32) ^ place[1], HD)

    qkv_low = qkv_weight.astype(jnp.bfloat16).reshape(shard_rows, 3 * local_dim)
    attend_low = jnp.concatenate([qkv_low, out_weight.T.astype(jnp.bfloat16)], 1)
    attend_full = lax.all_gather(attend_low, "dp", axis=0, tiled=True)
    qkv_full, out_full = attend_full[:, : 3 * local_dim], attend_full[:, 3 * local_dim :]
    gateup_low = with_layout_constraint(
        jnp.transpose(gateup_weight, (1, 2, 0)).astype(jnp.bfloat16),
        Layout(major_to_minor=(0, 1, 2)),
    )
    gateup_full = lax.all_gather(gateup_low, "dp", axis=2, tiled=True)
    down_full = lax.all_gather(down_weight.astype(jnp.bfloat16), "dp", axis=1, tiled=True)

    mask_f32 = target_mask.astype(jnp.float32)
    target_count = sum_everywhere(jnp.full((8, 128), jnp.sum(mask_f32)))[0, 0]

    cosine, target_count = lax.optimization_barrier((cosine, target_count))

    inputs = gather_rows(block_input)
    proj = jnp.dot(inputs, qkv_full, preferred_element_type=jnp.float32)
    *kept, attended = attend_forward(seq_info, proj, cosine, sine)
    attn_own = scatter_rows(
        far_first(
            attended,
            lambda rows: jnp.einsum(
                "te,de->td", rows, out_full, preferred_element_type=jnp.bfloat16
            ),
            two_pieces,
        )
    )
    hidden_one = deep_alpha * block_input.astype(jnp.float32) + attn_own
    middle, normed_one, inv_one = norm_forward(hidden_one, norm_params[0], norm_params[1])
    middle_low = gather_rows(middle.astype(jnp.bfloat16))

    live_units = (mp_index * local_units + jnp.arange(local_units) < FF).astype(jnp.float32)
    gate_up = jnp.einsum(
        "td,cfd->ctf", middle_low, gateup_full, preferred_element_type=jnp.float32
    )
    hidden_low = (jax.nn.gelu(gate_up[0]) * gate_up[1] * live_units).astype(jnp.bfloat16)
    ffn_own = scatter_rows(
        far_first(
            hidden_low,
            lambda rows: jnp.dot(rows, down_full, preferred_element_type=jnp.bfloat16),
            two_pieces,
        )
    )
    quarter = hidden_low.shape[0] // 4
    hidden_two = deep_alpha * middle + ffn_own
    output_rows, normed_two, inv_two = norm_forward(hidden_two, norm_params[2], norm_params[3])
    grad_rows = out_cotangent.astype(jnp.float32) * mask_f32[:, None]
    grad_two, gain_two, bias_two = norm_backward(grad_rows, normed_two, inv_two, norm_params[2])

    grad_gateups = [None] * 4

    def back_quarter(chunk, index):
        at = slice(index * quarter, (index + 1) * quarter)
        gate_act, gelu_pull = jax.vjp(jax.nn.gelu, gate_up[0, at])
        grad_hidden = (
            jnp.einsum("td,fd->tf", chunk, down_full, preferred_element_type=jnp.float32)
            * live_units
        )
        grad_gate = gelu_pull(grad_hidden * gate_up[1, at])[0]
        grads = jnp.stack([grad_gate, grad_hidden * gate_act], 0).astype(jnp.bfloat16)
        grad_gateups[index] = grads
        return jnp.einsum("ctf,cfd->td", grads, gateup_full, preferred_element_type=jnp.bfloat16)

    def back_rows(rows, index):
        return back_quarter(rows[index * quarter : (index + 1) * quarter], index)

    back_low = grad_two.astype(jnp.bfloat16)
    if near:
        ffn_back, own_part = gather_beside(back_low, back_quarter)
    else:
        ffn_back = gather_rows(back_low)
    down_grad = jnp.einsum("tf,td->fd", hidden_low, ffn_back, preferred_element_type=jnp.bfloat16)
    ffn_back, down_grad = lax.optimization_barrier((ffn_back, down_grad))
    down_grad = lax.psum_scatter(down_grad, "dp", scatter_dimension=1, tiled=True)

    def gateup_product():
        return jnp.einsum(
            "ctf,td->cfd",
            jnp.concatenate(grad_gateups, 1),
            middle_low,
            preferred_element_type=jnp.bfloat16,
        )

    if near:
        grad_middle, gateup_grad = scatter_beside(
            own_part, ffn_back, back_rows, gateup_product
        )
    else:
        grad_middle = scatter_all([back_rows(ffn_back, index) for index in range(4)])
        gateup_grad = gateup_product()
    grad_middle = grad_middle + deep_alpha * grad_two
    grad_one, gain_one, bias_one = norm_backward(grad_middle, normed_one, inv_one, norm_params[0])

    rate_list = (D ** (-0.5), 0.5, D ** (-0.5), (FF_PAD // 64) ** (-0.5), 0.4)
    scale = 1.0 / target_count
    down_res = adamw_as(
        (0, 1), down_weight, down_grad, down_first, down_second, rate_list[3], scale
    )
    attn_back, down_res = gather_rows(grad_one.astype(jnp.bfloat16), down_res)
    gateup_grad, down_grad = lax.optimization_barrier((gateup_grad, down_grad))
    gateup_grad = with_layout_constraint(
        lax.psum_scatter(gateup_grad, "dp", scatter_dimension=2, tiled=True),
        Layout(major_to_minor=(0, 1, 2)),
    )
    grad_attended = jnp.einsum(
        "td,de->te", attn_back, out_full, preferred_element_type=jnp.bfloat16
    )
    grad_proj = attend_backward(seq_info, *kept, grad_attended, cosine, sine)
    attended, grad_proj = lax.optimization_barrier((attended, grad_proj))
    attend_grad = jnp.concatenate(
        [
            jnp.einsum("te,td->ed", left, right, preferred_element_type=jnp.bfloat16)
            for left, right in ((attended, attn_back), (grad_proj, inputs))
        ],
        0,
    )
    grad_proj, attend_grad = lax.optimization_barrier((grad_proj, attend_grad))
    attend_grad, gateup_grad = lax.optimization_barrier((attend_grad, gateup_grad))
    attend_grad = lax.psum_scatter(attend_grad, "dp", scatter_dimension=1, tiled=True)
    gateup_res = adamw_as(
        (2, 1, 0),
        gateup_weight,
        gateup_grad.transpose(1, 0, 2),
        gateup_first,
        gateup_second,
        rate_list[2],
        scale,
    )
    input_raw, gateup_res = scatter_rows(
        far_first(
            grad_proj,
            lambda rows: jnp.einsum(
                "te,de->td", rows, qkv_full, preferred_element_type=jnp.bfloat16
            ),
            two_pieces,
        ),
        gateup_res,
    )
    input_raw = input_raw + deep_alpha * grad_one
    norm_grad = jnp.stack([gain_one, bias_one, gain_two, bias_two], 0)
    norm_grad, input_raw = lax.optimization_barrier((norm_grad, input_raw))
    norm_grad = sum_everywhere(norm_grad)
    out_grad = attend_grad[:local_dim]
    qkv_grad = attend_grad[local_dim:].reshape(3, local_dim, shard_rows)
    qkv_res = adamw_as(
        (1, 0, 2), qkv_weight, qkv_grad.transpose(0, 2, 1), qkv_first, qkv_second, rate_list[0], scale
    )
    out_res = adamw_as((0, 1), out_weight, out_grad, out_first, out_second, rate_list[1], scale)
    norm_res = adamw(norm_params, norm_grad * scale, norm_first, norm_second, rate_list[4])
    return (
        output_rows.astype(jnp.bfloat16),
        input_raw * scale,
        qkv_res[0],
        qkv_res[1],
        qkv_res[2],
        out_res[0],
        out_res[1],
        out_res[2],
        gateup_res[0],
        gateup_res[1],
        gateup_res[2],
        down_res[0],
        down_res[1],
        down_res[2],
        norm_res[0],
        norm_res[1],
        norm_res[2],
    )


def solution(mesh):
    return jax.shard_map(
        local,
        mesh=mesh,
        in_specs=(
            P(("dp", "mp"), None),
            P(("dp", "mp"), None),
            P("dp"),
            P("dp"),
            P(("dp", "mp")),
            P("dp", None, "mp"),
            P("mp", "dp"),
            P("dp", None, "mp"),
            P("mp", "dp"),
            P(),
            P("dp", None, "mp"),
            P("mp", "dp"),
            P("dp", None, "mp"),
            P("mp", "dp"),
            P(),
            P("dp", None, "mp"),
            P("mp", "dp"),
            P("dp", None, "mp"),
            P("mp", "dp"),
            P(),
        ),
        out_specs=(
            P(("dp", "mp"), None),
            P(("dp", "mp"), None),
            P("dp", None, "mp"),
            P("dp", None, "mp"),
            P("dp", None, "mp"),
            P("mp", "dp"),
            P("mp", "dp"),
            P("mp", "dp"),
            P("dp", None, "mp"),
            P("dp", None, "mp"),
            P("dp", None, "mp"),
            P("mp", "dp"),
            P("mp", "dp"),
            P("mp", "dp"),
            P(),
            P(),
            P(),
        ),
        check_vma=False,
    )
```

```python
import jax
import jax.numpy as jnp
from jax import lax
from jax.experimental import pallas as pl
from jax.experimental.layout import Layout, with_layout_constraint
from jax.experimental.pallas import tpu as pltpu
from jax.sharding import PartitionSpec as P

D = 2048
HD = 128
FF = 5461
FF_PAD = 5472
STEP = 5


deep_alpha = 48.0**0.5
norm_eps = 1e-05
masked_score = -1e30
rope_base = 10000.0
beta_one = 0.5
beta_two = 0.5
adam_eps = 1e-08
decay_rate = 0.1


def rope_tables(position, head_dim):
    freqs = rope_base ** (-jnp.arange(0, head_dim, 2, dtype=jnp.float32) / head_dim)
    angles = position.astype(jnp.float32)[:, None] * freqs[None, :]
    cosine, sine = jnp.cos(angles), jnp.sin(angles)
    return (jnp.concatenate([cosine, cosine], -1), jnp.concatenate([-sine, sine], -1))


def turn(values, cosine, sine):
    return values * cosine + pltpu.roll(values, HD // 2, 1) * sine


def dot_nt(left, right):
    return lax.dot_general(
        left, right, (((1,), (1,)), ((), ())), preferred_element_type=jnp.float32
    )


def dot_nn(left, right):
    return lax.dot_general(
        left, right, (((1,), (0,)), ((), ())), preferred_element_type=jnp.float32
    )


def dot_tn(left, right):
    return lax.dot_general(
        left, right, (((0,), (0,)), ((), ())), preferred_element_type=jnp.float32
    )


def soft_rows(objective_ref, prefix_ref, place_ref, query, key):
    seq_len = query.shape[0]
    seq, flip = pl.program_id(0) ^ place_ref[0], place_ref[1]
    row_at = lax.broadcasted_iota(jnp.int32, (seq_len, seq_len), 0) ^ flip
    col_at = lax.broadcasted_iota(jnp.int32, (seq_len, seq_len), 1) ^ flip
    bound = jnp.where(objective_ref[seq] > 0, seq_len, prefix_ref[seq])
    visible = (col_at < bound) | (col_at <= row_at)
    scores = jnp.where(visible, dot_nt(query, key) * HD ** (-0.5), masked_score)
    exp_scores = jnp.exp(scores - jnp.max(scores, -1, keepdims=True))
    return exp_scores / jnp.sum(exp_scores, -1, keepdims=True)


def attend_kernel(
    objective_ref,
    prefix_ref,
    place_ref,
    proj_ref,
    cos_ref,
    sin_ref,
    query_ref,
    key_ref,
    value_ref,
    out_ref,
):
    local_dim = out_ref.shape[1]
    cosine, sine = cos_ref[...], sin_ref[...]
    for start in range(0, local_dim, HD):
        cols = slice(start, start + HD)
        query = turn(proj_ref[:, start : start + HD], cosine, sine).astype(jnp.bfloat16)
        key_at = local_dim + start
        key = turn(proj_ref[:, key_at : key_at + HD], cosine, sine).astype(jnp.bfloat16)
        value_at = 2 * local_dim + start
        value = proj_ref[:, value_at : value_at + HD].astype(jnp.bfloat16)
        soft = soft_rows(objective_ref, prefix_ref, place_ref, query, key)
        query_ref[:, cols] = query
        key_ref[:, cols] = key
        value_ref[:, cols] = value
        out_ref[:, cols] = dot_nn(soft.astype(jnp.bfloat16), value).astype(jnp.bfloat16)


def attend_back_kernel(
    objective_ref,
    prefix_ref,
    place_ref,
    query_ref,
    key_ref,
    value_ref,
    grad_ref,
    cos_ref,
    sin_ref,
    out_ref,
):
    local_dim = grad_ref.shape[1]
    cosine, sine = cos_ref[...], sin_ref[...]
    scale = HD ** (-0.5)
    for start in range(0, local_dim, HD):
        cols = slice(start, start + HD)
        query, key, value = query_ref[:, cols], key_ref[:, cols], value_ref[:, cols]
        grad = grad_ref[:, cols]
        soft = soft_rows(objective_ref, prefix_ref, place_ref, query, key)
        grad_soft = dot_nt(grad, value)
        row_dot = jnp.sum(soft * grad_soft, -1, keepdims=True)
        grad_scores = (soft * (grad_soft - row_dot)).astype(jnp.bfloat16)
        value_grad = dot_tn(soft.astype(jnp.bfloat16), grad)
        query_grad = turn(dot_nn(grad_scores, key) * scale, cosine, -sine)
        key_grad = turn(dot_tn(grad_scores, query) * scale, cosine, -sine)
        for index, rows in enumerate((query_grad, key_grad, value_grad)):
            at = index * local_dim + start
            out_ref[:, at : at + HD] = rows.astype(jnp.bfloat16)


def seq_specs(seq_len, widths):
    scalars = pl.BlockSpec(memory_space=pltpu.SMEM)
    table = pl.BlockSpec((seq_len, HD), lambda seq: (0, 0))
    rows = [pl.BlockSpec((seq_len, width), lambda seq: (seq, 0)) for width in widths]
    return [scalars] * 3 + rows + [table] * 2


def attend_forward(seq_info, proj, cosine, sine):
    seq_len, (rows, width) = cosine.shape[0], proj.shape
    local_dim = width // 3
    low = jax.ShapeDtypeStruct((rows, local_dim), jnp.bfloat16)
    block = pl.BlockSpec((seq_len, local_dim), lambda seq: (seq, 0))
    return pl.pallas_call(
        attend_kernel,
        grid=(rows // seq_len,),
        out_shape=(low,) * 4,
        in_specs=seq_specs(seq_len, (width,)),
        out_specs=(block,) * 4,
        name="attend_forward",
    )(*seq_info, proj, cosine, sine)


def attend_backward(seq_info, query, key, value, grad, cosine, sine):
    seq_len, (rows, local_dim) = cosine.shape[0], query.shape
    return pl.pallas_call(
        attend_back_kernel,
        grid=(rows // seq_len,),
        out_shape=jax.ShapeDtypeStruct((rows, 3 * local_dim), jnp.bfloat16),
        in_specs=seq_specs(seq_len, (local_dim,) * 4),
        out_specs=pl.BlockSpec((seq_len, 3 * local_dim), lambda seq: (seq, 0)),
        name="attend_backward",
    )(*seq_info, query, key, value, grad, cosine, sine)


def norm_forward(hidden, norm_gain, norm_bias):
    row_mean = jnp.mean(hidden, -1, keepdims=True)
    centred = hidden - row_mean
    variance = jnp.mean(centred * centred, -1, keepdims=True)
    inv_std = lax.rsqrt(variance + norm_eps)
    normed = centred * inv_std
    return (normed * norm_gain + norm_bias, normed, inv_std)


def norm_backward(grad_rows, normed, inv_std, norm_gain):
    grad_normed = grad_rows * norm_gain
    mean_grad = jnp.mean(grad_normed, -1, keepdims=True)
    mean_proj = jnp.mean(grad_normed * normed, -1, keepdims=True)
    grad_in = inv_std * (grad_normed - mean_grad - normed * mean_proj)
    return (grad_in, jnp.sum(grad_rows * normed, 0), jnp.sum(grad_rows, 0))


def adamw(weight, gradient, first_moment, second, step_rate):
    first_new = beta_one * first_moment + (1.0 - beta_one) * gradient
    second_new = beta_two * second + (1.0 - beta_two) * gradient * gradient
    first_hat = first_new / (1.0 - beta_one**STEP)
    second_hat = second_new / (1.0 - beta_two**STEP)
    weight_new = weight - step_rate * (
        first_hat / (jnp.sqrt(second_hat) + adam_eps) + decay_rate * weight
    )
    return (weight_new, first_new, second_new)


def swap(values, axis, bit):
    size = lax.axis_size(axis)
    return lax.ppermute(values, axis, [(at, at ^ bit) for at in range(size)])


def sum_everywhere(values):
    for axis in ("mp", "dp"):
        bit = 1
        while bit < lax.axis_size(axis):
            values = values + swap(values, axis, bit)
            bit *= 2
    return values


def gather_near(rows, ahead=None):
    half = rows.shape[0] // 2
    near_x, near_y = swap(rows, "mp", 2), swap(rows, "mp", 4)
    if ahead is not None:
        near_x, near_y, ahead = lax.optimization_barrier((near_x, near_y, ahead))
    far_low, far_high = swap(near_x[:half], "mp", 4), swap(near_y[half:], "mp", 2)
    mates = [swap(part, "mp", 1) for part in (rows, near_x, near_y, far_low, far_high)]
    whole = jnp.concatenate(
        [rows, mates[0], near_x, mates[1], near_y, mates[2], far_low, far_high, mates[3], mates[4]],
        0,
    )
    return whole if ahead is None else (whole, ahead)


def far_first(rows, product, quarters):
    size = rows.shape[0] // 4
    pieces = []
    for first, last in quarters:
        if pieces:
            rows, pieces[0] = lax.optimization_barrier((rows, pieces[0]))
        pieces.insert(0, product(rows[first * size : last * size]))
    return pieces


def scatter_near(pieces, ahead=None):
    blocks = []
    own_rows = sum(piece.shape[0] for piece in pieces) // 8
    half = own_rows // 2
    for piece in pieces:
        blocks += [
            piece[at : at + own_rows] for at in range(0, piece.shape[0], own_rows)
        ]
    sums = [
        blocks[at].astype(jnp.float32) + swap(blocks[at + 1], "mp", 1).astype(jnp.float32)
        for at in range(0, 8, 2)
    ]
    far = sums[3].astype(jnp.bfloat16)
    far_low, far_high = swap(far[:half], "mp", 4), swap(far[half:], "mp", 2)
    if ahead is not None:
        far_low, far_high, ahead = lax.optimization_barrier((far_low, far_high, ahead))
    x_low = (sums[1][:half] + far_low.astype(jnp.float32)).astype(jnp.bfloat16)
    y_high = (sums[2][half:] + far_high.astype(jnp.float32)).astype(jnp.bfloat16)
    x_high, y_low = sums[1][half:].astype(jnp.bfloat16), sums[2][:half].astype(jnp.bfloat16)
    x_low, x_high = swap(x_low, "mp", 2), swap(x_high, "mp", 2)
    y_low, y_high = swap(y_low, "mp", 4), swap(y_high, "mp", 4)
    across_x = jnp.concatenate([x_low, x_high], 0).astype(jnp.float32)
    across_y = jnp.concatenate([y_low, y_high], 0).astype(jnp.float32)
    total = sums[0] + across_x + across_y
    return total if ahead is None else (total, ahead)


def core_sum(piece):
    half = piece.shape[0] // 2
    mate = swap(piece[half:], "mp", 1)
    return piece[:half].astype(jnp.float32) + mate.astype(jnp.float32)


def scatter_beside(own, near_x, rows, product, last):
    own, near_x = core_sum(own), core_sum(near_x)
    rows, own, near_x = lax.optimization_barrier((rows, own, near_x))
    far = core_sum(product(rows, 3)).astype(jnp.bfloat16)
    rows, far = lax.optimization_barrier((rows, far))
    half = far.shape[0] // 2
    far_low, far_high = swap(far[:half], "mp", 4), swap(far[half:], "mp", 2)
    near_y, far_low, far_high = lax.optimization_barrier((product(rows, 2), far_low, far_high))
    near_y = core_sum(near_y)
    low, high = slice(0, half), slice(half, 2 * half)
    x_low = (near_x[low] + far_low.astype(jnp.float32)).astype(jnp.bfloat16)
    y_high = (near_y[high] + far_high.astype(jnp.float32)).astype(jnp.bfloat16)
    x_high, y_low = near_x[high].astype(jnp.bfloat16), near_y[low].astype(jnp.bfloat16)
    across = [swap(x_low, "mp", 2), swap(x_high, "mp", 2), swap(y_low, "mp", 4), swap(y_high, "mp", 4)]
    across, ahead = lax.optimization_barrier((across, last()))
    across_x, across_y = jnp.concatenate(across[:2], 0), jnp.concatenate(across[2:], 0)
    return own + across_x.astype(jnp.float32) + across_y.astype(jnp.float32), ahead


def gather_beside(rows, product):
    half = rows.shape[0] // 2
    near_x, near_y, mate = swap(rows, "mp", 2), swap(rows, "mp", 4), swap(rows, "mp", 1)
    own = product(jnp.concatenate([rows, mate], 0), 0)
    near_x, near_y, own = lax.optimization_barrier((near_x, near_y, own))
    far_low, far_high = swap(near_x[:half], "mp", 4), swap(near_y[half:], "mp", 2)
    mate_x, mate_y = swap(near_x, "mp", 1), swap(near_y, "mp", 1)
    across_x = product(jnp.concatenate([near_x, mate_x], 0), 1)
    far_low, far_high, across_x = lax.optimization_barrier((far_low, far_high, across_x))
    mates = [swap(far_low, "mp", 1), swap(far_high, "mp", 1)]
    whole = jnp.concatenate(
        [rows, mate, near_x, mate_x, near_y, mate_y, far_low, far_high, *mates], 0
    )
    return whole, own, across_x


def gather_all(rows, ahead=None):
    whole = lax.all_gather(rows, "mp", axis=0, tiled=True)
    return whole if ahead is None else (whole, ahead)


def scatter_all(pieces, ahead=None):
    whole = jnp.concatenate(pieces, 0)
    total = lax.psum_scatter(whole, "mp", scatter_dimension=0, tiled=True).astype(jnp.float32)
    return total if ahead is None else (total, ahead)


def adamw_as(order, weight, gradient, first_moment, second, step_rate, scale):
    turned = [jnp.transpose(rows, order) for rows in (weight, first_moment, second)]
    rank = len(order)
    gradient = with_layout_constraint(gradient, Layout(major_to_minor=tuple(range(rank))))
    gradient = gradient.astype(jnp.float32) * scale
    news = adamw(turned[0], gradient, turned[1], turned[2], step_rate)
    back = tuple(order.index(dim) for dim in range(rank))
    stored = Layout(major_to_minor=order)
    return tuple(with_layout_constraint(jnp.transpose(rows, back), stored) for rows in news)


def local(
    block_input,
    out_cotangent,
    objective,
    prefix_len,
    target_mask,
    qkv_weight,
    out_weight,
    gateup_weight,
    down_weight,
    norm_params,
    qkv_first,
    out_first,
    gateup_first,
    down_first,
    norm_first,
    qkv_second,
    out_second,
    gateup_second,
    down_second,
    norm_second,
):
    mp_index = lax.axis_index("mp")
    own_rows = block_input.shape[0]
    seq_count = objective.shape[0]
    seq_len = own_rows * lax.axis_size("mp") // seq_count
    shard_rows, _, local_dim = qkv_weight.shape
    local_units = gateup_weight.shape[2]
    near = lax.axis_size("mp") == 8 and seq_count == 4 and own_rows % 32 == 0
    if near:
        gather_rows, scatter_rows = gather_near, scatter_near
        place = jnp.stack([mp_index // 2, (mp_index % 2) * own_rows]).astype(jnp.int32)
    else:
        gather_rows, scatter_rows = gather_all, scatter_all
        place = jnp.zeros((2,), jnp.int32)
    two_pieces = ((3, 4), (0, 3))
    seq_info = (objective, prefix_len, place)
    cosine, sine = rope_tables(jnp.arange(seq_len, dtype=jnp.int32) ^ place[1], HD)

    qkv_low = qkv_weight.astype(jnp.bfloat16).reshape(shard_rows, 3 * local_dim)
    attend_low = jnp.concatenate([qkv_low, out_weight.T.astype(jnp.bfloat16)], 1)
    attend_full = lax.all_gather(attend_low, "dp", axis=0, tiled=True)
    qkv_full, out_full = attend_full[:, : 3 * local_dim], attend_full[:, 3 * local_dim :]
    gateup_low = with_layout_constraint(
        jnp.transpose(gateup_weight, (1, 2, 0)).astype(jnp.bfloat16),
        Layout(major_to_minor=(0, 1, 2)),
    )
    gateup_full = lax.all_gather(gateup_low, "dp", axis=2, tiled=True)
    down_full = lax.all_gather(down_weight.astype(jnp.bfloat16), "dp", axis=1, tiled=True)

    mask_f32 = target_mask.astype(jnp.float32)
    target_count = sum_everywhere(jnp.full((8, 128), jnp.sum(mask_f32)))[0, 0]

    cosine, target_count = lax.optimization_barrier((cosine, target_count))

    inputs = gather_rows(block_input)
    proj = jnp.dot(inputs, qkv_full, preferred_element_type=jnp.float32)
    *kept, attended = attend_forward(seq_info, proj, cosine, sine)
    attn_own = scatter_rows(
        far_first(
            attended,
            lambda rows: jnp.einsum(
                "te,de->td", rows, out_full, preferred_element_type=jnp.bfloat16
            ),
            two_pieces,
        )
    )
    hidden_one = deep_alpha * block_input.astype(jnp.float32) + attn_own
    middle, normed_one, inv_one = norm_forward(hidden_one, norm_params[0], norm_params[1])
    middle_low = gather_rows(middle.astype(jnp.bfloat16))

    live_units = (mp_index * local_units + jnp.arange(local_units) < FF).astype(jnp.float32)
    gate_up = jnp.einsum(
        "td,cfd->ctf", middle_low, gateup_full, preferred_element_type=jnp.float32
    )
    hidden_low = (jax.nn.gelu(gate_up[0]) * gate_up[1] * live_units).astype(jnp.bfloat16)
    ffn_own = scatter_rows(
        far_first(
            hidden_low,
            lambda rows: jnp.dot(rows, down_full, preferred_element_type=jnp.bfloat16),
            two_pieces,
        )
    )
    quarter = hidden_low.shape[0] // 4
    hidden_two = deep_alpha * middle + ffn_own
    output_rows, normed_two, inv_two = norm_forward(hidden_two, norm_params[2], norm_params[3])
    grad_rows = out_cotangent.astype(jnp.float32) * mask_f32[:, None]
    grad_two, gain_two, bias_two = norm_backward(grad_rows, normed_two, inv_two, norm_params[2])

    grad_gateups = [None] * 4

    def back_quarter(chunk, index):
        at = slice(index * quarter, (index + 1) * quarter)
        gate_act, gelu_pull = jax.vjp(jax.nn.gelu, gate_up[0, at])
        grad_hidden = (
            jnp.einsum("td,fd->tf", chunk, down_full, preferred_element_type=jnp.float32)
            * live_units
        )
        grad_gate = gelu_pull(grad_hidden * gate_up[1, at])[0]
        grads = jnp.stack([grad_gate, grad_hidden * gate_act], 0).astype(jnp.bfloat16)
        grad_gateups[index] = grads
        return jnp.einsum("ctf,cfd->td", grads, gateup_full, preferred_element_type=jnp.bfloat16)

    def back_rows(rows, index):
        return back_quarter(rows[index * quarter : (index + 1) * quarter], index)

    back_low = grad_two.astype(jnp.bfloat16)
    if near:
        ffn_back, own_part, x_part = gather_beside(back_low, back_quarter)
    else:
        ffn_back = gather_rows(back_low)
    down_grad = jnp.einsum("tf,td->fd", hidden_low, ffn_back, preferred_element_type=jnp.bfloat16)
    ffn_back, down_grad = lax.optimization_barrier((ffn_back, down_grad))
    down_grad = lax.psum_scatter(down_grad, "dp", scatter_dimension=1, tiled=True)

    def gateup_product():
        return jnp.einsum(
            "ctf,td->cfd",
            jnp.concatenate(grad_gateups, 1),
            middle_low,
            preferred_element_type=jnp.bfloat16,
        )

    if near:
        grad_middle, gateup_grad = scatter_beside(
            own_part, x_part, ffn_back, back_rows, gateup_product
        )
    else:
        grad_middle = scatter_all([back_rows(ffn_back, index) for index in range(4)])
        gateup_grad = gateup_product()
    grad_middle = grad_middle + deep_alpha * grad_two
    grad_one, gain_one, bias_one = norm_backward(grad_middle, normed_one, inv_one, norm_params[0])

    rate_list = (D ** (-0.5), 0.5, D ** (-0.5), (FF_PAD // 64) ** (-0.5), 0.4)
    scale = 1.0 / target_count
    down_res = adamw_as(
        (0, 1), down_weight, down_grad, down_first, down_second, rate_list[3], scale
    )
    attn_back, down_res = gather_rows(grad_one.astype(jnp.bfloat16), down_res)
    gateup_grad, down_grad = lax.optimization_barrier((gateup_grad, down_grad))
    gateup_grad = with_layout_constraint(
        lax.psum_scatter(gateup_grad, "dp", scatter_dimension=2, tiled=True),
        Layout(major_to_minor=(0, 1, 2)),
    )
    grad_attended = jnp.einsum(
        "td,de->te", attn_back, out_full, preferred_element_type=jnp.bfloat16
    )
    grad_proj = attend_backward(seq_info, *kept, grad_attended, cosine, sine)
    attended, grad_proj = lax.optimization_barrier((attended, grad_proj))
    attend_grad = jnp.concatenate(
        [
            jnp.einsum("te,td->ed", left, right, preferred_element_type=jnp.bfloat16)
            for left, right in ((attended, attn_back), (grad_proj, inputs))
        ],
        0,
    )
    grad_proj, attend_grad = lax.optimization_barrier((grad_proj, attend_grad))
    attend_grad, gateup_grad = lax.optimization_barrier((attend_grad, gateup_grad))
    attend_grad = lax.psum_scatter(attend_grad, "dp", scatter_dimension=1, tiled=True)
    gateup_res = adamw_as(
        (2, 1, 0),
        gateup_weight,
        gateup_grad.transpose(1, 0, 2),
        gateup_first,
        gateup_second,
        rate_list[2],
        scale,
    )
    input_raw, gateup_res = scatter_rows(
        far_first(
            grad_proj,
            lambda rows: jnp.einsum(
                "te,de->td", rows, qkv_full, preferred_element_type=jnp.bfloat16
            ),
            two_pieces,
        ),
        gateup_res,
    )
    input_raw = input_raw + deep_alpha * grad_one
    norm_grad = jnp.stack([gain_one, bias_one, gain_two, bias_two], 0)
    norm_grad, input_raw = lax.optimization_barrier((norm_grad, input_raw))
    norm_grad = sum_everywhere(norm_grad)
    out_grad = attend_grad[:local_dim]
    qkv_grad = attend_grad[local_dim:].reshape(3, local_dim, shard_rows)
    qkv_res = adamw_as(
        (1, 0, 2), qkv_weight, qkv_grad.transpose(0, 2, 1), qkv_first, qkv_second, rate_list[0], scale
    )
    out_res = adamw_as((0, 1), out_weight, out_grad, out_first, out_second, rate_list[1], scale)
    norm_res = adamw(norm_params, norm_grad * scale, norm_first, norm_second, rate_list[4])
    return (
        output_rows.astype(jnp.bfloat16),
        input_raw * scale,
        qkv_res[0],
        qkv_res[1],
        qkv_res[2],
        out_res[0],
        out_res[1],
        out_res[2],
        gateup_res[0],
        gateup_res[1],
        gateup_res[2],
        down_res[0],
        down_res[1],
        down_res[2],
        norm_res[0],
        norm_res[1],
        norm_res[2],
    )


def solution(mesh):
    return jax.shard_map(
        local,
        mesh=mesh,
        in_specs=(
            P(("dp", "mp"), None),
            P(("dp", "mp"), None),
            P("dp"),
            P("dp"),
            P(("dp", "mp")),
            P("dp", None, "mp"),
            P("mp", "dp"),
            P("dp", None, "mp"),
            P("mp", "dp"),
            P(),
            P("dp", None, "mp"),
            P("mp", "dp"),
            P("dp", None, "mp"),
            P("mp", "dp"),
            P(),
            P("dp", None, "mp"),
            P("mp", "dp"),
            P("dp", None, "mp"),
            P("mp", "dp"),
            P(),
        ),
        out_specs=(
            P(("dp", "mp"), None),
            P(("dp", "mp"), None),
            P("dp", None, "mp"),
            P("dp", None, "mp"),
            P("dp", None, "mp"),
            P("mp", "dp"),
            P("mp", "dp"),
            P("mp", "dp"),
            P("dp", None, "mp"),
            P("dp", None, "mp"),
            P("dp", None, "mp"),
            P("mp", "dp"),
            P("mp", "dp"),
            P("mp", "dp"),
            P(),
            P(),
            P(),
        ),
        check_vma=False,
    )
```

```python
import jax
import jax.numpy as jnp
from jax import lax
from jax.experimental import pallas as pl
from jax.experimental.layout import Layout, with_layout_constraint
from jax.experimental.pallas import tpu as pltpu
from jax.sharding import PartitionSpec as P

D = 2048
HD = 128
FF = 5461
FF_PAD = 5472
STEP = 5


deep_alpha = 48.0**0.5
norm_eps = 1e-05
masked_score = -1e30
rope_base = 10000.0
beta_one = 0.5
beta_two = 0.5
adam_eps = 1e-08
decay_rate = 0.1


def rope_tables(position, head_dim):
    freqs = rope_base ** (-jnp.arange(0, head_dim, 2, dtype=jnp.float32) / head_dim)
    angles = position.astype(jnp.float32)[:, None] * freqs[None, :]
    cosine, sine = jnp.cos(angles), jnp.sin(angles)
    return (jnp.concatenate([cosine, cosine], -1), jnp.concatenate([-sine, sine], -1))


def turn(values, cosine, sine):
    return values * cosine + pltpu.roll(values, HD // 2, 1) * sine


def dot_nt(left, right):
    return lax.dot_general(
        left, right, (((1,), (1,)), ((), ())), preferred_element_type=jnp.float32
    )


def dot_nn(left, right):
    return lax.dot_general(
        left, right, (((1,), (0,)), ((), ())), preferred_element_type=jnp.float32
    )


def dot_tn(left, right):
    return lax.dot_general(
        left, right, (((0,), (0,)), ((), ())), preferred_element_type=jnp.float32
    )


def soft_rows(objective_ref, prefix_ref, place_ref, query, key):
    seq_len = query.shape[0]
    seq, flip = pl.program_id(0) ^ place_ref[0], place_ref[1]
    row_at = lax.broadcasted_iota(jnp.int32, (seq_len, seq_len), 0) ^ flip
    col_at = lax.broadcasted_iota(jnp.int32, (seq_len, seq_len), 1) ^ flip
    bound = jnp.where(objective_ref[seq] > 0, seq_len, prefix_ref[seq])
    visible = (col_at < bound) | (col_at <= row_at)
    scores = jnp.where(visible, dot_nt(query, key) * HD ** (-0.5), masked_score)
    exp_scores = jnp.exp(scores - jnp.max(scores, -1, keepdims=True))
    return exp_scores / jnp.sum(exp_scores, -1, keepdims=True)


def attend_kernel(
    objective_ref,
    prefix_ref,
    place_ref,
    proj_ref,
    cos_ref,
    sin_ref,
    query_ref,
    key_ref,
    value_ref,
    out_ref,
):
    local_dim = out_ref.shape[1]
    cosine, sine = cos_ref[...], sin_ref[...]
    for start in range(0, local_dim, HD):
        cols = slice(start, start + HD)
        query = turn(proj_ref[:, start : start + HD], cosine, sine).astype(jnp.bfloat16)
        key_at = local_dim + start
        key = turn(proj_ref[:, key_at : key_at + HD], cosine, sine).astype(jnp.bfloat16)
        value_at = 2 * local_dim + start
        value = proj_ref[:, value_at : value_at + HD].astype(jnp.bfloat16)
        soft = soft_rows(objective_ref, prefix_ref, place_ref, query, key)
        query_ref[:, cols] = query
        key_ref[:, cols] = key
        value_ref[:, cols] = value
        out_ref[:, cols] = dot_nn(soft.astype(jnp.bfloat16), value).astype(jnp.bfloat16)


def attend_back_kernel(
    objective_ref,
    prefix_ref,
    place_ref,
    query_ref,
    key_ref,
    value_ref,
    grad_ref,
    cos_ref,
    sin_ref,
    out_ref,
):
    local_dim = grad_ref.shape[1]
    cosine, sine = cos_ref[...], sin_ref[...]
    scale = HD ** (-0.5)
    for start in range(0, local_dim, HD):
        cols = slice(start, start + HD)
        query, key, value = query_ref[:, cols], key_ref[:, cols], value_ref[:, cols]
        grad = grad_ref[:, cols]
        soft = soft_rows(objective_ref, prefix_ref, place_ref, query, key)
        grad_soft = dot_nt(grad, value)
        row_dot = jnp.sum(soft * grad_soft, -1, keepdims=True)
        grad_scores = (soft * (grad_soft - row_dot)).astype(jnp.bfloat16)
        value_grad = dot_tn(soft.astype(jnp.bfloat16), grad)
        query_grad = turn(dot_nn(grad_scores, key) * scale, cosine, -sine)
        key_grad = turn(dot_tn(grad_scores, query) * scale, cosine, -sine)
        for index, rows in enumerate((query_grad, key_grad, value_grad)):
            at = index * local_dim + start
            out_ref[:, at : at + HD] = rows.astype(jnp.bfloat16)


def seq_specs(seq_len, widths):
    scalars = pl.BlockSpec(memory_space=pltpu.SMEM)
    table = pl.BlockSpec((seq_len, HD), lambda seq: (0, 0))
    rows = [pl.BlockSpec((seq_len, width), lambda seq: (seq, 0)) for width in widths]
    return [scalars] * 3 + rows + [table] * 2


def attend_forward(seq_info, proj, cosine, sine):
    seq_len, (rows, width) = cosine.shape[0], proj.shape
    local_dim = width // 3
    low = jax.ShapeDtypeStruct((rows, local_dim), jnp.bfloat16)
    block = pl.BlockSpec((seq_len, local_dim), lambda seq: (seq, 0))
    return pl.pallas_call(
        attend_kernel,
        grid=(rows // seq_len,),
        out_shape=(low,) * 4,
        in_specs=seq_specs(seq_len, (width,)),
        out_specs=(block,) * 4,
        name="attend_forward",
    )(*seq_info, proj, cosine, sine)


def attend_backward(seq_info, query, key, value, grad, cosine, sine):
    seq_len, (rows, local_dim) = cosine.shape[0], query.shape
    return pl.pallas_call(
        attend_back_kernel,
        grid=(rows // seq_len,),
        out_shape=jax.ShapeDtypeStruct((rows, 3 * local_dim), jnp.bfloat16),
        in_specs=seq_specs(seq_len, (local_dim,) * 4),
        out_specs=pl.BlockSpec((seq_len, 3 * local_dim), lambda seq: (seq, 0)),
        name="attend_backward",
    )(*seq_info, query, key, value, grad, cosine, sine)


def norm_forward(hidden, norm_gain, norm_bias):
    row_mean = jnp.mean(hidden, -1, keepdims=True)
    centred = hidden - row_mean
    variance = jnp.mean(centred * centred, -1, keepdims=True)
    inv_std = lax.rsqrt(variance + norm_eps)
    normed = centred * inv_std
    return (normed * norm_gain + norm_bias, normed, inv_std)


def norm_backward(grad_rows, normed, inv_std, norm_gain):
    grad_normed = grad_rows * norm_gain
    mean_grad = jnp.mean(grad_normed, -1, keepdims=True)
    mean_proj = jnp.mean(grad_normed * normed, -1, keepdims=True)
    grad_in = inv_std * (grad_normed - mean_grad - normed * mean_proj)
    return (grad_in, jnp.sum(grad_rows * normed, 0), jnp.sum(grad_rows, 0))


def adamw(weight, gradient, first_moment, second, step_rate):
    first_new = beta_one * first_moment + (1.0 - beta_one) * gradient
    second_new = beta_two * second + (1.0 - beta_two) * gradient * gradient
    first_hat = first_new / (1.0 - beta_one**STEP)
    second_hat = second_new / (1.0 - beta_two**STEP)
    weight_new = weight - step_rate * (
        first_hat / (jnp.sqrt(second_hat) + adam_eps) + decay_rate * weight
    )
    return (weight_new, first_new, second_new)


def swap(values, axis, bit):
    size = lax.axis_size(axis)
    return lax.ppermute(values, axis, [(at, at ^ bit) for at in range(size)])


def sum_everywhere(values):
    for axis in ("mp", "dp"):
        bit = 1
        while bit < lax.axis_size(axis):
            values = values + swap(values, axis, bit)
            bit *= 2
    return values


def gather_near(rows, ahead=None):
    half = rows.shape[0] // 2
    near_x, near_y = swap(rows, "mp", 2), swap(rows, "mp", 4)
    if ahead is not None:
        near_x, near_y, ahead = lax.optimization_barrier((near_x, near_y, ahead))
    far_low, far_high = swap(near_x[:half], "mp", 4), swap(near_y[half:], "mp", 2)
    mates = [swap(part, "mp", 1) for part in (rows, near_x, near_y, far_low, far_high)]
    whole = jnp.concatenate(
        [rows, mates[0], near_x, mates[1], near_y, mates[2], far_low, far_high, mates[3], mates[4]],
        0,
    )
    return whole if ahead is None else (whole, ahead)


def far_first(rows, product, quarters):
    size = rows.shape[0] // 4
    pieces = []
    for first, last in quarters:
        if pieces:
            rows, pieces[0] = lax.optimization_barrier((rows, pieces[0]))
        pieces.insert(0, product(rows[first * size : last * size]))
    return pieces


def scatter_near(pieces, ahead=None):
    blocks = []
    own_rows = sum(piece.shape[0] for piece in pieces) // 8
    half = own_rows // 2
    for piece in pieces:
        blocks += [
            piece[at : at + own_rows] for at in range(0, piece.shape[0], own_rows)
        ]
    sums = [
        blocks[at].astype(jnp.float32) + swap(blocks[at + 1], "mp", 1).astype(jnp.float32)
        for at in range(0, 8, 2)
    ]
    far = sums[3].astype(jnp.bfloat16)
    far_low, far_high = swap(far[:half], "mp", 4), swap(far[half:], "mp", 2)
    if ahead is not None:
        far_low, far_high, ahead = lax.optimization_barrier((far_low, far_high, ahead))
    x_low = (sums[1][:half] + far_low.astype(jnp.float32)).astype(jnp.bfloat16)
    y_high = (sums[2][half:] + far_high.astype(jnp.float32)).astype(jnp.bfloat16)
    x_high, y_low = sums[1][half:].astype(jnp.bfloat16), sums[2][:half].astype(jnp.bfloat16)
    x_low, x_high = swap(x_low, "mp", 2), swap(x_high, "mp", 2)
    y_low, y_high = swap(y_low, "mp", 4), swap(y_high, "mp", 4)
    across_x = jnp.concatenate([x_low, x_high], 0).astype(jnp.float32)
    across_y = jnp.concatenate([y_low, y_high], 0).astype(jnp.float32)
    total = sums[0] + across_x + across_y
    return total if ahead is None else (total, ahead)


def core_sum(piece):
    half = piece.shape[0] // 2
    mate = swap(piece[half:], "mp", 1)
    return piece[:half].astype(jnp.float32) + mate.astype(jnp.float32)


def scatter_beside(own, near_x, rows, product, last):
    far = product(rows, 3)
    rows, far = lax.optimization_barrier((rows, far))
    far = core_sum(far).astype(jnp.bfloat16)
    own, near_x = core_sum(own), core_sum(near_x)
    rows, far, own, near_x = lax.optimization_barrier((rows, far, own, near_x))
    half = far.shape[0] // 2
    far_low, far_high = swap(far[:half], "mp", 4), swap(far[half:], "mp", 2)
    near_y, far_low, far_high = lax.optimization_barrier((product(rows, 2), far_low, far_high))
    near_y = core_sum(near_y)
    low, high = slice(0, half), slice(half, 2 * half)
    x_low = (near_x[low] + far_low.astype(jnp.float32)).astype(jnp.bfloat16)
    y_high = (near_y[high] + far_high.astype(jnp.float32)).astype(jnp.bfloat16)
    x_high, y_low = near_x[high].astype(jnp.bfloat16), near_y[low].astype(jnp.bfloat16)
    across = [swap(x_low, "mp", 2), swap(x_high, "mp", 2), swap(y_low, "mp", 4), swap(y_high, "mp", 4)]
    across, ahead = lax.optimization_barrier((across, last()))
    across_x, across_y = jnp.concatenate(across[:2], 0), jnp.concatenate(across[2:], 0)
    return own + across_x.astype(jnp.float32) + across_y.astype(jnp.float32), ahead


def gather_beside(rows, product):
    half = rows.shape[0] // 2
    near_x, near_y, mate = swap(rows, "mp", 2), swap(rows, "mp", 4), swap(rows, "mp", 1)
    own = product(jnp.concatenate([rows, mate], 0), 0)
    near_x, near_y, own = lax.optimization_barrier((near_x, near_y, own))
    far_low, far_high = swap(near_x[:half], "mp", 4), swap(near_y[half:], "mp", 2)
    mate_x, mate_y = swap(near_x, "mp", 1), swap(near_y, "mp", 1)
    across_x = product(jnp.concatenate([near_x, mate_x], 0), 1)
    far_low, far_high, across_x = lax.optimization_barrier((far_low, far_high, across_x))
    mates = [swap(far_low, "mp", 1), swap(far_high, "mp", 1)]
    whole = jnp.concatenate(
        [rows, mate, near_x, mate_x, near_y, mate_y, far_low, far_high, *mates], 0
    )
    return whole, own, across_x


def gather_all(rows, ahead=None):
    whole = lax.all_gather(rows, "mp", axis=0, tiled=True)
    return whole if ahead is None else (whole, ahead)


def scatter_all(pieces, ahead=None):
    whole = jnp.concatenate(pieces, 0)
    total = lax.psum_scatter(whole, "mp", scatter_dimension=0, tiled=True).astype(jnp.float32)
    return total if ahead is None else (total, ahead)


def adamw_as(order, weight, gradient, first_moment, second, step_rate, scale):
    turned = [jnp.transpose(rows, order) for rows in (weight, first_moment, second)]
    rank = len(order)
    gradient = with_layout_constraint(gradient, Layout(major_to_minor=tuple(range(rank))))
    gradient = gradient.astype(jnp.float32) * scale
    news = adamw(turned[0], gradient, turned[1], turned[2], step_rate)
    back = tuple(order.index(dim) for dim in range(rank))
    stored = Layout(major_to_minor=order)
    return tuple(with_layout_constraint(jnp.transpose(rows, back), stored) for rows in news)


def local(
    block_input,
    out_cotangent,
    objective,
    prefix_len,
    target_mask,
    qkv_weight,
    out_weight,
    gateup_weight,
    down_weight,
    norm_params,
    qkv_first,
    out_first,
    gateup_first,
    down_first,
    norm_first,
    qkv_second,
    out_second,
    gateup_second,
    down_second,
    norm_second,
):
    mp_index = lax.axis_index("mp")
    own_rows = block_input.shape[0]
    seq_count = objective.shape[0]
    seq_len = own_rows * lax.axis_size("mp") // seq_count
    shard_rows, _, local_dim = qkv_weight.shape
    local_units = gateup_weight.shape[2]
    near = lax.axis_size("mp") == 8 and seq_count == 4 and own_rows % 32 == 0
    if near:
        gather_rows, scatter_rows = gather_near, scatter_near
        place = jnp.stack([mp_index // 2, (mp_index % 2) * own_rows]).astype(jnp.int32)
    else:
        gather_rows, scatter_rows = gather_all, scatter_all
        place = jnp.zeros((2,), jnp.int32)
    two_pieces = ((3, 4), (0, 3))
    seq_info = (objective, prefix_len, place)
    cosine, sine = rope_tables(jnp.arange(seq_len, dtype=jnp.int32) ^ place[1], HD)

    qkv_low = qkv_weight.astype(jnp.bfloat16).reshape(shard_rows, 3 * local_dim)
    attend_low = jnp.concatenate([qkv_low, out_weight.T.astype(jnp.bfloat16)], 1)
    attend_full = lax.all_gather(attend_low, "dp", axis=0, tiled=True)
    qkv_full, out_full = attend_full[:, : 3 * local_dim], attend_full[:, 3 * local_dim :]
    gateup_low = with_layout_constraint(
        jnp.transpose(gateup_weight, (1, 2, 0)).astype(jnp.bfloat16),
        Layout(major_to_minor=(0, 1, 2)),
    )
    gateup_full = lax.all_gather(gateup_low, "dp", axis=2, tiled=True)
    down_full = lax.all_gather(down_weight.astype(jnp.bfloat16), "dp", axis=1, tiled=True)

    mask_f32 = target_mask.astype(jnp.float32)
    target_count = sum_everywhere(jnp.full((8, 128), jnp.sum(mask_f32)))[0, 0]

    cosine, target_count = lax.optimization_barrier((cosine, target_count))

    inputs = gather_rows(block_input)
    proj = jnp.dot(inputs, qkv_full, preferred_element_type=jnp.float32)
    *kept, attended = attend_forward(seq_info, proj, cosine, sine)
    attn_own = scatter_rows(
        far_first(
            attended,
            lambda rows: jnp.einsum(
                "te,de->td", rows, out_full, preferred_element_type=jnp.bfloat16
            ),
            two_pieces,
        )
    )
    hidden_one = deep_alpha * block_input.astype(jnp.float32) + attn_own
    middle, normed_one, inv_one = norm_forward(hidden_one, norm_params[0], norm_params[1])
    middle_low = gather_rows(middle.astype(jnp.bfloat16))

    live_units = (mp_index * local_units + jnp.arange(local_units) < FF).astype(jnp.float32)
    gate_up = jnp.einsum(
        "td,cfd->ctf", middle_low, gateup_full, preferred_element_type=jnp.float32
    )
    hidden_low = (jax.nn.gelu(gate_up[0]) * gate_up[1] * live_units).astype(jnp.bfloat16)
    ffn_own = scatter_rows(
        far_first(
            hidden_low,
            lambda rows: jnp.dot(rows, down_full, preferred_element_type=jnp.bfloat16),
            two_pieces,
        )
    )
    quarter = hidden_low.shape[0] // 4
    hidden_two = deep_alpha * middle + ffn_own
    output_rows, normed_two, inv_two = norm_forward(hidden_two, norm_params[2], norm_params[3])
    grad_rows = out_cotangent.astype(jnp.float32) * mask_f32[:, None]
    grad_two, gain_two, bias_two = norm_backward(grad_rows, normed_two, inv_two, norm_params[2])

    grad_gateups = [None] * 4

    def back_quarter(chunk, index):
        at = slice(index * quarter, (index + 1) * quarter)
        gate_act, gelu_pull = jax.vjp(jax.nn.gelu, gate_up[0, at])
        grad_hidden = (
            jnp.einsum("td,fd->tf", chunk, down_full, preferred_element_type=jnp.float32)
            * live_units
        )
        grad_gate = gelu_pull(grad_hidden * gate_up[1, at])[0]
        grads = jnp.stack([grad_gate, grad_hidden * gate_act], 0).astype(jnp.bfloat16)
        grad_gateups[index] = grads
        return jnp.einsum("ctf,cfd->td", grads, gateup_full, preferred_element_type=jnp.bfloat16)

    def back_rows(rows, index):
        return back_quarter(rows[index * quarter : (index + 1) * quarter], index)

    back_low = grad_two.astype(jnp.bfloat16)
    if near:
        ffn_back, own_part, x_part = gather_beside(back_low, back_quarter)
    else:
        ffn_back = gather_rows(back_low)
    down_grad = jnp.einsum("tf,td->fd", hidden_low, ffn_back, preferred_element_type=jnp.bfloat16)
    ffn_back, down_grad = lax.optimization_barrier((ffn_back, down_grad))
    down_grad = lax.psum_scatter(down_grad, "dp", scatter_dimension=1, tiled=True)

    def gateup_product():
        return jnp.einsum(
            "ctf,td->cfd",
            jnp.concatenate(grad_gateups, 1),
            middle_low,
            preferred_element_type=jnp.bfloat16,
        )

    if near:
        grad_middle, gateup_grad = scatter_beside(
            own_part, x_part, ffn_back, back_rows, gateup_product
        )
    else:
        grad_middle = scatter_all([back_rows(ffn_back, index) for index in range(4)])
        gateup_grad = gateup_product()
    grad_middle = grad_middle + deep_alpha * grad_two
    grad_one, gain_one, bias_one = norm_backward(grad_middle, normed_one, inv_one, norm_params[0])

    rate_list = (D ** (-0.5), 0.5, D ** (-0.5), (FF_PAD // 64) ** (-0.5), 0.4)
    scale = 1.0 / target_count
    down_res = adamw_as(
        (0, 1), down_weight, down_grad, down_first, down_second, rate_list[3], scale
    )
    attn_back, down_res = gather_rows(grad_one.astype(jnp.bfloat16), down_res)
    gateup_grad, down_grad = lax.optimization_barrier((gateup_grad, down_grad))
    gateup_grad = with_layout_constraint(
        lax.psum_scatter(gateup_grad, "dp", scatter_dimension=2, tiled=True),
        Layout(major_to_minor=(0, 1, 2)),
    )
    grad_attended = jnp.einsum(
        "td,de->te", attn_back, out_full, preferred_element_type=jnp.bfloat16
    )
    grad_proj = attend_backward(seq_info, *kept, grad_attended, cosine, sine)
    attended, grad_proj = lax.optimization_barrier((attended, grad_proj))
    attend_grad = jnp.concatenate(
        [
            jnp.einsum("te,td->ed", left, right, preferred_element_type=jnp.bfloat16)
            for left, right in ((attended, attn_back), (grad_proj, inputs))
        ],
        0,
    )
    grad_proj, attend_grad = lax.optimization_barrier((grad_proj, attend_grad))
    attend_grad, gateup_grad = lax.optimization_barrier((attend_grad, gateup_grad))
    attend_grad = lax.psum_scatter(attend_grad, "dp", scatter_dimension=1, tiled=True)
    gateup_res = adamw_as(
        (2, 1, 0),
        gateup_weight,
        gateup_grad.transpose(1, 0, 2),
        gateup_first,
        gateup_second,
        rate_list[2],
        scale,
    )
    input_raw, gateup_res = scatter_rows(
        far_first(
            grad_proj,
            lambda rows: jnp.einsum(
                "te,de->td", rows, qkv_full, preferred_element_type=jnp.bfloat16
            ),
            two_pieces,
        ),
        gateup_res,
    )
    input_raw = input_raw + deep_alpha * grad_one
    norm_grad = jnp.stack([gain_one, bias_one, gain_two, bias_two], 0)
    norm_grad, input_raw = lax.optimization_barrier((norm_grad, input_raw))
    norm_grad = sum_everywhere(norm_grad)
    out_grad = attend_grad[:local_dim]
    qkv_grad = attend_grad[local_dim:].reshape(3, local_dim, shard_rows)
    qkv_res = adamw_as(
        (1, 0, 2), qkv_weight, qkv_grad.transpose(0, 2, 1), qkv_first, qkv_second, rate_list[0], scale
    )
    out_res = adamw_as((0, 1), out_weight, out_grad, out_first, out_second, rate_list[1], scale)
    norm_res = adamw(norm_params, norm_grad * scale, norm_first, norm_second, rate_list[4])
    return (
        output_rows.astype(jnp.bfloat16),
        input_raw * scale,
        qkv_res[0],
        qkv_res[1],
        qkv_res[2],
        out_res[0],
        out_res[1],
        out_res[2],
        gateup_res[0],
        gateup_res[1],
        gateup_res[2],
        down_res[0],
        down_res[1],
        down_res[2],
        norm_res[0],
        norm_res[1],
        norm_res[2],
    )


def solution(mesh):
    return jax.shard_map(
        local,
        mesh=mesh,
        in_specs=(
            P(("dp", "mp"), None),
            P(("dp", "mp"), None),
            P("dp"),
            P("dp"),
            P(("dp", "mp")),
            P("dp", None, "mp"),
            P("mp", "dp"),
            P("dp", None, "mp"),
            P("mp", "dp"),
            P(),
            P("dp", None, "mp"),
            P("mp", "dp"),
            P("dp", None, "mp"),
            P("mp", "dp"),
            P(),
            P("dp", None, "mp"),
            P("mp", "dp"),
            P("dp", None, "mp"),
            P("mp", "dp"),
            P(),
        ),
        out_specs=(
            P(("dp", "mp"), None),
            P(("dp", "mp"), None),
            P("dp", None, "mp"),
            P("dp", None, "mp"),
            P("dp", None, "mp"),
            P("mp", "dp"),
            P("mp", "dp"),
            P("mp", "dp"),
            P("dp", None, "mp"),
            P("dp", None, "mp"),
            P("dp", None, "mp"),
            P("mp", "dp"),
            P("mp", "dp"),
            P("mp", "dp"),
            P(),
            P(),
            P(),
        ),
        check_vma=False,
    )
```

```python
import jax
import jax.numpy as jnp
from jax import lax
from jax.experimental import pallas as pl
from jax.experimental.layout import Layout, with_layout_constraint
from jax.experimental.pallas import tpu as pltpu
from jax.sharding import PartitionSpec as P

D = 2048
HD = 128
FF = 5461
FF_PAD = 5472
STEP = 5


deep_alpha = 48.0**0.5
norm_eps = 1e-05
masked_score = -1e30
rope_base = 10000.0
beta_one = 0.5
beta_two = 0.5
adam_eps = 1e-08
decay_rate = 0.1


def rope_tables(position, head_dim):
    freqs = rope_base ** (-jnp.arange(0, head_dim, 2, dtype=jnp.float32) / head_dim)
    angles = position.astype(jnp.float32)[:, None] * freqs[None, :]
    cosine, sine = jnp.cos(angles), jnp.sin(angles)
    return (jnp.concatenate([cosine, cosine], -1), jnp.concatenate([-sine, sine], -1))


def turn(values, cosine, sine):
    return values * cosine + pltpu.roll(values, HD // 2, 1) * sine


def dot_nt(left, right):
    return lax.dot_general(
        left, right, (((1,), (1,)), ((), ())), preferred_element_type=jnp.float32
    )


def dot_nn(left, right):
    return lax.dot_general(
        left, right, (((1,), (0,)), ((), ())), preferred_element_type=jnp.float32
    )


def dot_tn(left, right):
    return lax.dot_general(
        left, right, (((0,), (0,)), ((), ())), preferred_element_type=jnp.float32
    )


def soft_rows(objective_ref, prefix_ref, place_ref, query, key):
    seq_len = query.shape[0]
    seq, flip = pl.program_id(0) ^ place_ref[0], place_ref[1]
    row_at = lax.broadcasted_iota(jnp.int32, (seq_len, seq_len), 0) ^ flip
    col_at = lax.broadcasted_iota(jnp.int32, (seq_len, seq_len), 1) ^ flip
    bound = jnp.where(objective_ref[seq] > 0, seq_len, prefix_ref[seq])
    visible = (col_at < bound) | (col_at <= row_at)
    scores = jnp.where(visible, dot_nt(query, key) * HD ** (-0.5), masked_score)
    exp_scores = jnp.exp(scores - jnp.max(scores, -1, keepdims=True))
    return exp_scores / jnp.sum(exp_scores, -1, keepdims=True)


def attend_kernel(
    objective_ref,
    prefix_ref,
    place_ref,
    proj_ref,
    cos_ref,
    sin_ref,
    query_ref,
    key_ref,
    value_ref,
    out_ref,
):
    local_dim = out_ref.shape[1]
    cosine, sine = cos_ref[...], sin_ref[...]
    for start in range(0, local_dim, HD):
        cols = slice(start, start + HD)
        query = turn(proj_ref[:, start : start + HD], cosine, sine).astype(jnp.bfloat16)
        key_at = local_dim + start
        key = turn(proj_ref[:, key_at : key_at + HD], cosine, sine).astype(jnp.bfloat16)
        value_at = 2 * local_dim + start
        value = proj_ref[:, value_at : value_at + HD].astype(jnp.bfloat16)
        soft = soft_rows(objective_ref, prefix_ref, place_ref, query, key)
        query_ref[:, cols] = query
        key_ref[:, cols] = key
        value_ref[:, cols] = value
        out_ref[:, cols] = dot_nn(soft.astype(jnp.bfloat16), value).astype(jnp.bfloat16)


def attend_back_kernel(
    objective_ref,
    prefix_ref,
    place_ref,
    query_ref,
    key_ref,
    value_ref,
    grad_ref,
    cos_ref,
    sin_ref,
    out_ref,
):
    local_dim = grad_ref.shape[1]
    cosine, sine = cos_ref[...], sin_ref[...]
    scale = HD ** (-0.5)
    for start in range(0, local_dim, HD):
        cols = slice(start, start + HD)
        query, key, value = query_ref[:, cols], key_ref[:, cols], value_ref[:, cols]
        grad = grad_ref[:, cols]
        soft = soft_rows(objective_ref, prefix_ref, place_ref, query, key)
        grad_soft = dot_nt(grad, value)
        row_dot = jnp.sum(soft * grad_soft, -1, keepdims=True)
        grad_scores = (soft * (grad_soft - row_dot)).astype(jnp.bfloat16)
        value_grad = dot_tn(soft.astype(jnp.bfloat16), grad)
        query_grad = turn(dot_nn(grad_scores, key) * scale, cosine, -sine)
        key_grad = turn(dot_tn(grad_scores, query) * scale, cosine, -sine)
        for index, rows in enumerate((query_grad, key_grad, value_grad)):
            at = index * local_dim + start
            out_ref[:, at : at + HD] = rows.astype(jnp.bfloat16)


def seq_specs(seq_len, widths):
    scalars = pl.BlockSpec(memory_space=pltpu.SMEM)
    table = pl.BlockSpec((seq_len, HD), lambda seq: (0, 0))
    rows = [pl.BlockSpec((seq_len, width), lambda seq: (seq, 0)) for width in widths]
    return [scalars] * 3 + rows + [table] * 2


def attend_forward(seq_info, proj, cosine, sine):
    seq_len, (rows, width) = cosine.shape[0], proj.shape
    local_dim = width // 3
    low = jax.ShapeDtypeStruct((rows, local_dim), jnp.bfloat16)
    block = pl.BlockSpec((seq_len, local_dim), lambda seq: (seq, 0))
    return pl.pallas_call(
        attend_kernel,
        grid=(rows // seq_len,),
        out_shape=(low,) * 4,
        in_specs=seq_specs(seq_len, (width,)),
        out_specs=(block,) * 4,
        name="attend_forward",
    )(*seq_info, proj, cosine, sine)


def attend_backward(seq_info, query, key, value, grad, cosine, sine):
    seq_len, (rows, local_dim) = cosine.shape[0], query.shape
    return pl.pallas_call(
        attend_back_kernel,
        grid=(rows // seq_len,),
        out_shape=jax.ShapeDtypeStruct((rows, 3 * local_dim), jnp.bfloat16),
        in_specs=seq_specs(seq_len, (local_dim,) * 4),
        out_specs=pl.BlockSpec((seq_len, 3 * local_dim), lambda seq: (seq, 0)),
        name="attend_backward",
    )(*seq_info, query, key, value, grad, cosine, sine)


def norm_forward(hidden, norm_gain, norm_bias):
    row_mean = jnp.mean(hidden, -1, keepdims=True)
    centred = hidden - row_mean
    variance = jnp.mean(centred * centred, -1, keepdims=True)
    inv_std = lax.rsqrt(variance + norm_eps)
    normed = centred * inv_std
    return (normed * norm_gain + norm_bias, normed, inv_std)


def norm_backward(grad_rows, normed, inv_std, norm_gain):
    grad_normed = grad_rows * norm_gain
    mean_grad = jnp.mean(grad_normed, -1, keepdims=True)
    mean_proj = jnp.mean(grad_normed * normed, -1, keepdims=True)
    grad_in = inv_std * (grad_normed - mean_grad - normed * mean_proj)
    return (grad_in, jnp.sum(grad_rows * normed, 0), jnp.sum(grad_rows, 0))


def adamw(weight, gradient, first_moment, second, step_rate):
    first_new = beta_one * first_moment + (1.0 - beta_one) * gradient
    second_new = beta_two * second + (1.0 - beta_two) * gradient * gradient
    first_hat = first_new / (1.0 - beta_one**STEP)
    second_hat = second_new / (1.0 - beta_two**STEP)
    weight_new = weight - step_rate * (
        first_hat / (jnp.sqrt(second_hat) + adam_eps) + decay_rate * weight
    )
    return (weight_new, first_new, second_new)


def swap(values, axis, bit):
    size = lax.axis_size(axis)
    return lax.ppermute(values, axis, [(at, at ^ bit) for at in range(size)])


def sum_everywhere(values):
    for axis in ("mp", "dp"):
        bit = 1
        while bit < lax.axis_size(axis):
            values = values + swap(values, axis, bit)
            bit *= 2
    return values


def gather_near(rows, ahead=None):
    half = rows.shape[0] // 2
    near_x, near_y = swap(rows, "mp", 2), swap(rows, "mp", 4)
    if ahead is not None:
        near_x, near_y, ahead = lax.optimization_barrier((near_x, near_y, ahead))
    far_low, far_high = swap(near_x[:half], "mp", 4), swap(near_y[half:], "mp", 2)
    mates = [swap(part, "mp", 1) for part in (rows, near_x, near_y, far_low, far_high)]
    whole = jnp.concatenate(
        [rows, mates[0], near_x, mates[1], near_y, mates[2], far_low, far_high, mates[3], mates[4]],
        0,
    )
    return whole if ahead is None else (whole, ahead)


def far_first(rows, product, quarters):
    size = rows.shape[0] // 4
    pieces = []
    for first, last in quarters:
        if pieces:
            rows, pieces[0] = lax.optimization_barrier((rows, pieces[0]))
        pieces.insert(0, product(rows[first * size : last * size]))
    return pieces


def scatter_near(pieces, ahead=None):
    blocks = []
    own_rows = sum(piece.shape[0] for piece in pieces) // 8
    half = own_rows // 2
    for piece in pieces:
        blocks += [
            piece[at : at + own_rows] for at in range(0, piece.shape[0], own_rows)
        ]
    sums = [
        blocks[at].astype(jnp.float32) + swap(blocks[at + 1], "mp", 1).astype(jnp.float32)
        for at in range(0, 8, 2)
    ]
    far = sums[3].astype(jnp.bfloat16)
    far_low, far_high = swap(far[:half], "mp", 4), swap(far[half:], "mp", 2)
    if ahead is not None:
        far_low, far_high, ahead = lax.optimization_barrier((far_low, far_high, ahead))
    x_low = (sums[1][:half] + far_low.astype(jnp.float32)).astype(jnp.bfloat16)
    y_high = (sums[2][half:] + far_high.astype(jnp.float32)).astype(jnp.bfloat16)
    x_high, y_low = sums[1][half:].astype(jnp.bfloat16), sums[2][:half].astype(jnp.bfloat16)
    x_low, x_high = swap(x_low, "mp", 2), swap(x_high, "mp", 2)
    y_low, y_high = swap(y_low, "mp", 4), swap(y_high, "mp", 4)
    across_x = jnp.concatenate([x_low, x_high], 0).astype(jnp.float32)
    across_y = jnp.concatenate([y_low, y_high], 0).astype(jnp.float32)
    total = sums[0] + across_x + across_y
    return total if ahead is None else (total, ahead)


def core_sum(piece):
    half = piece.shape[0] // 2
    mate = swap(piece[half:], "mp", 1)
    return piece[:half].astype(jnp.float32) + mate.astype(jnp.float32)


def scatter_beside(own, near_x, rows, product, last):
    own, near_x = core_sum(own), core_sum(near_x)
    rows, own, near_x = lax.optimization_barrier((rows, own, near_x))
    far = core_sum(product(rows, 3)).astype(jnp.bfloat16)
    rows, far = lax.optimization_barrier((rows, far))
    half = far.shape[0] // 2
    far_low, far_high = swap(far[:half], "mp", 4), swap(far[half:], "mp", 2)
    near_y, far_low, far_high = lax.optimization_barrier((product(rows, 2), far_low, far_high))
    near_y = core_sum(near_y)
    low, high = slice(0, half), slice(half, 2 * half)
    x_low = (near_x[low] + far_low.astype(jnp.float32)).astype(jnp.bfloat16)
    y_high = (near_y[high] + far_high.astype(jnp.float32)).astype(jnp.bfloat16)
    x_high, y_low = near_x[high].astype(jnp.bfloat16), near_y[low].astype(jnp.bfloat16)
    across = [swap(x_low, "mp", 2), swap(x_high, "mp", 2), swap(y_low, "mp", 4), swap(y_high, "mp", 4)]
    across, ahead = lax.optimization_barrier((across, last()))
    across_x, across_y = jnp.concatenate(across[:2], 0), jnp.concatenate(across[2:], 0)
    return own + across_x.astype(jnp.float32) + across_y.astype(jnp.float32), ahead


def gather_beside(rows, product):
    half = rows.shape[0] // 2
    near_x, near_y, mate = swap(rows, "mp", 2), swap(rows, "mp", 4), swap(rows, "mp", 1)
    own = product(jnp.concatenate([rows, mate], 0), 0)
    near_x, near_y, own = lax.optimization_barrier((near_x, near_y, own))
    far_low, far_high = swap(near_x[:half], "mp", 4), swap(near_y[half:], "mp", 2)
    mate_x, mate_y = swap(near_x, "mp", 1), swap(near_y, "mp", 1)
    across_x = product(jnp.concatenate([near_x, mate_x], 0), 1)
    far_low, far_high, across_x = lax.optimization_barrier((far_low, far_high, across_x))
    mates = [swap(far_low, "mp", 1), swap(far_high, "mp", 1)]
    whole = jnp.concatenate(
        [rows, mate, near_x, mate_x, near_y, mate_y, far_low, far_high, *mates], 0
    )
    return whole, own, across_x


def gather_all(rows, ahead=None):
    whole = lax.all_gather(rows, "mp", axis=0, tiled=True)
    return whole if ahead is None else (whole, ahead)


def scatter_all(pieces, ahead=None):
    whole = jnp.concatenate(pieces, 0)
    total = lax.psum_scatter(whole, "mp", scatter_dimension=0, tiled=True).astype(jnp.float32)
    return total if ahead is None else (total, ahead)


def adamw_as(order, weight, gradient, first_moment, second, step_rate, scale):
    turned = [jnp.transpose(rows, order) for rows in (weight, first_moment, second)]
    rank = len(order)
    gradient = with_layout_constraint(gradient, Layout(major_to_minor=tuple(range(rank))))
    gradient = gradient.astype(jnp.float32) * scale
    news = adamw(turned[0], gradient, turned[1], turned[2], step_rate)
    back = tuple(order.index(dim) for dim in range(rank))
    stored = Layout(major_to_minor=order)
    return tuple(with_layout_constraint(jnp.transpose(rows, back), stored) for rows in news)


def local(
    block_input,
    out_cotangent,
    objective,
    prefix_len,
    target_mask,
    qkv_weight,
    out_weight,
    gateup_weight,
    down_weight,
    norm_params,
    qkv_first,
    out_first,
    gateup_first,
    down_first,
    norm_first,
    qkv_second,
    out_second,
    gateup_second,
    down_second,
    norm_second,
):
    mp_index = lax.axis_index("mp")
    own_rows = block_input.shape[0]
    seq_count = objective.shape[0]
    seq_len = own_rows * lax.axis_size("mp") // seq_count
    shard_rows, _, local_dim = qkv_weight.shape
    local_units = gateup_weight.shape[2]
    near = lax.axis_size("mp") == 8 and seq_count == 4 and own_rows % 32 == 0
    if near:
        gather_rows, scatter_rows = gather_near, scatter_near
        place = jnp.stack([mp_index // 2, (mp_index % 2) * own_rows]).astype(jnp.int32)
    else:
        gather_rows, scatter_rows = gather_all, scatter_all
        place = jnp.zeros((2,), jnp.int32)
    two_pieces = ((3, 4), (0, 3))
    seq_info = (objective, prefix_len, place)
    cosine, sine = rope_tables(jnp.arange(seq_len, dtype=jnp.int32) ^ place[1], HD)

    qkv_low = qkv_weight.astype(jnp.bfloat16).reshape(shard_rows, 3 * local_dim)
    attend_low = jnp.concatenate([qkv_low, out_weight.T.astype(jnp.bfloat16)], 1)
    attend_full = lax.all_gather(attend_low, "dp", axis=0, tiled=True)
    qkv_full, out_full = attend_full[:, : 3 * local_dim], attend_full[:, 3 * local_dim :]
    gateup_low = with_layout_constraint(
        jnp.transpose(gateup_weight, (1, 2, 0)).astype(jnp.bfloat16),
        Layout(major_to_minor=(0, 1, 2)),
    )
    gateup_full = lax.all_gather(gateup_low, "dp", axis=2, tiled=True)
    down_full = lax.all_gather(down_weight.astype(jnp.bfloat16), "dp", axis=1, tiled=True)

    mask_f32 = target_mask.astype(jnp.float32)
    target_count = sum_everywhere(jnp.full((8, 128), jnp.sum(mask_f32)))[0, 0]

    cosine, target_count = lax.optimization_barrier((cosine, target_count))

    inputs = gather_rows(block_input)
    proj = jnp.dot(inputs, qkv_full, preferred_element_type=jnp.float32)
    *kept, attended = attend_forward(seq_info, proj, cosine, sine)
    attn_own = scatter_rows(
        far_first(
            attended,
            lambda rows: jnp.einsum(
                "te,de->td", rows, out_full, preferred_element_type=jnp.bfloat16
            ),
            two_pieces,
        )
    )
    hidden_one = deep_alpha * block_input.astype(jnp.float32) + attn_own
    middle, normed_one, inv_one = norm_forward(hidden_one, norm_params[0], norm_params[1])
    middle_low = gather_rows(middle.astype(jnp.bfloat16))

    live_units = (mp_index * local_units + jnp.arange(local_units) < FF).astype(jnp.float32)
    gate_up = jnp.einsum(
        "td,cfd->ctf", middle_low, gateup_full, preferred_element_type=jnp.float32
    )
    hidden_low = (jax.nn.gelu(gate_up[0]) * gate_up[1] * live_units).astype(jnp.bfloat16)
    ffn_own = scatter_rows(
        far_first(
            hidden_low,
            lambda rows: jnp.dot(rows, down_full, preferred_element_type=jnp.bfloat16),
            two_pieces,
        )
    )
    quarter = hidden_low.shape[0] // 4
    hidden_two = deep_alpha * middle + ffn_own
    output_rows, normed_two, inv_two = norm_forward(hidden_two, norm_params[2], norm_params[3])
    grad_rows = out_cotangent.astype(jnp.float32) * mask_f32[:, None]
    grad_two, gain_two, bias_two = norm_backward(grad_rows, normed_two, inv_two, norm_params[2])

    grad_gateups = [None] * 4

    def back_quarter(chunk, index):
        at = slice(index * quarter, (index + 1) * quarter)
        gate_act, gelu_pull = jax.vjp(jax.nn.gelu, gate_up[0, at])
        grad_hidden = (
            jnp.einsum("td,fd->tf", chunk, down_full, preferred_element_type=jnp.float32)
            * live_units
        )
        grad_gate = gelu_pull(grad_hidden * gate_up[1, at])[0]
        grads = jnp.stack([grad_gate, grad_hidden * gate_act], 0).astype(jnp.bfloat16)
        grad_gateups[index] = grads
        return jnp.einsum("ctf,cfd->td", grads, gateup_full, preferred_element_type=jnp.bfloat16)

    def back_rows(rows, index):
        return back_quarter(rows[index * quarter : (index + 1) * quarter], index)

    back_low = grad_two.astype(jnp.bfloat16)
    if near:
        ffn_back, own_part, x_part = gather_beside(back_low, back_quarter)
    else:
        ffn_back = gather_rows(back_low)
    down_grad = jnp.einsum("tf,td->fd", hidden_low, ffn_back, preferred_element_type=jnp.bfloat16)
    ffn_back, down_grad = lax.optimization_barrier((ffn_back, down_grad))
    down_grad = lax.psum_scatter(down_grad, "dp", scatter_dimension=1, tiled=True)

    middle_low, down_grad = lax.optimization_barrier((middle_low, down_grad))

    def gateup_product():
        return jnp.einsum(
            "ctf,td->cfd",
            jnp.concatenate(grad_gateups, 1),
            middle_low,
            preferred_element_type=jnp.bfloat16,
        )

    if near:
        grad_middle, gateup_grad = scatter_beside(
            own_part, x_part, ffn_back, back_rows, gateup_product
        )
    else:
        grad_middle = scatter_all([back_rows(ffn_back, index) for index in range(4)])
        gateup_grad = gateup_product()
    grad_middle = grad_middle + deep_alpha * grad_two
    grad_one, gain_one, bias_one = norm_backward(grad_middle, normed_one, inv_one, norm_params[0])

    rate_list = (D ** (-0.5), 0.5, D ** (-0.5), (FF_PAD // 64) ** (-0.5), 0.4)
    scale = 1.0 / target_count
    down_res = adamw_as(
        (0, 1), down_weight, down_grad, down_first, down_second, rate_list[3], scale
    )
    attn_back, down_res = gather_rows(grad_one.astype(jnp.bfloat16), down_res)
    gateup_grad, down_grad = lax.optimization_barrier((gateup_grad, down_grad))
    gateup_grad = with_layout_constraint(
        lax.psum_scatter(gateup_grad, "dp", scatter_dimension=2, tiled=True),
        Layout(major_to_minor=(0, 1, 2)),
    )
    grad_attended = jnp.einsum(
        "td,de->te", attn_back, out_full, preferred_element_type=jnp.bfloat16
    )
    grad_proj = attend_backward(seq_info, *kept, grad_attended, cosine, sine)
    attended, grad_proj = lax.optimization_barrier((attended, grad_proj))
    attend_grad = jnp.concatenate(
        [
            jnp.einsum("te,td->ed", left, right, preferred_element_type=jnp.bfloat16)
            for left, right in ((attended, attn_back), (grad_proj, inputs))
        ],
        0,
    )
    grad_proj, attend_grad = lax.optimization_barrier((grad_proj, attend_grad))
    attend_grad, gateup_grad = lax.optimization_barrier((attend_grad, gateup_grad))
    attend_grad = lax.psum_scatter(attend_grad, "dp", scatter_dimension=1, tiled=True)
    gateup_res = adamw_as(
        (2, 1, 0),
        gateup_weight,
        gateup_grad.transpose(1, 0, 2),
        gateup_first,
        gateup_second,
        rate_list[2],
        scale,
    )
    input_raw, gateup_res = scatter_rows(
        far_first(
            grad_proj,
            lambda rows: jnp.einsum(
                "te,de->td", rows, qkv_full, preferred_element_type=jnp.bfloat16
            ),
            two_pieces,
        ),
        gateup_res,
    )
    input_raw = input_raw + deep_alpha * grad_one
    norm_grad = jnp.stack([gain_one, bias_one, gain_two, bias_two], 0)
    norm_grad, input_raw = lax.optimization_barrier((norm_grad, input_raw))
    norm_grad = sum_everywhere(norm_grad)
    out_grad = attend_grad[:local_dim]
    qkv_grad = attend_grad[local_dim:].reshape(3, local_dim, shard_rows)
    qkv_res = adamw_as(
        (1, 0, 2), qkv_weight, qkv_grad.transpose(0, 2, 1), qkv_first, qkv_second, rate_list[0], scale
    )
    out_res = adamw_as((0, 1), out_weight, out_grad, out_first, out_second, rate_list[1], scale)
    norm_res = adamw(norm_params, norm_grad * scale, norm_first, norm_second, rate_list[4])
    return (
        output_rows.astype(jnp.bfloat16),
        input_raw * scale,
        qkv_res[0],
        qkv_res[1],
        qkv_res[2],
        out_res[0],
        out_res[1],
        out_res[2],
        gateup_res[0],
        gateup_res[1],
        gateup_res[2],
        down_res[0],
        down_res[1],
        down_res[2],
        norm_res[0],
        norm_res[1],
        norm_res[2],
    )


def solution(mesh):
    return jax.shard_map(
        local,
        mesh=mesh,
        in_specs=(
            P(("dp", "mp"), None),
            P(("dp", "mp"), None),
            P("dp"),
            P("dp"),
            P(("dp", "mp")),
            P("dp", None, "mp"),
            P("mp", "dp"),
            P("dp", None, "mp"),
            P("mp", "dp"),
            P(),
            P("dp", None, "mp"),
            P("mp", "dp"),
            P("dp", None, "mp"),
            P("mp", "dp"),
            P(),
            P("dp", None, "mp"),
            P("mp", "dp"),
            P("dp", None, "mp"),
            P("mp", "dp"),
            P(),
        ),
        out_specs=(
            P(("dp", "mp"), None),
            P(("dp", "mp"), None),
            P("dp", None, "mp"),
            P("dp", None, "mp"),
            P("dp", None, "mp"),
            P("mp", "dp"),
            P("mp", "dp"),
            P("mp", "dp"),
            P("dp", None, "mp"),
            P("dp", None, "mp"),
            P("dp", None, "mp"),
            P("mp", "dp"),
            P("mp", "dp"),
            P("mp", "dp"),
            P(),
            P(),
            P(),
        ),
        check_vma=False,
    )
```
